512 devices in a mesh: gx: 4 (over x), gy: 16 (over z, core), gz: 8 (over y).
Axes of the slice: x: 4, y: 8, z: 8, core: 2. Of those that a mesh axis runs over, the one named last changes fastest.
Arguments:
- features: bfloat16 [65536, 25, 128], P(('gx', 'gy', 'gz')), may hold values from -6 to 6
- positions: bfloat16 [3, 65536], P(None, ('gx', 'gy', 'gz')), may hold values from 0 to 4
- probe_positions: float32 [3, 131072], P(None, ('gx', 'gy', 'gz')), may hold values from 0 to 4
- neighbours: int32 [65536, 20], P(('gx', 'gy', 'gz')), may hold values from 0 to 235
- routes: int32 [65536, 1], P(('gx', 'gy', 'gz')), may hold values from 0 to 127; in each aligned block of 128 rows (0 to 127, 128 to 255, ...) at most 2 rows name the same one
- pattern: int32 [1024, 128], P(('gx', 'gy', 'gz')), may hold values 0 or 1
- charge_index: int32 [1], replicated, may hold values from 0 to 7
- charge_table: bfloat16 [8, 128], replicated, may hold values from -6 to 6
- w_radial_in: bfloat16 [8, 64], replicated, may hold values from -2 to 2
- w_radial_out: bfloat16 [64, 1280], replicated, may hold values from -0.75 to 0.75
- w_mix: bfloat16 [5, 128, 128], replicated, may hold values from -0.5 to 0.5
- w_self: bfloat16 [5, 128, 128], replicated, may hold values from -0.5 to 0.5
- w_gate: bfloat16 [128, 512], replicated, may hold values from -0.5 to 0.5
- w_read: bfloat16 [8, 5, 128], replicated, may hold values from -0.5 to 0.5
Outputs:
- atoms_out: bfloat16 [65536, 25, 128], P(('gx', 'gy', 'gz'))
- density: float32 [131072], P(('gx', 'gy', 'gz'))
The draws below stay inside these ranges and needn't reach their ends.
Inputs may be any that keep to these rules, and one draw needn't show every extreme that they name: In box (i, j, k) an index n >= 128 names a front atom of the box or of one of its 26 periodic neighbours, coded as in the reference program. `routes`: A tile number t is gy index times 8 plus gz index within the atom's gx plane; the rows of one box name each tile at most 2 times and name different tiles in one row.
All inputs are finite; a program needn't handle non-finite values. No bound on the sum of `pattern` on one device may be relied on, other than what follows from the above.
Results may differ from the reference program's by a relative error of at most 0.0031.
Values may be sent and summed in bfloat16 or wider, within the bound.
A program may use at most 64 MiB of HBM per device.

```python
import math
import jax
import jax.numpy as jnp
import numpy as np
from jax import lax

CH = 128
LMAX = 4
IRREPS = 25
NB = 8
RH = 64
K = 20
ATOMS_DEV = 128
BND = 4
PROBE_DEV = 256
PB = 128
NQ = 8
TOPC = 1
NSRC = 128
CAP = 2
ATOMS = 65536
PROBES = 131072
PBLOCKS = 1024
N_GX = 4
N_GY = 16
N_GZ = 8


def set_ends(entries, rng, low, top_value):
    longest = entries.shape.index(max(entries.shape))
    spots = []
    for shift in (0, 1):
        where = [jax.random.randint(jax.random.fold_in(rng, axis), (), 0, length) for axis, length in enumerate(entries.shape)]
        where[longest] = (where[longest] + shift) % entries.shape[longest]
        spots.append(tuple(where))
    return entries.at[spots[0]].set(low).at[spots[1]].set(top_value)


def block_levels(stream_key, shape, split, low, high):
    level = 1.0
    for dim, parts in split:
        draws = jax.random.uniform(jax.random.fold_in(jax.random.fold_in(stream_key, 6), dim), (parts,), jnp.float32, low / len(split), high / len(split))
        level = level * jnp.repeat(jnp.exp(draws), shape[dim] // parts).reshape((-1,) + (1,) * (len(shape) - 1 - dim))
    return level


def routed_block(key, own, number, rows, count, top, most, slope):
    sequence = jax.random.permutation(key, count)
    heavy_load, ordinary = portions_of(count, rows * top, most, slope, True), portions_of(count, rows * top, most, slope, False)
    places = jnp.arange(count)

    def named(lengths, turn):
        used = int((lengths > 0).sum())
        fixed = max(1, used // 4)
        shifted = fixed + (places - fixed + turn * (used - fixed)) % max(1, count - fixed)
        return jnp.zeros((count,), jnp.int32).at[sequence[jnp.where(places < fixed, places, shifted)]].set(jnp.asarray(lengths, jnp.int32))

    lengths = jnp.where(number % 4 == 0, named(heavy_load, number // 4), named(ordinary, number - number // 4 - 1))
    mixed = jax.random.permutation(jax.random.fold_in(own, 3), count)
    source_of, sink = mixed[0:count // 2 * 2:2], mixed[1:count // 2 * 2:2]
    room = jnp.minimum(lengths[source_of] - 1, most - lengths[sink]) // 2
    room = jnp.where((source_of == sequence[0]) | (sink == sequence[0]) | (lengths[sink] == 0), 0, jnp.maximum(room, 0))
    shifted = jax.random.randint(jax.random.fold_in(own, 4), (count // 2,), 0, 1 << 20) % (room + 1)
    lengths = lengths.at[source_of].add(-shifted).at[sink].add(shifted)
    items = jnp.searchsorted(jnp.cumsum(lengths), jnp.arange(rows * top), side="right").astype(jnp.int32)
    listing = items.reshape(top, rows).T
    listing = listing[jax.random.permutation(jax.random.fold_in(own, 1), rows)]
    turn = jax.random.randint(jax.random.fold_in(own, 2), (rows, 1), 0, top)
    return jnp.take_along_axis(listing, (jnp.arange(top)[None, :] + turn) % top, axis=1)


def portions_of(amount, total, bound, skew, full):
    portions = [(1 << 20) // math.isqrt(rank ** skew) + 1 for rank in range(1, amount + 1)]
    largest = bound if full else min(bound, max(-(-total // amount), total * portions[0] // sum(portions)))
    least = 1 if total - largest >= amount - 1 else 0
    holding, surplus = [largest] + [least] * (amount - 1), total - largest - least * (amount - 1)
    while surplus > 0:
        candidates = [i for i in range(1, amount) if holding[i] < largest] or [i for i in range(1, amount) if holding[i] < bound]
        whole, left = sum([portions[i] for i in candidates]), surplus
        for i in candidates:
            more = min(bound - holding[i], max(1, left * portions[i] // whole), surplus)
            holding[i] = holding[i] + more
            surplus = surplus - more
    return np.array(holding)


def scatter_about(stream_key, dims, width, reach, cuts=(), dtype=jnp.bfloat16):
    drawn = width * jax.random.normal(stream_key, dims, jnp.float32)
    if cuts:
        drawn = drawn * block_levels(stream_key, dims, cuts, -0.22, 0.18)
    return jnp.clip(drawn, -reach, reach).astype(dtype)


def setup_inputs(seed: int = 0) -> dict:
    streams_of = jax.random.split(jax.random.key(seed), 15)
    features = scatter_about(streams_of[0], (ATOMS, IRREPS, CH), 1.0, 6.0, ((0, 512),))
    positions = jnp.clip(4.0 * jax.random.uniform(streams_of[1], (3, ATOMS), jnp.float32) ** block_levels(streams_of[1], (3, ATOMS), ((1, 512),), -0.2, 0.2), 0.0, 4.0).astype(jnp.bfloat16)
    probe_positions = jnp.clip(4.0 * jax.random.uniform(streams_of[2], (3, PROBES), jnp.float32) ** block_levels(streams_of[2], (3, PROBES), ((1, 512),), -0.2, 0.2), 0.0, 4.0)
    neighbours = set_ends(jax.random.randint(streams_of[3], (ATOMS, K), 0, ATOMS_DEV + 27 * BND), jax.random.fold_in(streams_of[3], 1), 0, (ATOMS_DEV + 27 * BND) - 1).astype(jnp.int32)
    routes_keys = jax.random.split(jax.random.fold_in(streams_of[4], 1), ATOMS // ATOMS_DEV)
    routes_turns = jax.random.permutation(jax.random.fold_in(streams_of[4], 3), ATOMS // ATOMS_DEV)
    routes = jax.vmap(lambda own, number: routed_block(jax.random.fold_in(streams_of[4], 2), own, number, ATOMS_DEV, N_GY * N_GZ, TOPC, CAP, 2))(routes_keys, routes_turns).reshape((ATOMS, TOPC))
    pattern = set_ends((jax.random.randint(streams_of[5], (PBLOCKS, NSRC), 0, 2) < 1).astype(jnp.int32), jax.random.fold_in(streams_of[5], 1), 0, 1)
    charge_index = jax.random.randint(streams_of[6], (1,), 0, NQ).astype(jnp.int32)
    charge_table = scatter_about(streams_of[7], (NQ, CH), 1.0, 6.0)
    w_radial_in = scatter_about(streams_of[8], (NB, RH), NB ** -0.5, 2.0)
    w_radial_out = scatter_about(streams_of[9], (RH, 2 * (LMAX + 1) * CH), RH ** -0.5, 0.75)
    w_mix = scatter_about(streams_of[10], (LMAX + 1, CH, CH), CH ** -0.5, 0.5)
    w_self = scatter_about(streams_of[11], (LMAX + 1, CH, CH), CH ** -0.5, 0.5)
    w_gate = scatter_about(streams_of[12], (CH, LMAX * CH), CH ** -0.5, 0.5)
    w_read = scatter_about(streams_of[13], (NB, LMAX + 1, CH), CH ** -0.5, 0.5)
    return dict(features=features, positions=positions, probe_positions=probe_positions, neighbours=neighbours, routes=routes, pattern=pattern, charge_index=charge_index, charge_table=charge_table, w_radial_in=w_radial_in, w_radial_out=w_radial_out, w_mix=w_mix, w_self=w_self, w_gate=w_gate, w_read=w_read)


CUTOFF = 8.0
WIDTH_R = 0.75
REACH = 6.0
FLOOR = 0.25

def harmonics(comp_x, comp_y, comp_z):
    sq_x = comp_x * comp_x
    sq_y = comp_y * comp_y
    sq_z = comp_z * comp_z
    return jnp.stack([jnp.ones_like(comp_x), math.sqrt(3.0) * comp_y, math.sqrt(3.0) * comp_z, math.sqrt(3.0) * comp_x, math.sqrt(15.0) * comp_x * comp_y, math.sqrt(15.0) * comp_y * comp_z, 0.5 * math.sqrt(5.0) * (3.0 * sq_z - 1.0), math.sqrt(15.0) * comp_x * comp_z, 0.5 * math.sqrt(15.0) * (sq_x - sq_y), math.sqrt(35.0 / 8.0) * comp_y * (3.0 * sq_x - sq_y), math.sqrt(105.0) * comp_x * comp_y * comp_z, math.sqrt(21.0 / 8.0) * comp_y * (5.0 * sq_z - 1.0), 0.5 * math.sqrt(7.0) * comp_z * (5.0 * sq_z - 3.0), math.sqrt(21.0 / 8.0) * comp_x * (5.0 * sq_z - 1.0), 0.5 * math.sqrt(105.0) * comp_z * (sq_x - sq_y), math.sqrt(35.0 / 8.0) * comp_x * (sq_x - 3.0 * sq_y), 1.5 * math.sqrt(35.0) * comp_x * comp_y * (sq_x - sq_y), 1.5 * math.sqrt(17.5) * comp_y * comp_z * (3.0 * sq_x - sq_y), 1.5 * math.sqrt(5.0) * comp_x * comp_y * (7.0 * sq_z - 1.0), 1.5 * math.sqrt(2.5) * comp_y * comp_z * (7.0 * sq_z - 3.0), 0.375 * (35.0 * sq_z * sq_z - 30.0 * sq_z + 3.0), 1.5 * math.sqrt(2.5) * comp_x * comp_z * (7.0 * sq_z - 3.0), 0.75 * math.sqrt(5.0) * (sq_x - sq_y) * (7.0 * sq_z - 1.0), 1.5 * math.sqrt(17.5) * comp_x * comp_z * (sq_x - 3.0 * sq_y), 0.375 * math.sqrt(35.0) * (sq_x * sq_x - 6.0 * sq_x * sq_y + sq_y * sq_y)])

def radial_basis(distance, functions):
    centres = jnp.arange(functions).astype(jnp.float32) * (REACH / (functions - 1))
    bcast_shape = (functions,) + (1,) * distance.ndim
    envelope = jnp.square(1.0 - jnp.square(distance / CUTOFF))
    return jnp.exp(-jnp.square((distance[None] - centres.reshape(bcast_shape)) / WIDTH_R)) * envelope[None]

def geometry(offset_vec):
    distance = jnp.sqrt(lax.optimization_barrier(jnp.sum(offset_vec * offset_vec, axis=0)))
    direction = offset_vec / jnp.maximum(distance, FLOOR)[None]
    return (distance, harmonics(direction[0], direction[1], direction[2]))

def embed(features, charge_index, charge_table):
    levels = charge_table.shape[0]
    chosen = (jnp.arange(levels).astype(jnp.int32) == charge_index[0]).astype(jnp.float32)
    charge_shift = lax.optimization_barrier(jnp.sum(chosen[:, None] * charge_table.astype(jnp.float32), axis=0))
    scalar = (features[:, 0:1, :].astype(jnp.float32) + charge_shift[None, None, :]).astype(jnp.bfloat16)
    return jnp.concatenate([scalar, features[:, 1:, :]], axis=1)

def aggregate(feats_all, pos_all, neighbours, own_pos, w_radial_in, w_radial_out):
    row_count, fanout = neighbours.shape
    channels = feats_all.shape[-1]
    degrees = w_radial_out.shape[1] // (2 * channels)
    repeats = [2 * degree + 1 for degree in range(degrees)]
    components = degrees * degrees
    block_rows = 16

    def one_block(inputs):
        index_block, centre = inputs
        flat_index = index_block.reshape(-1)
        gathered = jnp.take(feats_all, flat_index, axis=0)
        offset_vec = (jnp.take(pos_all, flat_index, axis=0) - jnp.repeat(centre, fanout, axis=0)).T
        distance, angular = geometry(offset_vec)
        radial_in = radial_basis(distance, w_radial_in.shape[0]).T.astype(jnp.bfloat16)
        hidden = jax.nn.silu(jnp.dot(radial_in, w_radial_in, preferred_element_type=jnp.float32)).astype(jnp.bfloat16)
        radial = jnp.dot(hidden, w_radial_out, preferred_element_type=jnp.float32).reshape(-1, 2, degrees, channels)
        same_path = jnp.repeat(radial[:, 0], jnp.array(repeats), axis=1, total_repeat_length=components)
        cross_path = jnp.repeat(radial[:, 1], jnp.array(repeats), axis=1, total_repeat_length=components)
        values = gathered.astype(jnp.float32)
        message = same_path * values + cross_path * values[:, 0:1, :] * angular.T[:, :, None]
        return lax.optimization_barrier(jnp.sum(message.reshape(block_rows, fanout, components, channels), axis=1)) * (1.0 / math.sqrt(fanout))
    result = lax.map(one_block, (neighbours.reshape(row_count // block_rows, block_rows, fanout), own_pos.reshape(row_count // block_rows, block_rows, 3)))
    return result.reshape(row_count, components, channels).astype(jnp.bfloat16)

def update(embedded, aggregated, w_mix, w_self, w_gate):
    row_count, components, channels = embedded.shape
    degrees = w_mix.shape[0]
    gate_values = jax.nn.sigmoid(jnp.dot(aggregated[:, 0, :], w_gate, preferred_element_type=jnp.float32))
    gate_values = gate_values.reshape(row_count, degrees - 1, channels)
    pieces = []
    for degree in range(degrees):
        lower_end = degree * degree
        upper_end = lower_end + 2 * degree + 1
        mixed_term = jnp.dot(aggregated[:, lower_end:upper_end, :].reshape(-1, channels), w_mix[degree], preferred_element_type=jnp.float32)
        mixed_term = mixed_term + jnp.dot(embedded[:, lower_end:upper_end, :].reshape(-1, channels), w_self[degree], preferred_element_type=jnp.float32)
        mixed_term = mixed_term.reshape(row_count, upper_end - lower_end, channels)
        residual_part = embedded[:, lower_end:upper_end, :].astype(jnp.float32)
        if degree == 0:
            pieces.append(residual_part + jax.nn.silu(mixed_term))
        else:
            pieces.append(residual_part + mixed_term * gate_values[:, degree - 1][:, None, :])
    return jnp.concatenate(pieces, axis=1).astype(jnp.bfloat16)

def readout(features, w_read):
    row_count, components, channels = features.shape
    degrees = w_read.shape[1]
    pieces = []
    for degree in range(degrees):
        lower_end = degree * degree
        upper_end = lower_end + 2 * degree + 1
        partial_value = jnp.dot(features[:, lower_end:upper_end, :].reshape(-1, channels), w_read[:, degree, :].T, preferred_element_type=jnp.float32)
        pieces.append(partial_value.reshape(row_count, upper_end - lower_end, -1))
    return jnp.transpose(jnp.concatenate(pieces, axis=1), (0, 2, 1))

def slot_rows(routes, dests, capacity):
    row_count, cover_count = routes.shape
    flat_dest = routes.reshape(-1).astype(jnp.int32)
    onehot = (flat_dest[:, None] == jnp.arange(dests).astype(jnp.int32)[None, :]).astype(jnp.int32)
    rank_in_dest = lax.optimization_barrier(jnp.sum((jnp.cumsum(onehot, axis=0) - 1) * onehot, axis=1)).astype(jnp.int32)
    slot_index = flat_dest * capacity + rank_in_dest
    source_row = (jnp.arange(row_count * cover_count) // cover_count).astype(jnp.int32)
    return jnp.full((dests * capacity,), row_count, jnp.int32).at[slot_index].set(source_row)

def density_tile(probe_pos, pattern, slot_pos, slot_coeffs, capacity, probe_block):
    slot_count = slot_pos.shape[0]
    probe_count = probe_pos.shape[1]
    span = 128 if slot_count % 128 == 0 else slot_count
    keep_mask = jnp.repeat(jnp.repeat(pattern.astype(jnp.float32), probe_block, axis=0), capacity, axis=1)

    def one_span(total, start):
        where_pos = lax.dynamic_slice_in_dim(slot_pos, start, span, 0)
        coeffs = lax.dynamic_slice_in_dim(slot_coeffs, start, span, 0)
        keep = lax.dynamic_slice_in_dim(keep_mask, start, span, 1)
        offset_vec = probe_pos[:, :, None] - where_pos.T[:, None, :]
        distance, angular = geometry(offset_vec)
        radial_in = radial_basis(distance, coeffs.shape[1])
        contracted = jnp.einsum('lps,sbl->bps', angular, coeffs, precision=lax.Precision.HIGHEST)
        return (total + lax.optimization_barrier(jnp.sum(lax.optimization_barrier(jnp.sum(radial_in * contracted, axis=0)) * keep, axis=1)), None)
    starts = jnp.arange(0, slot_count, span).astype(jnp.int32)
    total, unused = lax.scan(one_span, jnp.zeros((probe_count,), jnp.float32), starts)
    return total * (1.0 / math.sqrt(slot_count))

def reference(features, positions, probe_positions, neighbours, routes, pattern, charge_index, charge_table, w_radial_in, w_radial_out, w_mix, w_self, w_gate, w_read):
    devices_all = N_GX * N_GY * N_GZ
    plane = N_GY * N_GZ
    per_dev = ATOMS_DEV
    rim = BND
    capacity = CAP
    embedded = embed(features, charge_index, charge_table)
    atom_pos = positions.astype(jnp.float32).T
    rim_feats = embedded.reshape(devices_all, per_dev, IRREPS, CH)[:, :rim]
    rim_pos = atom_pos.reshape(devices_all, per_dev, 3)[:, :rim]
    offsets = jnp.arange(27).astype(jnp.int32)
    off_x = offsets // 9 - 1
    off_y = offsets // 3 % 3 - 1
    off_z = offsets % 3 - 1

    def layer_one(device):
        pos_x = device // plane
        pos_y = device // N_GZ % N_GY
        pos_z = device % N_GZ
        sources = (pos_x + off_x) % N_GX * plane + (pos_y + off_y) % N_GY * N_GZ + (pos_z + off_z) % N_GZ
        ghost_feats = jnp.take(rim_feats, sources, axis=0).reshape(27 * rim, IRREPS, CH)
        ghost_pos = jnp.take(rim_pos, sources, axis=0).reshape(27 * rim, 3)
        own_feats = lax.dynamic_slice_in_dim(embedded, device * per_dev, per_dev, 0)
        own_pos = lax.dynamic_slice_in_dim(atom_pos, device * per_dev, per_dev, 0)
        own_lists = lax.dynamic_slice_in_dim(neighbours, device * per_dev, per_dev, 0)
        feats_all = jnp.concatenate([own_feats, ghost_feats], axis=0)
        pos_all = jnp.concatenate([own_pos, ghost_pos], axis=0)
        aggregated = aggregate(feats_all, pos_all, own_lists, own_pos, w_radial_in, w_radial_out)
        updated = update(own_feats, aggregated, w_mix, w_self, w_gate)
        return (updated, readout(updated, w_read))
    device_ids = jnp.arange(devices_all).astype(jnp.int32)
    updated_all, coeffs_all = lax.map(layer_one, device_ids)

    def table_one(route_block):
        return slot_rows(route_block, plane, capacity)
    tables = lax.map(table_one, routes.reshape(devices_all, per_dev, TOPC))
    flat_coeffs = jnp.concatenate([coeffs_all.reshape(-1, NB, IRREPS), jnp.zeros((1, NB, IRREPS), jnp.float32)], axis=0)
    flat_pos = jnp.concatenate([atom_pos, jnp.zeros((1, 3), jnp.float32)], axis=0)
    pattern_rows = PROBE_DEV // PB

    def tile_one(device):
        pos_x = device // plane
        target = device % plane
        sources = pos_x * plane + jnp.arange(plane).astype(jnp.int32)
        rows_here = lax.dynamic_slice_in_dim(jnp.take(tables, sources, axis=0), target * capacity, capacity, 1)
        global_rows = jnp.where(rows_here < per_dev, sources[:, None] * per_dev + rows_here, devices_all * per_dev).reshape(-1)
        slot_coeffs = jnp.take(flat_coeffs, global_rows, axis=0)
        slot_pos = jnp.take(flat_pos, global_rows, axis=0)
        probe_pos = lax.dynamic_slice_in_dim(probe_positions, device * PROBE_DEV, PROBE_DEV, 1)
        tile_pattern = lax.dynamic_slice_in_dim(pattern, device * pattern_rows, pattern_rows, 0)
        return density_tile(probe_pos, tile_pattern, slot_pos, slot_coeffs, capacity, PB)
    density = lax.map(tile_one, device_ids).reshape(-1)
    return (updated_all.reshape(ATOMS, IRREPS, CH), density)
```

```python
import functools, math
import jax
import jax.numpy as jnp
from jax import lax
from jax.experimental import pallas as pl
from jax.experimental.pallas import tpu as pltpu
from jax.sharding import PartitionSpec as P

F32 = jnp.float32
BF16 = jnp.bfloat16
CUTOFF = 8.0
WIDTH_R = 0.75
REACH = 6.0
FLOOR = 0.25
N_FUN = 8
DEG = 5
COMP = 25
CH = 128
ATOMS = 128
FAN = 20
GROUP = 8
N_GROUP = 16
EDGE = GROUP * FAN
CHUNK = 4
MAXN = 256


def degree_of(component):
    return int(math.isqrt(component))


def harmonics(x, y, z):
    xx, yy, zz = x * x, y * y, z * z
    c = math.sqrt
    return [
        jnp.ones_like(x),
        c(3.0) * y,
        c(3.0) * z,
        c(3.0) * x,
        c(15.0) * x * y,
        c(15.0) * y * z,
        0.5 * c(5.0) * (3.0 * zz - 1.0),
        c(15.0) * x * z,
        0.5 * c(15.0) * (xx - yy),
        c(35.0 / 8.0) * y * (3.0 * xx - yy),
        c(105.0) * x * y * z,
        c(21.0 / 8.0) * y * (5.0 * zz - 1.0),
        0.5 * c(7.0) * z * (5.0 * zz - 3.0),
        c(21.0 / 8.0) * x * (5.0 * zz - 1.0),
        0.5 * c(105.0) * z * (xx - yy),
        c(35.0 / 8.0) * x * (xx - 3.0 * yy),
        1.5 * c(35.0) * x * y * (xx - yy),
        1.5 * c(17.5) * y * z * (3.0 * xx - yy),
        1.5 * c(5.0) * x * y * (7.0 * zz - 1.0),
        1.5 * c(2.5) * y * z * (7.0 * zz - 3.0),
        0.375 * (35.0 * zz * zz - 30.0 * zz + 3.0),
        1.5 * c(2.5) * x * z * (7.0 * zz - 3.0),
        0.75 * c(5.0) * (xx - yy) * (7.0 * zz - 1.0),
        1.5 * c(17.5) * x * z * (xx - 3.0 * yy),
        0.375 * c(35.0) * (xx * xx - 6.0 * xx * yy + yy * yy),
    ]


def radial_funs(d):
    q = d * (1.0 / CUTOFF)
    env = 1.0 - q * q
    env = env * env
    out = []
    for b in range(N_FUN):
        v = (d - b * (REACH / (N_FUN - 1))) * (1.0 / WIDTH_R)
        out.append(jnp.exp(-(v * v)) * env)
    return out


def geometry(dx, dy, dz):
    d = jnp.sqrt(dx * dx + dy * dy + dz * dz)
    inv = 1.0 / jnp.maximum(d, FLOOR)
    return d, dx * inv, dy * inv, dz * inv


def iota(shape, dim):
    return lax.broadcasted_iota(jnp.int32, shape, dim)


def dot(a, b, dims=None):
    if dims is None:
        dims = (((1,), (0,)), ((), ()))
    return lax.dot_general(a, b, dims, preferred_element_type=F32)


NT = (((1,), (1,)), ((), ()))
TN = (((0,), (0,)), ((), ()))


def atom_kernel(
    ci_ref, nbr_ref, routes_ref, pos_ref, feats_ref, ghost_ref, table_ref, w_in_ref, w_out_ref,
    w_mix_ref, w_self_ref, w_gate_ref, w_read_ref, upd_ref, send_ref,
    f_ref, oh_ref, xyz_ref, ys_ref, bas_ref, r_ref, agg_ref,
):
    lvl = iota((8, CH), 0)
    shift = jnp.sum(
        jnp.where(lvl == ci_ref[0], table_ref[...].astype(F32), 0.0), axis=0, keepdims=True
    )
    keep = iota((112, CH), 0) < 108
    zero16 = jnp.zeros((16, CH), BF16)
    for m in range(COMP):
        own = feats_ref[m]
        gh = ghost_ref[m].astype(F32)
        if m == 0:
            own = (own.astype(F32) + shift).astype(BF16)
            gh = gh + shift
        gh = jnp.where(keep, gh, 0.0).astype(BF16)
        lanes = slice(m * CH, (m + 1) * CH)
        f_ref[0:ATOMS, lanes] = own
        f_ref[ATOMS : ATOMS + 112, lanes] = gh
        f_ref[ATOMS + 112 :, lanes] = zero16
    nbr = nbr_ref[...]
    col = iota((ATOMS, MAXN), 1)
    for k in range(0, FAN, 2):
        halves = []
        for kk in (k, k + 1):
            hot = jnp.where(nbr[:, kk : kk + 1] == col, 1.0, 0.0)
            halves.append(hot.reshape(N_GROUP, GROUP, MAXN))
        oh_ref[:, k * GROUP : (k + 2) * GROUP, :] = jnp.concatenate(halves, axis=1).astype(BF16)
    pos = pos_ref[...].astype(F32)
    gpos = jnp.where(keep, ghost_ref[COMP].astype(F32), 0.0)
    gpos_t = jnp.concatenate([gpos, jnp.zeros((16, CH), F32)], axis=0).T
    pos8 = jnp.concatenate([pos, jnp.zeros((5, ATOMS), F32)], axis=0)
    pt = jnp.concatenate([pos8, gpos_t[0:8]], axis=1).astype(BF16)
    own_group = iota((N_GROUP, ATOMS), 1) // GROUP == iota((N_GROUP, ATOMS), 0)
    tile_sel = jnp.where(
        iota((ATOMS, EDGE), 0) % GROUP == iota((ATOMS, EDGE), 1) % GROUP, 1.0, 0.0
    ).astype(BF16)
    for g in range(N_GROUP):
        got = dot(pt, oh_ref[g], NT)
        for c in range(3):
            xyz_ref[c, g : g + 1, :] = got[c : c + 1, :]
    rel = []
    for c in range(3):
        mine = jnp.where(own_group, pos[c : c + 1, :], 0.0).astype(BF16)
        rel.append(xyz_ref[c] - dot(mine, tile_sel))
    d, ux, uy, uz = geometry(*rel)
    for m, val in enumerate(harmonics(ux, uy, uz)):
        ys_ref[:, m, :] = val
    for b, val in enumerate(radial_funs(d)):
        bas_ref[:, b, :] = val
    mask8 = jnp.where(iota((GROUP, EDGE), 1) % GROUP == iota((GROUP, EDGE), 0), 1.0, 0.0)
    w_in = w_in_ref[...]
    scale = 1.0 / math.sqrt(FAN)

    def one_chunk(ch, carry):
        base = ch * CHUNK
        hot = oh_ref[pl.ds(base, CHUNK)].reshape(CHUNK * EDGE, MAXN)
        first = dot(hot, f_ref[:, 0:CH]).reshape(CHUNK, EDGE, CH)
        for q in range(CHUNK):
            h = dot(bas_ref[base + q].astype(BF16), w_in, TN)
            h = (h * jax.nn.sigmoid(h)).astype(BF16)
            rad = dot(h, w_out_ref[...])
            r_ref[q] = rad[:, 0 : DEG * CH]
            y = ys_ref[base + q]
            for l in range(DEG):
                lo = l * l
                cross = rad[:, (DEG + l) * CH : (DEG + l + 1) * CH] * first[q]
                rows = [y[m : m + 1, :] * mask8 for m in range(lo, lo + 2 * l + 1)]
                rows.append(jnp.zeros((GROUP, EDGE), F32))
                lhs = jnp.concatenate(rows, axis=0).astype(BF16)
                got = dot(lhs, cross.astype(BF16))
                for j in range(2 * l + 1):
                    m = lo + j
                    agg_ref[base + q, :, m * CH : (m + 1) * CH] = got[
                        j * GROUP : (j + 1) * GROUP, :
                    ]
        for m in range(0, COMP, 2):
            comps = [m] + ([m + 1] if m + 1 < COMP else [])
            got = dot(hot, f_ref[:, m * CH : (m + len(comps)) * CH])
            for j, mm in enumerate(comps):
                l = degree_of(mm)
                part = got[:, j * CH : (j + 1) * CH].reshape(CHUNK, FAN, GROUP, CH)
                rad = r_ref[:, :, l * CH : (l + 1) * CH].reshape(CHUNK, FAN, GROUP, CH)
                lanes = slice(mm * CH, (mm + 1) * CH)
                agg_ref[pl.ds(base, CHUNK), :, lanes] = agg_ref[
                    pl.ds(base, CHUNK), :, lanes
                ] + jnp.sum(part * rad, axis=1)
        return carry

    lax.fori_loop(0, N_GROUP // CHUNK, one_chunk, 0)

    scale = 1.0 / math.sqrt(FAN)

    def agg_of(m):
        return (agg_ref[:, :, m * CH : (m + 1) * CH].reshape(ATOMS, CH) * scale).astype(BF16)

    gates = jax.nn.sigmoid(dot(agg_of(0), w_gate_ref[...]))
    lane_slot = iota((ATOMS, CH), 1) // N_FUN
    halves = [jnp.zeros((ATOMS, CH), F32), jnp.zeros((ATOMS, CH), F32)]
    for l in range(DEG):
        w_cat = jnp.concatenate([w_mix_ref[l], w_self_ref[l]], axis=0)
        w_r = jnp.concatenate([w_read_ref[:, l, :].astype(F32)] * 16, axis=0).astype(BF16)
        for m in range(l * l, (l + 1) * (l + 1)):
            emb = f_ref[0:ATOMS, m * CH : (m + 1) * CH]
            mixed = dot(jnp.concatenate([agg_of(m), emb], axis=1), w_cat)
            if l == 0:
                add = mixed * jax.nn.sigmoid(mixed)
            else:
                add = mixed * gates[:, (l - 1) * CH : l * CH]
            upd = (emb.astype(F32) + add).astype(BF16)
            upd_ref[m] = upd
            coef = dot(upd, w_r, NT)
            halves[m // 16] = halves[m // 16] + jnp.where(lane_slot == m % 16, coef, 0.0)
    put = jnp.where(iota((8, CH), 1) == iota((8, CH), 0) + 72, 1.0, 0.0).astype(BF16)
    halves[1] = jnp.where(
        lane_slot == 9, dot(pos8.astype(BF16), put, TN), halves[1]
    )
    r_col = jnp.broadcast_to(routes_ref[...].astype(F32), (ATOMS, ATOMS))
    r_row = r_col.T
    before = iota((ATOMS, ATOMS), 0) < iota((ATOMS, ATOMS), 1)
    rank = jnp.sum(
        jnp.where(before, jnp.where(r_col == r_row, 1.0, 0.0), 0.0), axis=0, keepdims=True
    )
    target = (r_row[0:1, :] * 4.0 + rank * 2.0).astype(jnp.int32)
    row = iota((512, ATOMS), 0)
    place = jnp.concatenate(
        [jnp.where(row == target, 1.0, 0.0), jnp.where(row == target + 1, 1.0, 0.0)], axis=1
    ).astype(BF16)
    coefs = jnp.concatenate(halves, axis=0)
    high = coefs.astype(BF16)
    low = (coefs - high.astype(F32)).astype(BF16)
    send_ref[...] = dot(place, high) + dot(place, low)


def atom_call(ci, nbr, routes, pos, feats, ghost, table, w_in, w_out, w_mix, w_self, w_gate, w_read):
    vm = pl.BlockSpec(memory_space=pltpu.VMEM)
    return pl.pallas_call(
        atom_kernel,
        out_shape=(
            jax.ShapeDtypeStruct((COMP, ATOMS, CH), BF16),
            jax.ShapeDtypeStruct((512, CH), F32),
        ),
        in_specs=[pl.BlockSpec(memory_space=pltpu.SMEM)] + [vm] * 12,
        out_specs=(vm, vm),
        scratch_shapes=[
            pltpu.VMEM((MAXN, COMP * CH), BF16),
            pltpu.VMEM((N_GROUP, EDGE, MAXN), BF16),
            pltpu.VMEM((3, N_GROUP, EDGE), F32),
            pltpu.VMEM((N_GROUP, COMP, EDGE), F32),
            pltpu.VMEM((N_GROUP, N_FUN, EDGE), F32),
            pltpu.VMEM((CHUNK, EDGE, DEG * CH), F32),
            pltpu.VMEM((N_GROUP, GROUP, COMP * CH), F32),
        ],
        name="atoms",
    )(ci, nbr, routes, pos, feats, ghost, table, w_in, w_out, w_mix, w_self, w_gate, w_read)


PROBES = 256
SLOTS = 256


def density_kernel(probe_ref, pat_ref, recv_ref, out_ref, ct_ref, px_ref, keep_ref, tot_ref):
    for h in range(2):
        ct_ref[h * CH : (h + 1) * CH, :] = recv_ref[pl.ds(h, SLOTS, stride=2), :].T
    px = jnp.concatenate([probe_ref[...], jnp.zeros((5, PROBES), F32)], axis=0)
    px_ref[...] = px.T
    pat = pat_ref[...].astype(F32).astype(BF16)
    spread = jnp.where(
        iota((SLOTS // 2, SLOTS), 0) == iota((SLOTS // 2, SLOTS), 1) // 2, 1.0, 0.0
    ).astype(BF16)
    keep_ref[...] = dot(pat, spread) * (1.0 / math.sqrt(SLOTS))
    rows = 16

    def block(i, carry):
        start = pl.multiple_of(i * rows, rows)
        p = px_ref[pl.ds(start, rows), :]
        rel = [p[:, c : c + 1] - ct_ref[200 + c : 201 + c, :] for c in range(3)]
        d, ux, uy, uz = geometry(*rel)
        total = [None] * N_FUN
        for m, val in enumerate(harmonics(ux, uy, uz)):
            for b in range(N_FUN):
                term = val * ct_ref[m * N_FUN + b : m * N_FUN + b + 1, :]
                total[b] = term if m == 0 else total[b] + term
        out = None
        for b, phi in enumerate(radial_funs(d)):
            out = phi * total[b] if out is None else out + phi * total[b]
        out = out * keep_ref[pl.ds(i // (PROBES // 2 // rows), 1), :]
        tot_ref[pl.ds(start, rows), :] = jnp.broadcast_to(
            jnp.sum(out, axis=1, keepdims=True), (rows, CH)
        )
        return carry

    lax.fori_loop(0, PROBES // rows, block, 0)
    for h in range(2):
        out_ref[h : h + 1, :] = tot_ref[h * CH : (h + 1) * CH, :].T[0:1, :]


def density_call(probes, pattern, recv):
    vm = pl.BlockSpec(memory_space=pltpu.VMEM)
    return pl.pallas_call(
        density_kernel,
        out_shape=jax.ShapeDtypeStruct((2, CH), F32),
        in_specs=[vm] * 3,
        out_specs=vm,
        scratch_shapes=[
            pltpu.VMEM((2 * CH, SLOTS), F32),
            pltpu.VMEM((PROBES, 8), F32),
            pltpu.VMEM((2, SLOTS), F32),
            pltpu.VMEM((PROBES, CH), F32),
        ],
        name="density",
    )(probes, pattern, recv)


MESH = pl.DeviceIdType.MESH


def halo_kernel(src_ref, dst_ref, send_sem, recv_sem, own_sem):
    gx, gy, gz = lax.axis_index("gx"), lax.axis_index("gy"), lax.axis_index("gz")
    nx, ny, nz = lax.axis_size("gx"), lax.axis_size("gy"), lax.axis_size("gz")
    peers = []
    for n in range(27):
        a, b, c = n // 9 - 1, n // 3 % 3 - 1, n % 3 - 1
        peers.append(
            (
                lax.rem(gx - a + nx, nx),
                lax.rem(gy - b + ny, ny),
                lax.rem(gz - c + nz, nz),
            )
        )
    barrier = pltpu.get_barrier_semaphore()
    for n in range(27):
        if n != 13:
            pl.semaphore_signal(barrier, inc=1, device_id=peers[n], device_id_type=MESH)
    pl.semaphore_wait(barrier, 26)
    copies = []
    for n in range(27):
        if n == 13:
            continue
        copy = pltpu.make_async_remote_copy(
            src_ref=src_ref,
            dst_ref=dst_ref.at[:, n],
            send_sem=send_sem.at[n],
            recv_sem=recv_sem.at[n],
            device_id=peers[n],
            device_id_type=MESH,
        )
        copy.start()
        copies.append(copy)
    own = pltpu.make_async_copy(src_ref, dst_ref.at[:, 13], own_sem)
    own.start()
    own.wait()
    for copy in copies:
        copy.wait()


def halo_call(front):
    vm = pl.BlockSpec(memory_space=pltpu.VMEM)
    return pl.pallas_call(
        halo_kernel,
        out_shape=jax.ShapeDtypeStruct((COMP + 1, 28, 4, CH), BF16),
        in_specs=[vm],
        out_specs=vm,
        scratch_shapes=[
            pltpu.SemaphoreType.DMA((27,)),
            pltpu.SemaphoreType.DMA((27,)),
            pltpu.SemaphoreType.DMA,
        ],
        compiler_params=pltpu.CompilerParams(collective_id=0, has_side_effects=True),
        name="halo",
    )(front)


def tiles_kernel(src_ref, dst_ref, send_sem, recv_sem, own_sem):
    gx, gy, gz = lax.axis_index("gx"), lax.axis_index("gy"), lax.axis_index("gz")
    ny, nz = lax.axis_size("gy"), lax.axis_size("gz")
    count = ny * nz
    me = gy * nz + gz
    barrier = pltpu.get_barrier_semaphore()

    def greet(j, carry):
        t = lax.rem(me + j, count)
        pl.semaphore_signal(
            barrier, inc=1, device_id=(gx, t // nz, lax.rem(t, nz)), device_id_type=MESH
        )
        return carry

    lax.fori_loop(1, count, greet, 0)
    pl.semaphore_wait(barrier, count - 1)

    def post(j, carry):
        t = lax.rem(me + j, count)
        pltpu.make_async_remote_copy(
            src_ref=src_ref.at[t],
            dst_ref=dst_ref.at[me],
            send_sem=send_sem,
            recv_sem=recv_sem,
            device_id=(gx, t // nz, lax.rem(t, nz)),
            device_id_type=MESH,
        ).start()
        return carry

    lax.fori_loop(1, count, post, 0)
    own = pltpu.make_async_copy(src_ref.at[me], dst_ref.at[me], own_sem)
    own.start()
    own.wait()
    part = pl.ds(0, count - 1)
    pltpu.make_async_copy(src_ref.at[part], dst_ref.at[part], send_sem).wait()
    pltpu.make_async_copy(src_ref.at[part], dst_ref.at[part], recv_sem).wait()


def tiles_call(send):
    vm = pl.BlockSpec(memory_space=pltpu.VMEM)
    return pl.pallas_call(
        tiles_kernel,
        out_shape=jax.ShapeDtypeStruct(send.shape, send.dtype),
        in_specs=[vm],
        out_specs=vm,
        scratch_shapes=[pltpu.SemaphoreType.DMA] * 3,
        compiler_params=pltpu.CompilerParams(collective_id=1, has_side_effects=True),
        name="tiles",
    )(send)


def per_device(
    features, positions, probe_positions, neighbours, routes, pattern, charge_index, charge_table,
    w_radial_in, w_radial_out, w_mix, w_self, w_gate, w_read,
):
    feats = jnp.transpose(features, (1, 0, 2))
    coords = jnp.pad(positions[:, :4].T, ((0, 0), (0, CH - 3)))[None]
    front = jnp.concatenate([feats[:, :4], coords], axis=0)
    ghost = halo_call(front).reshape(COMP + 1, 112, CH)
    upd, send = atom_call(
        charge_index, neighbours, routes, positions, feats, ghost, charge_table, w_radial_in,
        w_radial_out, w_mix, w_self, w_gate, w_read,
    )
    recv = tiles_call(send.reshape(128, 4, CH)).reshape(512, CH)
    density = density_call(probe_positions, pattern, recv)
    return jnp.transpose(upd, (1, 0, 2)), density.reshape(PROBES)


def solution(mesh):
    split = ("gx", "gy", "gz")
    rows = P(split, None)
    in_specs = (
        (P(split, None, None), P(None, split), P(None, split), rows, rows, rows) + (P(),) * 8
    )
    out_specs = (P(split, None, None), P(split))
    return jax.shard_map(
        per_device, mesh=mesh, in_specs=in_specs, out_specs=out_specs, check_vma=False
    )
```

```python
import functools, math
import jax
import jax.numpy as jnp
from jax import lax
from jax.experimental import pallas as pl
from jax.experimental.pallas import tpu as pltpu
from jax.sharding import PartitionSpec as P

F32 = jnp.float32
BF16 = jnp.bfloat16
CUTOFF = 8.0
WIDTH_R = 0.75
REACH = 6.0
FLOOR = 0.25
N_FUN = 8
DEG = 5
COMP = 25
CH = 128
ATOMS = 128
FAN = 20
GROUP = 8
N_GROUP = 16
EDGE = GROUP * FAN
CHUNK = 4
MAXN = 256


def degree_of(component):
    return int(math.isqrt(component))


def harmonics(x, y, z):
    xx, yy, zz = x * x, y * y, z * z
    c = math.sqrt
    return [
        jnp.ones_like(x),
        c(3.0) * y,
        c(3.0) * z,
        c(3.0) * x,
        c(15.0) * x * y,
        c(15.0) * y * z,
        0.5 * c(5.0) * (3.0 * zz - 1.0),
        c(15.0) * x * z,
        0.5 * c(15.0) * (xx - yy),
        c(35.0 / 8.0) * y * (3.0 * xx - yy),
        c(105.0) * x * y * z,
        c(21.0 / 8.0) * y * (5.0 * zz - 1.0),
        0.5 * c(7.0) * z * (5.0 * zz - 3.0),
        c(21.0 / 8.0) * x * (5.0 * zz - 1.0),
        0.5 * c(105.0) * z * (xx - yy),
        c(35.0 / 8.0) * x * (xx - 3.0 * yy),
        1.5 * c(35.0) * x * y * (xx - yy),
        1.5 * c(17.5) * y * z * (3.0 * xx - yy),
        1.5 * c(5.0) * x * y * (7.0 * zz - 1.0),
        1.5 * c(2.5) * y * z * (7.0 * zz - 3.0),
        0.375 * (35.0 * zz * zz - 30.0 * zz + 3.0),
        1.5 * c(2.5) * x * z * (7.0 * zz - 3.0),
        0.75 * c(5.0) * (xx - yy) * (7.0 * zz - 1.0),
        1.5 * c(17.5) * x * z * (xx - 3.0 * yy),
        0.375 * c(35.0) * (xx * xx - 6.0 * xx * yy + yy * yy),
    ]


def radial_funs(d):
    q = d * (1.0 / CUTOFF)
    env = 1.0 - q * q
    env = env * env
    out = []
    for b in range(N_FUN):
        v = (d - b * (REACH / (N_FUN - 1))) * (1.0 / WIDTH_R)
        out.append(jnp.exp(-(v * v)) * env)
    return out


def geometry(dx, dy, dz):
    d = jnp.sqrt(dx * dx + dy * dy + dz * dz)
    inv = 1.0 / jnp.maximum(d, FLOOR)
    return d, dx * inv, dy * inv, dz * inv


def iota(shape, dim):
    return lax.broadcasted_iota(jnp.int32, shape, dim)


def dot(a, b, dims=None):
    if dims is None:
        dims = (((1,), (0,)), ((), ()))
    return lax.dot_general(a, b, dims, preferred_element_type=F32)


NT = (((1,), (1,)), ((), ()))
TN = (((0,), (0,)), ((), ()))


MESH = pl.DeviceIdType.MESH


def atom_kernel(
    ci_ref, nbr_ref, routes_ref, pos_ref, table_ref, w_in_ref, feats_hbm, w_out_hbm, w_mix_hbm,
    w_self_hbm, w_gate_hbm, w_read_hbm, upd_hbm, recv_ref,
    f_ref, e_ref, oh_ref, xyz_ref, ys_ref, bas_ref, r_ref, agg_ref, upd_ref, send_ref,
    w_out_ref, w_mix_ref, w_self_ref, w_gate_ref, w_read_ref,
    load_sem, halo_send, halo_recv, tile_sem, plane_sem,
):
    gx, gy, gz = lax.axis_index("gx"), lax.axis_index("gy"), lax.axis_index("gz")
    nx, ny, nz = lax.axis_size("gx"), lax.axis_size("gy"), lax.axis_size("gz")

    def place(a, b, c):
        return (
            lax.rem(gx + a + nx, nx), lax.rem(gy + b + ny, ny), lax.rem(gz + c + nz, nz)
        )

    peers = [place(1 - n // 9, 1 - n // 3 % 3, 1 - n % 3) for n in range(27)]
    others = [n for n in range(27) if n != 13]
    around = [(b, c) for b in (-1, 0, 1) for c in (-1, 0, 1) if (b, c) != (0, 0)]

    def plane_signal(step):
        for b, c in around:
            pl.semaphore_signal(
                plane_sem.at[step],
                inc=1,
                device_id=place(0, b << step, c << step),
                device_id_type=MESH,
            )

    first = pltpu.make_async_copy(
        feats_hbm.at[:, 0:1], f_ref.at[0:COMP, 0:1], load_sem.at[0]
    )
    first.start()
    barrier = pltpu.get_barrier_semaphore()
    for n in others:
        pl.semaphore_signal(barrier, inc=1, device_id=peers[n], device_id_type=MESH)
    rest = pltpu.make_async_copy(
        feats_hbm.at[:, 1:32], f_ref.at[0:COMP, 1:32], load_sem.at[1]
    )
    loads = [
        pltpu.make_async_copy(src, dst, load_sem.at[2 + i])
        for i, (src, dst) in enumerate(
            (
                (w_out_hbm, w_out_ref),
                (w_mix_hbm, w_mix_ref),
                (w_self_hbm, w_self_ref),
                (w_gate_hbm, w_gate_ref),
                (w_read_hbm, w_read_ref),
            )
        )
    ]
    rest.start()
    for load in loads:
        load.start()
    pos = pos_ref[...].astype(F32)
    pos8 = jnp.concatenate([pos, jnp.zeros((5, ATOMS), F32)], axis=0)
    eye = jnp.where(iota((8, CH), 1) == iota((8, CH), 0), 1.0, 0.0).astype(BF16)
    f_ref[COMP, 0] = dot(pos8.astype(BF16), eye, TN)[0:4].astype(BF16)
    f_ref[:, 59:64] = jnp.zeros((COMP + 1, 5, 4, CH), BF16)
    first.wait()
    pl.semaphore_wait(barrier, 26)
    halo = []
    for n in others:
        copy = pltpu.make_async_remote_copy(
            src_ref=f_ref.at[:, 0],
            dst_ref=f_ref.at[:, 32 + n],
            send_sem=halo_send.at[n],
            recv_sem=halo_recv.at[n],
            device_id=peers[n],
            device_id_type=MESH,
        )
        copy.start()
        halo.append(copy)
    mine = pltpu.make_async_copy(f_ref.at[:, 0], f_ref.at[:, 45], load_sem.at[7])
    mine.start()
    plane_signal(0)
    nbr = jnp.concatenate(
        [nbr_ref[...].astype(F32), jnp.zeros((4, ATOMS), F32)], axis=0
    ).T
    col = iota((ATOMS, MAXN), 1).astype(F32)
    for k in range(0, FAN, 2):
        halves = []
        for kk in (k, k + 1):
            hot = jnp.where(nbr[:, kk : kk + 1] == col, 1.0, 0.0)
            halves.append(hot.reshape(N_GROUP, GROUP, MAXN))
        oh_ref[:, k * GROUP : (k + 2) * GROUP, :] = jnp.concatenate(halves, axis=1).astype(BF16)
    lvl = iota((8, CH), 0)
    shift = jnp.sum(
        jnp.where(lvl == ci_ref[0], table_ref[...].astype(F32), 0.0), axis=0, keepdims=True
    )
    flat = f_ref.reshape(COMP + 1, MAXN, CH)
    rest.wait()
    mine.wait()
    for copy in halo:
        copy.wait()
    pl.semaphore_wait(plane_sem.at[0], 8)
    plane_signal(1)
    for load in loads:
        load.wait()
    e_ref[...] = (flat[0].astype(F32) + shift).astype(BF16)
    gpos_t = flat[COMP, ATOMS:MAXN].astype(F32).T
    pt = jnp.concatenate([pos8, gpos_t[0:8]], axis=1).astype(BF16)

    def comp(m):
        return e_ref[...] if m == 0 else flat[m]

    own_group = iota((N_GROUP, ATOMS), 1) // GROUP == iota((N_GROUP, ATOMS), 0)
    tile_sel = jnp.where(
        iota((ATOMS, EDGE), 0) % GROUP == iota((ATOMS, EDGE), 1) % GROUP, 1.0, 0.0
    ).astype(BF16)
    for g in range(N_GROUP):
        got = dot(pt, oh_ref[g], NT)
        for c in range(3):
            xyz_ref[c, g : g + 1, :] = got[c : c + 1, :]
    rel = []
    for c in range(3):
        mine = jnp.where(own_group, pos[c : c + 1, :], 0.0).astype(BF16)
        rel.append(xyz_ref[c] - dot(mine, tile_sel))
    d, ux, uy, uz = geometry(*rel)
    for m, val in enumerate(harmonics(ux, uy, uz)):
        ys_ref[:, m, :] = val
    for b, val in enumerate(radial_funs(d)):
        bas_ref[:, b, :] = val
    mask8 = jnp.where(iota((GROUP, EDGE), 1) % GROUP == iota((GROUP, EDGE), 0), 1.0, 0.0)
    w_in = w_in_ref[...]
    scale = 1.0 / math.sqrt(FAN)

    def one_chunk(ch, carry):
        base = ch * CHUNK
        hot = oh_ref[pl.ds(base, CHUNK)].reshape(CHUNK * EDGE, MAXN)
        scalars = dot(hot, comp(0)).reshape(CHUNK, EDGE, CH)
        for q in range(CHUNK):
            h = dot(bas_ref[base + q].astype(BF16), w_in, TN)
            h = (h * jax.nn.sigmoid(h)).astype(BF16)
            rad = dot(h, w_out_ref[...])
            r_ref[q] = rad[:, 0 : DEG * CH]
            y = ys_ref[base + q]
            for l in range(DEG):
                lo = l * l
                cross = rad[:, (DEG + l) * CH : (DEG + l + 1) * CH] * scalars[q]
                rows = [y[m : m + 1, :] * mask8 for m in range(lo, lo + 2 * l + 1)]
                rows.append(jnp.zeros((GROUP, EDGE), F32))
                lhs = jnp.concatenate(rows, axis=0).astype(BF16)
                got = dot(lhs, cross.astype(BF16))
                for j in range(2 * l + 1):
                    m = lo + j
                    agg_ref[base + q, :, m * CH : (m + 1) * CH] = got[
                        j * GROUP : (j + 1) * GROUP, :
                    ]
        for m in range(0, COMP, 2):
            comps = [m] + ([m + 1] if m + 1 < COMP else [])
            got = dot(hot, jnp.concatenate([comp(mm) for mm in comps], axis=1))
            for j, mm in enumerate(comps):
                l = degree_of(mm)
                part = got[:, j * CH : (j + 1) * CH].reshape(CHUNK, FAN, GROUP, CH)
                rad = r_ref[:, :, l * CH : (l + 1) * CH].reshape(CHUNK, FAN, GROUP, CH)
                lanes = slice(mm * CH, (mm + 1) * CH)
                agg_ref[pl.ds(base, CHUNK), :, lanes] = agg_ref[
                    pl.ds(base, CHUNK), :, lanes
                ] + jnp.sum(part * rad, axis=1)
        return carry

    lax.fori_loop(0, N_GROUP // CHUNK, one_chunk, 0)

    pl.semaphore_wait(plane_sem.at[1], 8)
    plane_signal(2)

    scale = 1.0 / math.sqrt(FAN)

    def agg_of(m):
        return (agg_ref[:, :, m * CH : (m + 1) * CH].reshape(ATOMS, CH) * scale).astype(BF16)

    gates = jax.nn.sigmoid(dot(agg_of(0), w_gate_ref[...]))
    lane_slot = iota((ATOMS, CH), 1) // N_FUN
    halves = [jnp.zeros((ATOMS, CH), F32), jnp.zeros((ATOMS, CH), F32)]
    for l in range(DEG):
        w_cat = jnp.concatenate([w_mix_ref[l], w_self_ref[l]], axis=0)
        w_r = jnp.concatenate([w_read_ref[l].astype(F32)] * 16, axis=0).astype(BF16)
        for m in range(l * l, (l + 1) * (l + 1)):
            emb = comp(m)[0:ATOMS]
            mixed = dot(jnp.concatenate([agg_of(m), emb], axis=1), w_cat)
            if l == 0:
                add = mixed * jax.nn.sigmoid(mixed)
            else:
                add = mixed * gates[:, (l - 1) * CH : l * CH]
            upd = (emb.astype(F32) + add).astype(BF16)
            upd_ref[m] = upd
            coef = dot(upd, w_r, NT)
            halves[m // 16] = halves[m // 16] + jnp.where(lane_slot == m % 16, coef, 0.0)
    put = jnp.where(iota((8, CH), 1) == iota((8, CH), 0) + 72, 1.0, 0.0).astype(BF16)
    halves[1] = jnp.where(
        lane_slot == 9, dot(pos8.astype(BF16), put, TN), halves[1]
    )
    store = pltpu.make_async_copy(upd_ref, upd_hbm, load_sem.at[8])
    store.start()
    r_row = jnp.broadcast_to(routes_ref[...].astype(F32), (ATOMS, ATOMS))
    r_col = r_row.T
    before = iota((ATOMS, ATOMS), 0) < iota((ATOMS, ATOMS), 1)
    rank = jnp.sum(
        jnp.where(before, jnp.where(r_col == r_row, 1.0, 0.0), 0.0), axis=0, keepdims=True
    )
    target = (r_row[0:1, :] * 4.0 + rank * 2.0).astype(jnp.int32)
    row = iota((512, ATOMS), 0)
    put_rows = jnp.concatenate(
        [jnp.where(row == target, 1.0, 0.0), jnp.where(row == target + 1, 1.0, 0.0)], axis=1
    ).astype(BF16)
    coefs = jnp.concatenate(halves, axis=0)
    high = coefs.astype(BF16)
    low = (coefs - high.astype(F32)).astype(BF16)
    send_ref[...] = (dot(put_rows, high) + dot(put_rows, low)).reshape(128, 4, CH)
    pl.semaphore_wait(plane_sem.at[2], 8)
    count = ny * nz
    me = gy * nz + gz

    def post(j, carry):
        t = lax.rem(me + j, count)
        pltpu.make_async_remote_copy(
            src_ref=send_ref.at[t],
            dst_ref=recv_ref.at[me],
            send_sem=tile_sem.at[0],
            recv_sem=tile_sem.at[1],
            device_id=(gx, t // nz, lax.rem(t, nz)),
            device_id_type=MESH,
        ).start()
        return carry

    lax.fori_loop(1, count, post, 0)
    own = pltpu.make_async_copy(send_ref.at[me], recv_ref.at[me], tile_sem.at[2])
    own.start()
    own.wait()
    store.wait()
    part = pl.ds(0, count - 1)
    pltpu.make_async_copy(send_ref.at[part], recv_ref.at[part], tile_sem.at[0]).wait()
    pltpu.make_async_copy(send_ref.at[part], recv_ref.at[part], tile_sem.at[1]).wait()


def atom_call(ci, nbr, routes, pos, table, w_in, feats, w_out, w_mix, w_self, w_gate, w_read):
    vm = pl.BlockSpec(memory_space=pltpu.VMEM)
    hbm = pl.BlockSpec(memory_space=pl.ANY)
    return pl.pallas_call(
        atom_kernel,
        out_shape=(
            jax.ShapeDtypeStruct((COMP, ATOMS, CH), BF16),
            jax.ShapeDtypeStruct((128, 4, CH), F32),
        ),
        in_specs=[pl.BlockSpec(memory_space=pltpu.SMEM)] + [vm] * 5 + [hbm] * 6,
        out_specs=(hbm, hbm),
        scratch_shapes=[
            pltpu.VMEM((COMP + 1, 64, 4, CH), BF16),
            pltpu.VMEM((MAXN, CH), BF16),
            pltpu.VMEM((N_GROUP, EDGE, MAXN), BF16),
            pltpu.VMEM((3, N_GROUP, EDGE), F32),
            pltpu.VMEM((N_GROUP, COMP, EDGE), F32),
            pltpu.VMEM((N_GROUP, N_FUN, EDGE), F32),
            pltpu.VMEM((CHUNK, EDGE, DEG * CH), F32),
            pltpu.VMEM((N_GROUP, GROUP, COMP * CH), F32),
            pltpu.VMEM((COMP, ATOMS, CH), BF16),
            pltpu.VMEM((128, 4, CH), F32),
            pltpu.VMEM((64, 2 * DEG * CH), BF16),
            pltpu.VMEM((DEG, CH, CH), BF16),
            pltpu.VMEM((DEG, CH, CH), BF16),
            pltpu.VMEM((CH, (DEG - 1) * CH), BF16),
            pltpu.VMEM((DEG, N_FUN, CH), BF16),
            pltpu.SemaphoreType.DMA((9,)),
            pltpu.SemaphoreType.DMA((27,)),
            pltpu.SemaphoreType.DMA((27,)),
            pltpu.SemaphoreType.DMA((3,)),
            pltpu.SemaphoreType.REGULAR((3,)),
        ],
        compiler_params=pltpu.CompilerParams(collective_id=0, has_side_effects=True),
        name="atoms",
    )(ci, nbr, routes, pos, table, w_in, feats, w_out, w_mix, w_self, w_gate, w_read)


PROBES = 256
SLOTS = 256


def density_kernel(
    probe_ref, pat_ref, recv_ref, upd_hbm, out_ref, atoms_hbm,
    ct_ref, px_ref, keep_ref, tot_ref, upd_ref, sem,
):
    take = pltpu.make_async_copy(upd_hbm, upd_ref, sem.at[0])
    give = pltpu.make_async_copy(upd_ref, atoms_hbm, sem.at[1])
    take.start()
    for h in range(2):
        ct_ref[h * CH : (h + 1) * CH, :] = recv_ref[pl.ds(h, SLOTS, stride=2), :].T
    px = jnp.concatenate([probe_ref[...], jnp.zeros((5, PROBES), F32)], axis=0)
    px_ref[...] = px.T
    pat = pat_ref[...].astype(F32).astype(BF16)
    spread = jnp.where(
        iota((SLOTS // 2, SLOTS), 0) == iota((SLOTS // 2, SLOTS), 1) // 2, 1.0, 0.0
    ).astype(BF16)
    keep_ref[...] = dot(pat, spread) * (1.0 / math.sqrt(SLOTS))
    rows = 16

    def block(i, carry):
        start = pl.multiple_of(i * rows, rows)
        p = px_ref[pl.ds(start, rows), :]
        rel = [p[:, c : c + 1] - ct_ref[200 + c : 201 + c, :] for c in range(3)]
        d, ux, uy, uz = geometry(*rel)
        total = [None] * N_FUN
        for m, val in enumerate(harmonics(ux, uy, uz)):
            for b in range(N_FUN):
                term = val * ct_ref[m * N_FUN + b : m * N_FUN + b + 1, :]
                total[b] = term if m == 0 else total[b] + term
        out = None
        for b, phi in enumerate(radial_funs(d)):
            out = phi * total[b] if out is None else out + phi * total[b]
        out = out * keep_ref[pl.ds(i // (PROBES // 2 // rows), 1), :]
        tot_ref[pl.ds(start, rows), :] = jnp.broadcast_to(
            jnp.sum(out, axis=1, keepdims=True), (rows, CH)
        )
        return carry

    steps = PROBES // rows
    lax.fori_loop(0, steps // 4, block, 0)
    take.wait()
    give.start()
    lax.fori_loop(steps // 4, steps, block, 0)
    for h in range(2):
        out_ref[h : h + 1, :] = tot_ref[h * CH : (h + 1) * CH, :].T[0:1, :]
    give.wait()


def density_call(probes, pattern, recv, upd):
    vm = pl.BlockSpec(memory_space=pltpu.VMEM)
    hbm = pl.BlockSpec(memory_space=pl.ANY)
    return pl.pallas_call(
        density_kernel,
        out_shape=(
            jax.ShapeDtypeStruct((2, CH), F32),
            jax.ShapeDtypeStruct((COMP, ATOMS, CH), BF16),
        ),
        in_specs=[vm] * 3 + [hbm],
        out_specs=(vm, hbm),
        scratch_shapes=[
            pltpu.VMEM((2 * CH, SLOTS), F32),
            pltpu.VMEM((PROBES, 8), F32),
            pltpu.VMEM((2, SLOTS), F32),
            pltpu.VMEM((PROBES, CH), F32),
            pltpu.VMEM((COMP, ATOMS, CH), BF16),
            pltpu.SemaphoreType.DMA((2,)),
        ],
        name="density",
    )(probes, pattern, recv, upd)


def per_device(
    features, positions, probe_positions, neighbours, routes, pattern, charge_index, charge_table,
    w_radial_in, w_radial_out, w_mix, w_self, w_gate, w_read,
):
    feats = jnp.transpose(features, (1, 0, 2)).reshape(COMP, 32, 4, CH)
    upd, recv = atom_call(
        charge_index, neighbours.T, routes.T, positions, charge_table, w_radial_in, feats,
        w_radial_out, w_mix, w_self, w_gate, jnp.transpose(w_read, (1, 0, 2)),
    )
    density, atoms = density_call(probe_positions, pattern, recv.reshape(512, CH), upd)
    return jnp.transpose(atoms, (1, 0, 2)), density.reshape(PROBES)


def solution(mesh):
    split = ("gx", "gy", "gz")
    rows = P(split, None)
    in_specs = (
        (P(split, None, None), P(None, split), P(None, split), rows, rows, rows) + (P(),) * 8
    )
    out_specs = (P(split, None, None), P(split))
    return jax.shard_map(
        per_device, mesh=mesh, in_specs=in_specs, out_specs=out_specs, check_vma=False
    )
```

```python
import functools, math
import jax
import jax.numpy as jnp
from jax import lax
from jax.experimental import pallas as pl
from jax.experimental.pallas import tpu as pltpu
from jax.sharding import PartitionSpec as P

F32 = jnp.float32
BF16 = jnp.bfloat16
CUTOFF = 8.0
WIDTH_R = 0.75
REACH = 6.0
FLOOR = 0.25
N_FUN = 8
DEG = 5
COMP = 25
CH = 128
ATOMS = 128
FAN = 20
GROUP = 8
N_GROUP = 16
EDGE = GROUP * FAN
CHUNK = 4
MAXN = 256


def degree_of(component):
    return int(math.isqrt(component))


def harmonics(x, y, z):
    xx, yy, zz = x * x, y * y, z * z
    c = math.sqrt
    return [
        jnp.ones_like(x),
        c(3.0) * y,
        c(3.0) * z,
        c(3.0) * x,
        c(15.0) * x * y,
        c(15.0) * y * z,
        0.5 * c(5.0) * (3.0 * zz - 1.0),
        c(15.0) * x * z,
        0.5 * c(15.0) * (xx - yy),
        c(35.0 / 8.0) * y * (3.0 * xx - yy),
        c(105.0) * x * y * z,
        c(21.0 / 8.0) * y * (5.0 * zz - 1.0),
        0.5 * c(7.0) * z * (5.0 * zz - 3.0),
        c(21.0 / 8.0) * x * (5.0 * zz - 1.0),
        0.5 * c(105.0) * z * (xx - yy),
        c(35.0 / 8.0) * x * (xx - 3.0 * yy),
        1.5 * c(35.0) * x * y * (xx - yy),
        1.5 * c(17.5) * y * z * (3.0 * xx - yy),
        1.5 * c(5.0) * x * y * (7.0 * zz - 1.0),
        1.5 * c(2.5) * y * z * (7.0 * zz - 3.0),
        0.375 * (35.0 * zz * zz - 30.0 * zz + 3.0),
        1.5 * c(2.5) * x * z * (7.0 * zz - 3.0),
        0.75 * c(5.0) * (xx - yy) * (7.0 * zz - 1.0),
        1.5 * c(17.5) * x * z * (xx - 3.0 * yy),
        0.375 * c(35.0) * (xx * xx - 6.0 * xx * yy + yy * yy),
    ]


def radial_funs(d):
    q = d * (1.0 / CUTOFF)
    env = 1.0 - q * q
    env = env * env
    out = []
    for b in range(N_FUN):
        v = (d - b * (REACH / (N_FUN - 1))) * (1.0 / WIDTH_R)
        out.append(jnp.exp(-(v * v)) * env)
    return out


def geometry(dx, dy, dz):
    d = jnp.sqrt(dx * dx + dy * dy + dz * dz)
    inv = 1.0 / jnp.maximum(d, FLOOR)
    return d, dx * inv, dy * inv, dz * inv


def iota(shape, dim):
    return lax.broadcasted_iota(jnp.int32, shape, dim)


def dot(a, b, dims=None):
    if dims is None:
        dims = (((1,), (0,)), ((), ()))
    return lax.dot_general(a, b, dims, preferred_element_type=F32)


NT = (((1,), (1,)), ((), ()))
TN = (((0,), (0,)), ((), ()))


MESH = pl.DeviceIdType.MESH
ROW_OF = (0, 16, 48, 96, 160)
ROWS = 240


def atom_kernel(
    ci_ref, nbr_ref, routes_ref, pos_ref, table_ref, w_in_ref, feats_hbm, w_out_hbm, w_mix_hbm,
    w_self_hbm, w_gate_hbm, w_read_hbm, upd_hbm, recv_ref,
    f_ref, e_ref, oh_ref, xyz_ref, ys_ref, bas_ref, y_ref, r_ref, s_ref, agg_ref, cross_ref,
    upd_ref, send_ref, w_out_ref, w_mix_ref, w_self_ref, w_gate_ref, w_read_ref, spread_ref,
    load_sem, pos_send, pos_recv, halo_send, halo_recv, tile_sem, plane_sem,
):
    gx, gy, gz = lax.axis_index("gx"), lax.axis_index("gy"), lax.axis_index("gz")
    nx, ny, nz = lax.axis_size("gx"), lax.axis_size("gy"), lax.axis_size("gz")

    def place(a, b, c):
        return (
            lax.rem(gx + a + nx, nx), lax.rem(gy + b + ny, ny), lax.rem(gz + c + nz, nz)
        )

    peers = [place(1 - n // 9, 1 - n // 3 % 3, 1 - n % 3) for n in range(27)]
    others = [n for n in range(27) if n != 13]
    around = [(b, c) for b in (-1, 0, 1) for c in (-1, 0, 1) if (b, c) != (0, 0)]

    def plane_signal(step):
        for b, c in around:
            pl.semaphore_signal(
                plane_sem.at[step],
                inc=1,
                device_id=place(0, b << step, c << step),
                device_id_type=MESH,
            )

    first = pltpu.make_async_copy(
        feats_hbm.at[:, 0:1], f_ref.at[0:COMP, 0:1], load_sem.at[0]
    )
    first.start()
    barrier = pltpu.get_barrier_semaphore()
    for n in others:
        pl.semaphore_signal(barrier, inc=1, device_id=peers[n], device_id_type=MESH)
    rest = pltpu.make_async_copy(
        feats_hbm.at[:, 1:32], f_ref.at[0:COMP, 1:32], load_sem.at[1]
    )
    loads = [
        pltpu.make_async_copy(src, dst, load_sem.at[2 + i])
        for i, (src, dst) in enumerate(
            (
                (w_out_hbm, w_out_ref),
                (w_mix_hbm, w_mix_ref),
                (w_self_hbm, w_self_ref),
                (w_gate_hbm, w_gate_ref),
                (w_read_hbm, w_read_ref),
            )
        )
    ]
    rest.start()
    for load in loads:
        load.start()
    pos = pos_ref[...].astype(F32)
    pos8 = jnp.concatenate(
        [pos, jnp.ones((1, ATOMS), F32), jnp.zeros((4, ATOMS), F32)], axis=0
    )
    eye = jnp.where(iota((8, CH), 1) == iota((8, CH), 0), 1.0, 0.0).astype(BF16)
    f_ref[COMP, 0] = dot(pos8.astype(BF16), eye, TN)[0:4].astype(BF16)
    f_ref[:, 59:64] = jnp.zeros((COMP + 1, 5, 4, CH), BF16)
    first.wait()
    pl.semaphore_wait(barrier, 26)
    sent, halo = [], []
    for n in others:
        copy = pltpu.make_async_remote_copy(
            src_ref=f_ref.at[COMP, 0],
            dst_ref=f_ref.at[COMP, 32 + n],
            send_sem=pos_send.at[n],
            recv_sem=pos_recv.at[n],
            device_id=peers[n],
            device_id_type=MESH,
        )
        copy.start()
        sent.append(copy)
    for n in others:
        copy = pltpu.make_async_remote_copy(
            src_ref=f_ref.at[0:COMP, 0],
            dst_ref=f_ref.at[0:COMP, 32 + n],
            send_sem=halo_send.at[n],
            recv_sem=halo_recv.at[n],
            device_id=peers[n],
            device_id_type=MESH,
        )
        copy.start()
        halo.append(copy)
    mine = pltpu.make_async_copy(f_ref.at[:, 0], f_ref.at[:, 45], load_sem.at[7])
    mine.start()
    plane_signal(0)
    nbr = jnp.concatenate(
        [nbr_ref[...].astype(F32), jnp.zeros((4, ATOMS), F32)], axis=0
    ).T
    col = iota((ATOMS, MAXN), 1).astype(F32)
    for k in range(0, FAN, 2):
        halves = []
        for kk in (k, k + 1):
            hot = jnp.where(nbr[:, kk : kk + 1] == col, 1.0, 0.0)
            halves.append(hot.reshape(N_GROUP, GROUP, MAXN))
        oh_ref[:, k * GROUP : (k + 2) * GROUP, :] = jnp.concatenate(halves, axis=1).astype(BF16)
    lvl = iota((8, CH), 0)
    shift = jnp.sum(
        jnp.where(lvl == ci_ref[0], table_ref[...].astype(F32), 0.0), axis=0, keepdims=True
    )
    flat = f_ref.reshape(COMP + 1, MAXN, CH)
    mine.wait()
    for load in loads:
        load.wait()
    spread_ref[...] = jnp.zeros((MAXN, COMP * CH), BF16)
    none8 = jnp.zeros((N_FUN, CH), F32)
    for m in range(COMP):
        one = w_read_ref[degree_of(m)].astype(F32)
        two = [one, none8] if m % 2 == 0 else [none8, one]
        start = (m - m % 2) * N_FUN
        spread_ref[start : start + 16, m * CH : (m + 1) * CH] = jnp.concatenate(
            two, axis=0
        ).astype(BF16)
    for copy in sent:
        copy.wait()
    gpos_t = flat[COMP, ATOMS:MAXN].astype(F32).T
    pt = jnp.concatenate([pos8, gpos_t[0:8]], axis=1).astype(BF16)
    own_group = iota((N_GROUP, ATOMS), 1) // GROUP == iota((N_GROUP, ATOMS), 0)
    tile_sel = jnp.where(
        iota((ATOMS, EDGE), 0) % GROUP == iota((ATOMS, EDGE), 1) % GROUP, 1.0, 0.0
    ).astype(BF16)
    for g in range(N_GROUP):
        got = dot(pt, oh_ref[g], NT)
        for c in range(3):
            xyz_ref[c, g : g + 1, :] = got[c : c + 1, :]
    rel = []
    for c in range(3):
        mine_c = jnp.where(own_group, pos[c : c + 1, :], 0.0).astype(BF16)
        rel.append(xyz_ref[c] - dot(mine_c, tile_sel))
    d, ux, uy, uz = geometry(*rel)
    for m, val in enumerate(harmonics(ux, uy, uz)):
        ys_ref[:, m, :] = val
    for b, val in enumerate(radial_funs(d)):
        bas_ref[:, b, :] = val
    mask8 = jnp.where(iota((GROUP, EDGE), 1) % GROUP == iota((GROUP, EDGE), 0), 1.0, 0.0)
    w_in = w_in_ref[...]
    pl.semaphore_wait(plane_sem.at[0], 8)
    plane_signal(1)

    def radial_chunk(ch, carry):
        base = ch * CHUNK
        for q in range(CHUNK):
            h = dot(bas_ref[base + q].astype(BF16), w_in, TN)
            h = (h * jax.nn.sigmoid(h)).astype(BF16)
            r_ref[base + q] = dot(h, w_out_ref[...])
            y = ys_ref[base + q]
            for l in range(DEG):
                lo = l * l
                rows = [y[m : m + 1, :] * mask8 for m in range(lo, lo + 2 * l + 1)]
                rows.append(jnp.zeros((GROUP, EDGE), F32))
                y_ref[base + q, ROW_OF[l] : ROW_OF[l] + (2 * l + 2) * GROUP] = jnp.concatenate(
                    rows, axis=0
                ).astype(BF16)
        return carry

    lax.fori_loop(0, N_GROUP // CHUNK, radial_chunk, 0)
    rest.wait()
    for copy in halo:
        copy.wait()
    pl.semaphore_wait(plane_sem.at[1], 8)
    plane_signal(2)
    e_ref[...] = (flat[0].astype(F32) + shift).astype(BF16)

    def comp(m):
        return e_ref[...] if m == 0 else flat[m]

    def cross_unit(base, q, l):
        rad = r_ref[base + q, :, (DEG + l) * CH : (DEG + l + 1) * CH]
        part = (rad * s_ref[q]).astype(BF16)
        lhs = y_ref[base + q, ROW_OF[l] : ROW_OF[l] + (2 * l + 2) * GROUP]
        got = dot(lhs, part)
        for j in range(2 * l + 1):
            m = l * l + j
            cross_ref[base + q, :, m * CH : (m + 1) * CH] = got[j * GROUP : (j + 1) * GROUP, :]

    units = [(q, l) for l in range(DEG) for q in range(CHUNK)]

    def one_chunk(ch, carry):
        base = ch * CHUNK
        hot = oh_ref[pl.ds(base, CHUNK)].reshape(CHUNK * EDGE, MAXN)
        todo = list(units)
        for m in range(0, COMP, 2):
            comps = [m] + ([m + 1] if m + 1 < COMP else [])
            got = dot(hot, jnp.concatenate([comp(mm) for mm in comps], axis=1))
            if m == 0:
                s_ref[...] = got[:, 0:CH].reshape(CHUNK, EDGE, CH)
            else:
                for q, l in todo[:2]:
                    cross_unit(base, q, l)
                todo = todo[2:]
            for j, mm in enumerate(comps):
                l = degree_of(mm)
                part = got[:, j * CH : (j + 1) * CH].reshape(CHUNK, FAN, GROUP, CH)
                rad = r_ref[pl.ds(base, CHUNK), :, l * CH : (l + 1) * CH].reshape(
                    CHUNK, FAN, GROUP, CH
                )
                agg_ref[pl.ds(base, CHUNK), :, mm * CH : (mm + 1) * CH] = jnp.sum(
                    part * rad, axis=1
                )
        return carry

    lax.fori_loop(0, N_GROUP // CHUNK, one_chunk, 0)

    scale = 1.0 / math.sqrt(FAN)

    def agg_of(m):
        lanes = slice(m * CH, (m + 1) * CH)
        both = agg_ref[:, :, lanes] + cross_ref[:, :, lanes]
        return (both.reshape(ATOMS, CH) * scale).astype(BF16)

    gates = jax.nn.sigmoid(dot(agg_of(0), w_gate_ref[...]))
    for l in range(DEG):
        w_cat = jnp.concatenate([w_mix_ref[l], w_self_ref[l]], axis=0)
        for m in range(l * l, (l + 1) * (l + 1)):
            emb = comp(m)[0:ATOMS]
            mixed = dot(jnp.concatenate([agg_of(m), emb], axis=1), w_cat)
            if l == 0:
                add = mixed * jax.nn.sigmoid(mixed)
            else:
                add = mixed * gates[:, (l - 1) * CH : l * CH]
            upd_ref[m] = (emb.astype(F32) + add).astype(BF16)
    store = pltpu.make_async_copy(upd_ref, upd_hbm, load_sem.at[8])
    store.start()
    coef = dot(
        jnp.concatenate([upd_ref[m] for m in range(COMP)], axis=1), spread_ref[...], NT
    )
    put = jnp.where(iota((8, CH), 1) == iota((8, CH), 0) + 72, 1.0, 0.0).astype(BF16)
    coefs = jnp.concatenate(
        [coef[:, 0:CH], coef[:, CH:] + dot(pos8.astype(BF16), put, TN)], axis=0
    )
    r_row = jnp.broadcast_to(routes_ref[...].astype(F32), (ATOMS, ATOMS))
    r_col = r_row.T
    before = iota((ATOMS, ATOMS), 0) < iota((ATOMS, ATOMS), 1)
    rank = jnp.sum(
        jnp.where(before, jnp.where(r_col == r_row, 1.0, 0.0), 0.0), axis=0, keepdims=True
    )
    target = (r_row[0:1, :] * 4.0 + rank * 2.0).astype(jnp.int32)
    row = iota((512, ATOMS), 0)
    put_rows = jnp.concatenate(
        [jnp.where(row == target, 1.0, 0.0), jnp.where(row == target + 1, 1.0, 0.0)], axis=1
    ).astype(BF16)
    high = coefs.astype(BF16)
    low = (coefs - high.astype(F32)).astype(BF16)
    send_ref[...] = (dot(put_rows, high) + dot(put_rows, low)).reshape(128, 4, CH)
    pl.semaphore_wait(plane_sem.at[2], 8)
    count = ny * nz
    me = gy * nz + gz

    def post(j, carry):
        t = lax.rem(me + j, count)
        pltpu.make_async_remote_copy(
            src_ref=send_ref.at[t],
            dst_ref=recv_ref.at[me],
            send_sem=tile_sem.at[0],
            recv_sem=tile_sem.at[1],
            device_id=(gx, t // nz, lax.rem(t, nz)),
            device_id_type=MESH,
        ).start()
        return carry

    lax.fori_loop(1, count, post, 0)
    own = pltpu.make_async_copy(send_ref.at[me], recv_ref.at[me], tile_sem.at[2])
    own.start()
    own.wait()
    store.wait()
    part = pl.ds(0, count - 1)
    pltpu.make_async_copy(send_ref.at[part], recv_ref.at[part], tile_sem.at[0]).wait()
    pltpu.make_async_copy(send_ref.at[part], recv_ref.at[part], tile_sem.at[1]).wait()


def atom_call(ci, nbr, routes, pos, table, w_in, feats, w_out, w_mix, w_self, w_gate, w_read):
    vm = pl.BlockSpec(memory_space=pltpu.VMEM)
    hbm = pl.BlockSpec(memory_space=pl.ANY)
    return pl.pallas_call(
        atom_kernel,
        out_shape=(
            jax.ShapeDtypeStruct((COMP, ATOMS, CH), BF16),
            jax.ShapeDtypeStruct((128, 4, CH), F32),
        ),
        in_specs=[pl.BlockSpec(memory_space=pltpu.SMEM)] + [vm] * 5 + [hbm] * 6,
        out_specs=(hbm, hbm),
        scratch_shapes=[
            pltpu.VMEM((COMP + 1, 64, 4, CH), BF16),
            pltpu.VMEM((MAXN, CH), BF16),
            pltpu.VMEM((N_GROUP, EDGE, MAXN), BF16),
            pltpu.VMEM((3, N_GROUP, EDGE), F32),
            pltpu.VMEM((N_GROUP, COMP, EDGE), F32),
            pltpu.VMEM((N_GROUP, N_FUN, EDGE), F32),
            pltpu.VMEM((N_GROUP, ROWS, EDGE), BF16),
            pltpu.VMEM((N_GROUP, EDGE, 2 * DEG * CH), F32),
            pltpu.VMEM((CHUNK, EDGE, CH), F32),
            pltpu.VMEM((N_GROUP, GROUP, COMP * CH), F32),
            pltpu.VMEM((N_GROUP, GROUP, COMP * CH), F32),
            pltpu.VMEM((COMP, ATOMS, CH), BF16),
            pltpu.VMEM((128, 4, CH), F32),
            pltpu.VMEM((64, 2 * DEG * CH), BF16),
            pltpu.VMEM((DEG, CH, CH), BF16),
            pltpu.VMEM((DEG, CH, CH), BF16),
            pltpu.VMEM((CH, (DEG - 1) * CH), BF16),
            pltpu.VMEM((DEG, N_FUN, CH), BF16),
            pltpu.VMEM((MAXN, COMP * CH), BF16),
            pltpu.SemaphoreType.DMA((9,)),
            pltpu.SemaphoreType.DMA((27,)),
            pltpu.SemaphoreType.DMA((27,)),
            pltpu.SemaphoreType.DMA((27,)),
            pltpu.SemaphoreType.DMA((27,)),
            pltpu.SemaphoreType.DMA((3,)),
            pltpu.SemaphoreType.REGULAR((3,)),
        ],
        compiler_params=pltpu.CompilerParams(collective_id=0, has_side_effects=True),
        name="atoms",
    )(ci, nbr, routes, pos, table, w_in, feats, w_out, w_mix, w_self, w_gate, w_read)


PROBES = 256
SLOTS = 256


def density_kernel(
    probe_ref, pat_ref, recv_ref, upd_hbm, out_ref, atoms_hbm,
    ct_ref, px_ref, keep_ref, tot_ref, upd_ref, sem,
):
    take = pltpu.make_async_copy(upd_hbm, upd_ref, sem.at[0])
    give = pltpu.make_async_copy(upd_ref, atoms_hbm, sem.at[1])
    take.start()
    for h in range(2):
        ct_ref[h * CH : (h + 1) * CH, :] = recv_ref[pl.ds(h, SLOTS, stride=2), :].T
    px = jnp.concatenate([probe_ref[...], jnp.zeros((5, PROBES), F32)], axis=0)
    px_ref[...] = px.T
    pat = pat_ref[...].astype(F32).astype(BF16)
    spread = jnp.where(
        iota((SLOTS // 2, SLOTS), 0) == iota((SLOTS // 2, SLOTS), 1) // 2, 1.0, 0.0
    ).astype(BF16)
    keep_ref[...] = dot(pat, spread) * (1.0 / math.sqrt(SLOTS))
    rows = 16

    def block(i, carry):
        start = pl.multiple_of(i * rows, rows)
        p = px_ref[pl.ds(start, rows), :]
        rel = [p[:, c : c + 1] - ct_ref[200 + c : 201 + c, :] for c in range(3)]
        d, ux, uy, uz = geometry(*rel)
        total = [None] * N_FUN
        for m, val in enumerate(harmonics(ux, uy, uz)):
            for b in range(N_FUN):
                term = val * ct_ref[m * N_FUN + b : m * N_FUN + b + 1, :]
                total[b] = term if m == 0 else total[b] + term
        out = None
        for b, phi in enumerate(radial_funs(d)):
            out = phi * total[b] if out is None else out + phi * total[b]
        out = out * keep_ref[pl.ds(i // (PROBES // 2 // rows), 1), :]
        tot_ref[pl.ds(start, rows), :] = jnp.broadcast_to(
            jnp.sum(out, axis=1, keepdims=True), (rows, CH)
        )
        return carry

    steps = PROBES // rows
    lax.fori_loop(0, steps // 4, block, 0)
    take.wait()
    give.start()
    lax.fori_loop(steps // 4, steps, block, 0)
    for h in range(2):
        out_ref[h : h + 1, :] = tot_ref[h * CH : (h + 1) * CH, :].T[0:1, :]
    give.wait()


def density_call(probes, pattern, recv, upd):
    vm = pl.BlockSpec(memory_space=pltpu.VMEM)
    hbm = pl.BlockSpec(memory_space=pl.ANY)
    return pl.pallas_call(
        density_kernel,
        out_shape=(
            jax.ShapeDtypeStruct((2, CH), F32),
            jax.ShapeDtypeStruct((COMP, ATOMS, CH), BF16),
        ),
        in_specs=[vm] * 3 + [hbm],
        out_specs=(vm, hbm),
        scratch_shapes=[
            pltpu.VMEM((2 * CH, SLOTS), F32),
            pltpu.VMEM((PROBES, 8), F32),
            pltpu.VMEM((2, SLOTS), F32),
            pltpu.VMEM((PROBES, CH), F32),
            pltpu.VMEM((COMP, ATOMS, CH), BF16),
            pltpu.SemaphoreType.DMA((2,)),
        ],
        name="density",
    )(probes, pattern, recv, upd)


def per_device(
    features, positions, probe_positions, neighbours, routes, pattern, charge_index, charge_table,
    w_radial_in, w_radial_out, w_mix, w_self, w_gate, w_read,
):
    feats = jnp.transpose(features, (1, 0, 2)).reshape(COMP, 32, 4, CH)
    upd, recv = atom_call(
        charge_index, neighbours.T, routes.T, positions, charge_table, w_radial_in, feats,
        w_radial_out, w_mix, w_self, w_gate, jnp.transpose(w_read, (1, 0, 2)),
    )
    density, atoms = density_call(probe_positions, pattern, recv.reshape(512, CH), upd)
    return jnp.transpose(atoms, (1, 0, 2)), density.reshape(PROBES)


def solution(mesh):
    split = ("gx", "gy", "gz")
    rows = P(split, None)
    in_specs = (
        (P(split, None, None), P(None, split), P(None, split), rows, rows, rows) + (P(),) * 8
    )
    out_specs = (P(split, None, None), P(split))
    return jax.shard_map(
        per_device, mesh=mesh, in_specs=in_specs, out_specs=out_specs, check_vma=False
    )
```

```python
import functools, math
import jax
import jax.numpy as jnp
from jax import lax
from jax.experimental import pallas as pl
from jax.experimental.pallas import tpu as pltpu
from jax.sharding import PartitionSpec as P

F32 = jnp.float32
BF16 = jnp.bfloat16
CUTOFF = 8.0
WIDTH_R = 0.75
REACH = 6.0
FLOOR = 0.25
N_FUN = 8
DEG = 5
COMP = 25
CH = 128
ATOMS = 128
FAN = 20
GROUP = 8
N_GROUP = 16
EDGE = GROUP * FAN
CHUNK = 4
MAXN = 256


def degree_of(component):
    return int(math.isqrt(component))


def harmonics(x, y, z):
    xx, yy, zz = x * x, y * y, z * z
    c = math.sqrt
    return [
        jnp.ones_like(x),
        c(3.0) * y,
        c(3.0) * z,
        c(3.0) * x,
        c(15.0) * x * y,
        c(15.0) * y * z,
        0.5 * c(5.0) * (3.0 * zz - 1.0),
        c(15.0) * x * z,
        0.5 * c(15.0) * (xx - yy),
        c(35.0 / 8.0) * y * (3.0 * xx - yy),
        c(105.0) * x * y * z,
        c(21.0 / 8.0) * y * (5.0 * zz - 1.0),
        0.5 * c(7.0) * z * (5.0 * zz - 3.0),
        c(21.0 / 8.0) * x * (5.0 * zz - 1.0),
        0.5 * c(105.0) * z * (xx - yy),
        c(35.0 / 8.0) * x * (xx - 3.0 * yy),
        1.5 * c(35.0) * x * y * (xx - yy),
        1.5 * c(17.5) * y * z * (3.0 * xx - yy),
        1.5 * c(5.0) * x * y * (7.0 * zz - 1.0),
        1.5 * c(2.5) * y * z * (7.0 * zz - 3.0),
        0.375 * (35.0 * zz * zz - 30.0 * zz + 3.0),
        1.5 * c(2.5) * x * z * (7.0 * zz - 3.0),
        0.75 * c(5.0) * (xx - yy) * (7.0 * zz - 1.0),
        1.5 * c(17.5) * x * z * (xx - 3.0 * yy),
        0.375 * c(35.0) * (xx * xx - 6.0 * xx * yy + yy * yy),
    ]


def radial_funs(d):
    q = d * (1.0 / CUTOFF)
    env = 1.0 - q * q
    env = env * env
    out = []
    for b in range(N_FUN):
        v = (d - b * (REACH / (N_FUN - 1))) * (1.0 / WIDTH_R)
        out.append(jnp.exp(-(v * v)) * env)
    return out


def geometry(dx, dy, dz):
    d = jnp.sqrt(dx * dx + dy * dy + dz * dz)
    inv = 1.0 / jnp.maximum(d, FLOOR)
    return d, dx * inv, dy * inv, dz * inv


def iota(shape, dim):
    return lax.broadcasted_iota(jnp.int32, shape, dim)


def dot(a, b, dims=None):
    if dims is None:
        dims = (((1,), (0,)), ((), ()))
    return lax.dot_general(a, b, dims, preferred_element_type=F32)


NT = (((1,), (1,)), ((), ()))
TN = (((0,), (0,)), ((), ()))


MESH = pl.DeviceIdType.MESH
ROW_OF = (0, 16, 48, 96, 160)
ROWS = 240


def atom_kernel(
    ci_ref, nbr_ref, routes_ref, pos_ref, table_ref, w_in_ref, feats_hbm, w_out_hbm, w_mix_hbm,
    w_self_hbm, w_gate_hbm, w_read_hbm, upd_hbm, recv_ref,
    f_ref, e_ref, oh_ref, xyz_ref, ys_ref, bas_ref, y_ref, r_ref, s_ref, agg_ref, cross_ref,
    upd_ref, send_ref, w_out_ref, w_mix_ref, w_self_ref, w_gate_ref, w_read_ref, spread_ref,
    load_sem, pos_send, pos_recv, halo_send, halo_recv, tile_sem, plane_sem,
):
    gx, gy, gz = lax.axis_index("gx"), lax.axis_index("gy"), lax.axis_index("gz")
    nx, ny, nz = lax.axis_size("gx"), lax.axis_size("gy"), lax.axis_size("gz")

    def place(a, b, c):
        return (
            lax.rem(gx + a + nx, nx), lax.rem(gy + b + ny, ny), lax.rem(gz + c + nz, nz)
        )

    peers = [place(1 - n // 9, 1 - n // 3 % 3, 1 - n % 3) for n in range(27)]
    others = [n for n in range(27) if n != 13]
    around = [(b, c) for b in (-1, 0, 1) for c in (-1, 0, 1) if (b, c) != (0, 0)]

    def plane_signal(step):
        for b, c in around:
            pl.semaphore_signal(
                plane_sem.at[step],
                inc=1,
                device_id=place(0, b << step, c << step),
                device_id_type=MESH,
            )

    first = pltpu.make_async_copy(
        feats_hbm.at[:, 0:1], f_ref.at[0:COMP, 0:1], load_sem.at[0]
    )
    first.start()
    barrier = pltpu.get_barrier_semaphore()
    for n in others:
        pl.semaphore_signal(barrier, inc=1, device_id=peers[n], device_id_type=MESH)
    rest = pltpu.make_async_copy(
        feats_hbm.at[:, 1:32], f_ref.at[0:COMP, 1:32], load_sem.at[1]
    )
    loads = [
        pltpu.make_async_copy(src, dst, load_sem.at[2 + i])
        for i, (src, dst) in enumerate(
            (
                (w_out_hbm, w_out_ref),
                (w_mix_hbm, w_mix_ref),
                (w_self_hbm, w_self_ref),
                (w_gate_hbm, w_gate_ref),
                (w_read_hbm, w_read_ref),
            )
        )
    ]
    rest.start()
    for load in loads:
        load.start()
    pos = pos_ref[...].astype(F32)
    pos8 = jnp.concatenate(
        [pos, jnp.ones((1, ATOMS), F32), jnp.zeros((4, ATOMS), F32)], axis=0
    )
    eye = jnp.where(iota((8, CH), 1) == iota((8, CH), 0), 1.0, 0.0).astype(BF16)
    f_ref[COMP, 0] = dot(pos8.astype(BF16), eye, TN)[0:4].astype(BF16)
    f_ref[:, 59:64] = jnp.zeros((COMP + 1, 5, 4, CH), BF16)
    first.wait()
    pl.semaphore_wait(barrier, 26)
    sent, halo = [], []
    for n in others:
        copy = pltpu.make_async_remote_copy(
            src_ref=f_ref.at[COMP, 0],
            dst_ref=f_ref.at[COMP, 32 + n],
            send_sem=pos_send.at[n],
            recv_sem=pos_recv.at[n],
            device_id=peers[n],
            device_id_type=MESH,
        )
        copy.start()
        sent.append(copy)
    for n in others:
        copy = pltpu.make_async_remote_copy(
            src_ref=f_ref.at[0:COMP, 0],
            dst_ref=f_ref.at[0:COMP, 32 + n],
            send_sem=halo_send.at[n],
            recv_sem=halo_recv.at[n],
            device_id=peers[n],
            device_id_type=MESH,
        )
        copy.start()
        halo.append(copy)
    mine = pltpu.make_async_copy(f_ref.at[:, 0], f_ref.at[:, 45], load_sem.at[7])
    mine.start()
    plane_signal(0)
    nbr = jnp.concatenate(
        [nbr_ref[...].astype(F32), jnp.zeros((4, ATOMS), F32)], axis=0
    ).T
    col = iota((ATOMS, MAXN), 1).astype(F32)
    for k in range(0, FAN, 2):
        halves = []
        for kk in (k, k + 1):
            hot = jnp.where(nbr[:, kk : kk + 1] == col, 1.0, 0.0)
            halves.append(hot.reshape(N_GROUP, GROUP, MAXN))
        oh_ref[:, k * GROUP : (k + 2) * GROUP, :] = jnp.concatenate(halves, axis=1).astype(BF16)
    lvl = iota((8, CH), 0)
    shift = jnp.sum(
        jnp.where(lvl == ci_ref[0], table_ref[...].astype(F32), 0.0), axis=0, keepdims=True
    )
    flat = f_ref.reshape(COMP + 1, MAXN, CH)
    mine.wait()
    for load in loads:
        load.wait()
    spread_ref[...] = jnp.zeros((MAXN, COMP * CH), BF16)
    none8 = jnp.zeros((N_FUN, CH), F32)
    for m in range(COMP):
        one = w_read_ref[degree_of(m)].astype(F32)
        two = [one, none8] if m % 2 == 0 else [none8, one]
        start = (m - m % 2) * N_FUN
        spread_ref[start : start + 16, m * CH : (m + 1) * CH] = jnp.concatenate(
            two, axis=0
        ).astype(BF16)
    for copy in sent:
        copy.wait()
    gpos_t = flat[COMP, ATOMS:MAXN].astype(F32).T
    pt = jnp.concatenate([pos8, gpos_t[0:8]], axis=1).astype(BF16)
    own_group = iota((N_GROUP, ATOMS), 1) // GROUP == iota((N_GROUP, ATOMS), 0)
    tile_sel = jnp.where(
        iota((ATOMS, EDGE), 0) % GROUP == iota((ATOMS, EDGE), 1) % GROUP, 1.0, 0.0
    ).astype(BF16)
    for g in range(N_GROUP):
        got = dot(pt, oh_ref[g], NT)
        for c in range(3):
            xyz_ref[c, g : g + 1, :] = got[c : c + 1, :]
    rel = []
    for c in range(3):
        mine_c = jnp.where(own_group, pos[c : c + 1, :], 0.0).astype(BF16)
        rel.append(xyz_ref[c] - dot(mine_c, tile_sel))
    d, ux, uy, uz = geometry(*rel)
    for m, val in enumerate(harmonics(ux, uy, uz)):
        ys_ref[:, m, :] = val
    for b, val in enumerate(radial_funs(d)):
        bas_ref[:, b, :] = val
    mask8 = jnp.where(iota((GROUP, EDGE), 1) % GROUP == iota((GROUP, EDGE), 0), 1.0, 0.0)
    w_in = w_in_ref[...]
    pl.semaphore_wait(plane_sem.at[0], 8)
    plane_signal(1)

    def radial_chunk(ch, carry):
        base = ch * CHUNK
        for q in range(CHUNK):
            h = dot(bas_ref[base + q].astype(BF16), w_in, TN)
            h = (h * jax.nn.sigmoid(h)).astype(BF16)
            r_ref[base + q] = dot(h, w_out_ref[...])
            y = ys_ref[base + q]
            for l in range(DEG):
                lo = l * l
                rows = [y[m : m + 1, :] * mask8 for m in range(lo, lo + 2 * l + 1)]
                rows.append(jnp.zeros((GROUP, EDGE), F32))
                y_ref[base + q, ROW_OF[l] : ROW_OF[l] + (2 * l + 2) * GROUP] = jnp.concatenate(
                    rows, axis=0
                ).astype(BF16)
        return carry

    lax.fori_loop(0, N_GROUP // CHUNK, radial_chunk, 0)
    rest.wait()
    for copy in halo:
        copy.wait()
    pl.semaphore_wait(plane_sem.at[1], 8)
    plane_signal(2)
    e_ref[...] = (flat[0].astype(F32) + shift).astype(BF16)

    def comp(m):
        return e_ref[...] if m == 0 else flat[m]

    def cross_unit(base, q, l):
        rad = r_ref[base + q, :, (DEG + l) * CH : (DEG + l + 1) * CH]
        part = (rad * s_ref[q]).astype(BF16)
        lhs = y_ref[base + q, ROW_OF[l] : ROW_OF[l] + (2 * l + 2) * GROUP]
        got = dot(lhs, part)
        for j in range(2 * l + 1):
            m = l * l + j
            cross_ref[base + q, :, m * CH : (m + 1) * CH] = got[j * GROUP : (j + 1) * GROUP, :]

    units = [(q, l) for l in range(DEG) for q in range(CHUNK)]

    def one_chunk(ch, carry):
        base = ch * CHUNK
        hot = oh_ref[pl.ds(base, CHUNK)].reshape(CHUNK * EDGE, MAXN)
        todo = list(units)
        for m in range(0, COMP, 2):
            comps = [m] + ([m + 1] if m + 1 < COMP else [])
            got = dot(hot, jnp.concatenate([comp(mm) for mm in comps], axis=1))
            if m == 0:
                s_ref[...] = got[:, 0:CH].reshape(CHUNK, EDGE, CH)
            else:
                for q, l in todo[:2]:
                    cross_unit(base, q, l)
                todo = todo[2:]
            for j, mm in enumerate(comps):
                l = degree_of(mm)
                part = got[:, j * CH : (j + 1) * CH].reshape(CHUNK, FAN, GROUP, CH)
                rad = r_ref[pl.ds(base, CHUNK), :, l * CH : (l + 1) * CH].reshape(
                    CHUNK, FAN, GROUP, CH
                )
                agg_ref[pl.ds(base, CHUNK), :, mm * CH : (mm + 1) * CH] = jnp.sum(
                    part * rad, axis=1
                )
        return carry

    lax.fori_loop(0, N_GROUP // CHUNK, one_chunk, 0)

    scale = 1.0 / math.sqrt(FAN)

    def agg_of(m):
        lanes = slice(m * CH, (m + 1) * CH)
        both = agg_ref[:, :, lanes] + cross_ref[:, :, lanes]
        return (both.reshape(ATOMS, CH) * scale).astype(BF16)

    gates = jax.nn.sigmoid(dot(agg_of(0), w_gate_ref[...]))
    for l in range(DEG):
        w_cat = jnp.concatenate([w_mix_ref[l], w_self_ref[l]], axis=0)
        for m in range(l * l, (l + 1) * (l + 1)):
            emb = comp(m)[0:ATOMS]
            mixed = dot(jnp.concatenate([agg_of(m), emb], axis=1), w_cat)
            if l == 0:
                add = mixed * jax.nn.sigmoid(mixed)
            else:
                add = mixed * gates[:, (l - 1) * CH : l * CH]
            upd_ref[m] = (emb.astype(F32) + add).astype(BF16)
    store = pltpu.make_async_copy(upd_ref, upd_hbm, load_sem.at[8])
    store.start()
    coef = dot(
        jnp.concatenate([upd_ref[m] for m in range(COMP)], axis=1), spread_ref[...], NT
    )
    put = jnp.where(iota((8, CH), 1) == iota((8, CH), 0) + 72, 1.0, 0.0).astype(BF16)
    coefs = [coef[:, 0:CH], coef[:, CH:] + dot(pos8.astype(BF16), put, TN)]
    r_row = jnp.broadcast_to(routes_ref[...].astype(F32), (ATOMS, ATOMS))
    r_col = r_row.T
    before = iota((ATOMS, ATOMS), 0) < iota((ATOMS, ATOMS), 1)
    rank = jnp.sum(
        jnp.where(before, jnp.where(r_col == r_row, 1.0, 0.0), 0.0), axis=0, keepdims=True
    )
    target = (r_row[0:1, :] * 2.0 + rank).astype(jnp.int32)
    put_rows = jnp.where(iota((MAXN, ATOMS), 0) == target, 1.0, 0.0).astype(BF16)
    flat_send = send_ref.reshape(2, 2 * 128, CH)
    for h in range(2):
        flat_send[h] = dot(put_rows, coefs[h].astype(BF16)).astype(BF16)
    pl.semaphore_wait(plane_sem.at[2], 8)
    count = ny * nz
    me = gy * nz + gz

    def post(j, carry):
        t = lax.rem(me + j, count)
        pltpu.make_async_remote_copy(
            src_ref=send_ref.at[:, t],
            dst_ref=recv_ref.at[:, me],
            send_sem=tile_sem.at[0],
            recv_sem=tile_sem.at[1],
            device_id=(gx, t // nz, lax.rem(t, nz)),
            device_id_type=MESH,
        ).start()
        return carry

    lax.fori_loop(1, count, post, 0)
    own = pltpu.make_async_copy(send_ref.at[:, me], recv_ref.at[:, me], tile_sem.at[2])
    own.start()
    own.wait()
    store.wait()
    part = pl.ds(0, count - 1)
    pltpu.make_async_copy(send_ref.at[:, part], recv_ref.at[:, part], tile_sem.at[0]).wait()
    pltpu.make_async_copy(send_ref.at[:, part], recv_ref.at[:, part], tile_sem.at[1]).wait()


def atom_call(ci, nbr, routes, pos, table, w_in, feats, w_out, w_mix, w_self, w_gate, w_read):
    vm = pl.BlockSpec(memory_space=pltpu.VMEM)
    hbm = pl.BlockSpec(memory_space=pl.ANY)
    return pl.pallas_call(
        atom_kernel,
        out_shape=(
            jax.ShapeDtypeStruct((COMP, ATOMS, CH), BF16),
            jax.ShapeDtypeStruct((2, 128, 2, CH), BF16),
        ),
        in_specs=[pl.BlockSpec(memory_space=pltpu.SMEM)] + [vm] * 5 + [hbm] * 6,
        out_specs=(hbm, hbm),
        scratch_shapes=[
            pltpu.VMEM((COMP + 1, 64, 4, CH), BF16),
            pltpu.VMEM((MAXN, CH), BF16),
            pltpu.VMEM((N_GROUP, EDGE, MAXN), BF16),
            pltpu.VMEM((3, N_GROUP, EDGE), F32),
            pltpu.VMEM((N_GROUP, COMP, EDGE), F32),
            pltpu.VMEM((N_GROUP, N_FUN, EDGE), F32),
            pltpu.VMEM((N_GROUP, ROWS, EDGE), BF16),
            pltpu.VMEM((N_GROUP, EDGE, 2 * DEG * CH), F32),
            pltpu.VMEM((CHUNK, EDGE, CH), F32),
            pltpu.VMEM((N_GROUP, GROUP, COMP * CH), F32),
            pltpu.VMEM((N_GROUP, GROUP, COMP * CH), F32),
            pltpu.VMEM((COMP, ATOMS, CH), BF16),
            pltpu.VMEM((2, 128, 2, CH), BF16),
            pltpu.VMEM((64, 2 * DEG * CH), BF16),
            pltpu.VMEM((DEG, CH, CH), BF16),
            pltpu.VMEM((DEG, CH, CH), BF16),
            pltpu.VMEM((CH, (DEG - 1) * CH), BF16),
            pltpu.VMEM((DEG, N_FUN, CH), BF16),
            pltpu.VMEM((MAXN, COMP * CH), BF16),
            pltpu.SemaphoreType.DMA((9,)),
            pltpu.SemaphoreType.DMA((27,)),
            pltpu.SemaphoreType.DMA((27,)),
            pltpu.SemaphoreType.DMA((27,)),
            pltpu.SemaphoreType.DMA((27,)),
            pltpu.SemaphoreType.DMA((3,)),
            pltpu.SemaphoreType.REGULAR((3,)),
        ],
        compiler_params=pltpu.CompilerParams(collective_id=0, has_side_effects=True),
        name="atoms",
    )(ci, nbr, routes, pos, table, w_in, feats, w_out, w_mix, w_self, w_gate, w_read)


PROBES = 256
SLOTS = 256
BLOCK = 128
UNIT = 16
ROWS_C = 208


def split3(x):
    high = x.astype(BF16)
    x = x - high.astype(F32)
    mid = x.astype(BF16)
    return high, mid, (x - mid.astype(F32)).astype(BF16)


def density_kernel(
    probe_ref, pat_ref, recv_ref, upd_hbm, out_ref, atoms_hbm, rt_ref, px_ref, ct_ref, w_ref,
    upd_ref, sem,
):
    take = pltpu.make_async_copy(upd_hbm, upd_ref, sem.at[0])
    give = pltpu.make_async_copy(upd_ref, atoms_hbm, sem.at[1])
    take.start()
    keep = iota((8, 64), 1) % 8 == iota((8, 64), 0)
    rows = []
    for c in range(3):
        for q in range(4):
            rows.append(
                jnp.where(keep, probe_ref[c : c + 1, q * 64 : (q + 1) * 64], 0.0)
            )
    rows = jnp.concatenate(rows, axis=0)
    widen = jnp.where(iota((64, CH), 0) // 8 == iota((64, CH), 1) // UNIT, 1.0, 0.0).astype(BF16)
    high, mid, low = split3(rows)
    px_ref[...] = (dot(low, widen) + dot(mid, widen)) + dot(high, widen)
    spread = jnp.where(
        iota((SLOTS // 2, SLOTS), 0) == iota((SLOTS // 2, SLOTS), 1) // 2, 1.0, 0.0
    ).astype(BF16)
    wanted = dot(pat_ref[...].astype(F32).astype(BF16), spread)
    before = jnp.where(
        iota((SLOTS, SLOTS), 0) < iota((SLOTS, SLOTS), 1), 1.0, 0.0
    ).astype(BF16)
    for h in range(2):
        rt_ref[h * CH : (h + 1) * CH, :] = (
            recv_ref[h * SLOTS : (h + 1) * SLOTS, :].astype(F32).T.astype(BF16)
        )
    active = wanted * rt_ref[192:208, :].astype(F32)[11:12, :]
    rank = dot(active.astype(BF16), before)
    w_ref[...] = jnp.where(active > 0.5, rank, -1.0)
    most = jnp.max(jnp.sum(active, axis=1, keepdims=True)).astype(jnp.int32)
    place = (iota((BLOCK, SLOTS), 0) % UNIT).astype(F32)

    def fetch(u, buf):
        at = place + (u * UNIT).astype(F32)
        pick = jnp.concatenate(
            [jnp.where(at == w_ref[k : k + 1, :], 1.0, 0.0) for k in range(2)], axis=0
        ).astype(BF16)
        ct_ref[buf] = dot(rt_ref[0:ROWS_C, :], pick, NT)

    def add_unit(buf, totals):
        out = []
        for k in range(2):
            lanes = slice(k * BLOCK, (k + 1) * BLOCK)

            def row(j):
                return ct_ref[buf, j : j + 1, lanes]

            rel = [
                px_ref[c * 32 + k * 16 : c * 32 + (k + 1) * 16, :] - row(200 + c)
                for c in range(3)
            ]
            d, ux, uy, uz = geometry(*rel)
            total = [None] * N_FUN
            for m, val in enumerate(harmonics(ux, uy, uz)):
                for b in range(N_FUN):
                    term = row(m * N_FUN + b)
                    total[b] = term if m == 0 else total[b] + val * term
            add = totals[k]
            for b, phi in enumerate(radial_funs(d)):
                add = add + phi * total[b]
            out.append(add)
        return tuple(out)

    fetch(jnp.int32(0), 0)

    def two_units(i, totals):
        fetch(2 * i + 1, 1)
        totals = add_unit(0, totals)
        fetch(2 * i + 2, 0)
        return add_unit(1, totals)

    zero = jnp.zeros((16, BLOCK), F32)
    totals = two_units(jnp.int32(0), (zero, zero))
    take.wait()
    give.start()
    totals = lax.fori_loop(1, (most + 2 * UNIT - 1) // (2 * UNIT), two_units, totals)
    narrow = jnp.where(iota((CH, 64), 0) // UNIT == iota((CH, 64), 1) // 8, 1.0, 0.0).astype(BF16)
    high, mid, low = split3(jnp.concatenate(totals, axis=0))
    sums = (dot(low, narrow) + dot(mid, narrow)) + dot(high, narrow)
    for q in range(4):
        part = jnp.where(keep, sums[q * 8 : (q + 1) * 8], 0.0)
        out_ref[q // 2 : q // 2 + 1, (q % 2) * 64 : (q % 2 + 1) * 64] = jnp.sum(
            part, axis=0, keepdims=True
        ) * (1.0 / math.sqrt(SLOTS))
    give.wait()


def density_call(probes, pattern, recv, upd):
    vm = pl.BlockSpec(memory_space=pltpu.VMEM)
    hbm = pl.BlockSpec(memory_space=pl.ANY)
    return pl.pallas_call(
        density_kernel,
        out_shape=(
            jax.ShapeDtypeStruct((2, CH), F32),
            jax.ShapeDtypeStruct((COMP, ATOMS, CH), BF16),
        ),
        in_specs=[vm] * 3 + [hbm],
        out_specs=(vm, hbm),
        scratch_shapes=[
            pltpu.VMEM((2 * CH, SLOTS), BF16),
            pltpu.VMEM((96, CH), F32),
            pltpu.VMEM((2, ROWS_C, 2 * BLOCK), F32),
            pltpu.VMEM((2, SLOTS), F32),
            pltpu.VMEM((COMP, ATOMS, CH), BF16),
            pltpu.SemaphoreType.DMA((2,)),
        ],
        name="density",
    )(probes, pattern, recv, upd)


def per_device(
    features, positions, probe_positions, neighbours, routes, pattern, charge_index, charge_table,
    w_radial_in, w_radial_out, w_mix, w_self, w_gate, w_read,
):
    feats = jnp.transpose(features, (1, 0, 2)).reshape(COMP, 32, 4, CH)
    upd, recv = atom_call(
        charge_index, neighbours.T, routes.T, positions, charge_table, w_radial_in, feats,
        w_radial_out, w_mix, w_self, w_gate, jnp.transpose(w_read, (1, 0, 2)),
    )
    density, atoms = density_call(probe_positions, pattern, recv.reshape(512, CH), upd)
    return jnp.transpose(atoms, (1, 0, 2)), density.reshape(PROBES)


def solution(mesh):
    split = ("gx", "gy", "gz")
    rows = P(split, None)
    in_specs = (
        (P(split, None, None), P(None, split), P(None, split), rows, rows, rows) + (P(),) * 8
    )
    out_specs = (P(split, None, None), P(split))
    return jax.shard_map(
        per_device, mesh=mesh, in_specs=in_specs, out_specs=out_specs, check_vma=False
    )
```

```python
import functools, math
import jax
import jax.numpy as jnp
from jax import lax
from jax.experimental import pallas as pl
from jax.experimental.pallas import tpu as pltpu
from jax.sharding import PartitionSpec as P

F32 = jnp.float32
BF16 = jnp.bfloat16
CUTOFF = 8.0
WIDTH_R = 0.75
REACH = 6.0
FLOOR = 0.25
N_FUN = 8
DEG = 5
COMP = 25
CH = 128
ATOMS = 128
FAN = 20
GROUP = 8
N_GROUP = 16
EDGE = GROUP * FAN
CHUNK = 4
MAXN = 256


def degree_of(component):
    return int(math.isqrt(component))


def harmonics(x, y, z):
    xx, yy, zz = x * x, y * y, z * z
    c = math.sqrt
    return [
        jnp.ones_like(x),
        c(3.0) * y,
        c(3.0) * z,
        c(3.0) * x,
        c(15.0) * x * y,
        c(15.0) * y * z,
        0.5 * c(5.0) * (3.0 * zz - 1.0),
        c(15.0) * x * z,
        0.5 * c(15.0) * (xx - yy),
        c(35.0 / 8.0) * y * (3.0 * xx - yy),
        c(105.0) * x * y * z,
        c(21.0 / 8.0) * y * (5.0 * zz - 1.0),
        0.5 * c(7.0) * z * (5.0 * zz - 3.0),
        c(21.0 / 8.0) * x * (5.0 * zz - 1.0),
        0.5 * c(105.0) * z * (xx - yy),
        c(35.0 / 8.0) * x * (xx - 3.0 * yy),
        1.5 * c(35.0) * x * y * (xx - yy),
        1.5 * c(17.5) * y * z * (3.0 * xx - yy),
        1.5 * c(5.0) * x * y * (7.0 * zz - 1.0),
        1.5 * c(2.5) * y * z * (7.0 * zz - 3.0),
        0.375 * (35.0 * zz * zz - 30.0 * zz + 3.0),
        1.5 * c(2.5) * x * z * (7.0 * zz - 3.0),
        0.75 * c(5.0) * (xx - yy) * (7.0 * zz - 1.0),
        1.5 * c(17.5) * x * z * (xx - 3.0 * yy),
        0.375 * c(35.0) * (xx * xx - 6.0 * xx * yy + yy * yy),
    ]


def radial_funs(d):
    q = d * (1.0 / CUTOFF)
    env = 1.0 - q * q
    env = env * env
    out = []
    for b in range(N_FUN):
        v = (d - b * (REACH / (N_FUN - 1))) * (1.0 / WIDTH_R)
        out.append(jnp.exp(-(v * v)) * env)
    return out


def geometry(dx, dy, dz):
    d = jnp.sqrt(dx * dx + dy * dy + dz * dz)
    inv = 1.0 / jnp.maximum(d, FLOOR)
    return d, dx * inv, dy * inv, dz * inv


def iota(shape, dim):
    return lax.broadcasted_iota(jnp.int32, shape, dim)


def dot(a, b, dims=None):
    if dims is None:
        dims = (((1,), (0,)), ((), ()))
    return lax.dot_general(a, b, dims, preferred_element_type=F32)


NT = (((1,), (1,)), ((), ()))
TN = (((0,), (0,)), ((), ()))


MESH = pl.DeviceIdType.MESH
ROW_OF = (0, 16, 48, 96, 160)
ROWS = 240
PARTS = ((0, 10), (10, 18), (18, 25))


def atom_kernel(
    ci_ref, nbr_ref, routes_ref, pos_ref, table_ref, w_in_ref, feats_hbm, w_out_hbm, w_mix_hbm,
    w_self_hbm, w_gate_hbm, w_read_hbm, upd_hbm, recv_ref,
    f_ref, e_ref, oh_ref, xyz_ref, ys_ref, bas_ref, y_ref, r_ref, s_ref, agg_ref, cross_ref,
    upd_ref, send_ref, gate_ref, w_out_ref, w_mix_ref, w_self_ref, w_gate_ref, w_read_ref, spread_ref,
    load_sem, pos_send, pos_recv, halo_send, halo_recv, tile_sem, plane_sem,
):
    gx, gy, gz = lax.axis_index("gx"), lax.axis_index("gy"), lax.axis_index("gz")
    nx, ny, nz = lax.axis_size("gx"), lax.axis_size("gy"), lax.axis_size("gz")

    def place(a, b, c):
        return (
            lax.rem(gx + a + nx, nx), lax.rem(gy + b + ny, ny), lax.rem(gz + c + nz, nz)
        )

    peers = [place(1 - n // 9, 1 - n // 3 % 3, 1 - n % 3) for n in range(27)]
    others = [n for n in range(27) if n != 13]
    around = [(b, c) for b in (-1, 0, 1) for c in (-1, 0, 1) if (b, c) != (0, 0)]

    def plane_signal(step):
        for b, c in around:
            pl.semaphore_signal(
                plane_sem.at[step],
                inc=1,
                device_id=place(0, b << step, c << step),
                device_id_type=MESH,
            )

    first = pltpu.make_async_copy(
        feats_hbm.at[:, 0:1], f_ref.at[0:COMP, 0:1], load_sem.at[0]
    )
    first.start()
    barrier = pltpu.get_barrier_semaphore()
    for n in others:
        pl.semaphore_signal(barrier, inc=1, device_id=peers[n], device_id_type=MESH)
    rest = pltpu.make_async_copy(
        feats_hbm.at[:, 1:32], f_ref.at[0:COMP, 1:32], load_sem.at[1]
    )
    loads = [
        pltpu.make_async_copy(src, dst, load_sem.at[2 + i])
        for i, (src, dst) in enumerate(
            (
                (w_out_hbm, w_out_ref),
                (w_mix_hbm, w_mix_ref),
                (w_self_hbm, w_self_ref),
                (w_gate_hbm, w_gate_ref),
                (w_read_hbm, w_read_ref),
            )
        )
    ]
    rest.start()
    for load in loads:
        load.start()
    pos = pos_ref[...].astype(F32)
    pos8 = jnp.concatenate(
        [pos, jnp.ones((1, ATOMS), F32), jnp.zeros((4, ATOMS), F32)], axis=0
    )
    eye = jnp.where(iota((8, CH), 1) == iota((8, CH), 0), 1.0, 0.0).astype(BF16)
    f_ref[COMP, 0] = dot(pos8.astype(BF16), eye, TN)[0:4].astype(BF16)
    f_ref[:, 59:64] = jnp.zeros((COMP + 1, 5, 4, CH), BF16)
    first.wait()
    pl.semaphore_wait(barrier, 26)
    sent, halo = [], []
    for n in others:
        copy = pltpu.make_async_remote_copy(
            src_ref=f_ref.at[COMP, 0],
            dst_ref=f_ref.at[COMP, 32 + n],
            send_sem=pos_send.at[n],
            recv_sem=pos_recv.at[n],
            device_id=peers[n],
            device_id_type=MESH,
        )
        copy.start()
        sent.append(copy)
    for part, (lo, hi) in enumerate(PARTS):
        for n in others:
            copy = pltpu.make_async_remote_copy(
                src_ref=f_ref.at[lo:hi, 0],
                dst_ref=f_ref.at[lo:hi, 32 + n],
                send_sem=halo_send.at[part, n],
                recv_sem=halo_recv.at[part, n],
                device_id=peers[n],
                device_id_type=MESH,
            )
            copy.start()
            halo.append(copy)
    mine = pltpu.make_async_copy(f_ref.at[:, 0], f_ref.at[:, 45], load_sem.at[7])
    mine.start()
    plane_signal(0)
    nbr = jnp.concatenate(
        [nbr_ref[...].astype(F32), jnp.zeros((4, ATOMS), F32)], axis=0
    ).T
    col = iota((ATOMS, MAXN), 1).astype(F32)
    for k in range(0, FAN, 2):
        halves = []
        for kk in (k, k + 1):
            hot = jnp.where(nbr[:, kk : kk + 1] == col, 1.0, 0.0)
            halves.append(hot.reshape(N_GROUP, GROUP, MAXN))
        oh_ref[:, k * GROUP : (k + 2) * GROUP, :] = jnp.concatenate(halves, axis=1).astype(BF16)
    lvl = iota((8, CH), 0)
    shift = jnp.sum(
        jnp.where(lvl == ci_ref[0], table_ref[...].astype(F32), 0.0), axis=0, keepdims=True
    )
    flat = f_ref.reshape(COMP + 1, MAXN, CH)
    mine.wait()
    for load in loads:
        load.wait()
    spread_ref[...] = jnp.zeros((MAXN, COMP * CH), BF16)
    none8 = jnp.zeros((N_FUN, CH), F32)
    for m in range(COMP):
        one = w_read_ref[degree_of(m)].astype(F32)
        two = [one, none8] if m % 2 == 0 else [none8, one]
        start = (m - m % 2) * N_FUN
        spread_ref[start : start + 16, m * CH : (m + 1) * CH] = jnp.concatenate(
            two, axis=0
        ).astype(BF16)
    for copy in sent:
        copy.wait()
    gpos_t = flat[COMP, ATOMS:MAXN].astype(F32).T
    pt = jnp.concatenate([pos8, gpos_t[0:8]], axis=1).astype(BF16)
    own_group = iota((N_GROUP, ATOMS), 1) // GROUP == iota((N_GROUP, ATOMS), 0)
    tile_sel = jnp.where(
        iota((ATOMS, EDGE), 0) % GROUP == iota((ATOMS, EDGE), 1) % GROUP, 1.0, 0.0
    ).astype(BF16)
    for g in range(N_GROUP):
        got = dot(pt, oh_ref[g], NT)
        for c in range(3):
            xyz_ref[c, g : g + 1, :] = got[c : c + 1, :]
    rel = []
    for c in range(3):
        mine_c = jnp.where(own_group, pos[c : c + 1, :], 0.0).astype(BF16)
        rel.append(xyz_ref[c] - dot(mine_c, tile_sel))
    d, ux, uy, uz = geometry(*rel)
    for m, val in enumerate(harmonics(ux, uy, uz)):
        ys_ref[:, m, :] = val
    for b, val in enumerate(radial_funs(d)):
        bas_ref[:, b, :] = val
    mask8 = jnp.where(iota((GROUP, EDGE), 1) % GROUP == iota((GROUP, EDGE), 0), 1.0, 0.0)
    w_in = w_in_ref[...]
    pl.semaphore_wait(plane_sem.at[0], 8)
    plane_signal(1)

    def radial_chunk(ch, carry):
        base = ch * CHUNK
        for q in range(CHUNK):
            h = dot(bas_ref[base + q].astype(BF16), w_in, TN)
            h = (h * jax.nn.sigmoid(h)).astype(BF16)
            r_ref[base + q] = dot(h, w_out_ref[...])
            y = ys_ref[base + q]
            for l in range(DEG):
                lo = l * l
                rows = [y[m : m + 1, :] * mask8 for m in range(lo, lo + 2 * l + 1)]
                rows.append(jnp.zeros((GROUP, EDGE), F32))
                y_ref[base + q, ROW_OF[l] : ROW_OF[l] + (2 * l + 2) * GROUP] = jnp.concatenate(
                    rows, axis=0
                ).astype(BF16)
        return carry

    lax.fori_loop(0, N_GROUP // CHUNK, radial_chunk, 0)
    rest.wait()
    scale = 1.0 / math.sqrt(FAN)

    def comp(m):
        return e_ref[...] if m == 0 else flat[m]

    def cross_chunk(ch, carry):
        base = ch * CHUNK
        for l in range(DEG):
            for q in range(CHUNK):
                rad = r_ref[base + q, :, (DEG + l) * CH : (DEG + l + 1) * CH]
                part = (rad * s_ref[base + q]).astype(BF16)
                lhs = y_ref[base + q, ROW_OF[l] : ROW_OF[l] + (2 * l + 2) * GROUP]
                got = dot(lhs, part)
                for j in range(2 * l + 1):
                    m = l * l + j
                    cross_ref[base + q, :, m * CH : (m + 1) * CH] = got[
                        j * GROUP : (j + 1) * GROUP, :
                    ]
        return carry

    def agg_of(m):
        lanes = slice(m * CH, (m + 1) * CH)
        both = agg_ref[:, :, lanes] + cross_ref[:, :, lanes]
        return (both.reshape(ATOMS, CH) * scale).astype(BF16)

    def gather_part(lo, hi):
        def one_chunk(ch, carry):
            base = ch * CHUNK
            hot = oh_ref[pl.ds(base, CHUNK)].reshape(CHUNK * EDGE, MAXN)
            for m in range(lo, hi, 2):
                comps = list(range(m, min(m + 2, hi)))
                got = dot(hot, jnp.concatenate([comp(mm) for mm in comps], axis=1))
                if m == 0:
                    s_ref[pl.ds(base, CHUNK)] = got[:, 0:CH].reshape(CHUNK, EDGE, CH)
                for j, mm in enumerate(comps):
                    l = degree_of(mm)
                    part = got[:, j * CH : (j + 1) * CH].reshape(CHUNK, FAN, GROUP, CH)
                    rad = r_ref[pl.ds(base, CHUNK), :, l * CH : (l + 1) * CH].reshape(
                        CHUNK, FAN, GROUP, CH
                    )
                    agg_ref[pl.ds(base, CHUNK), :, mm * CH : (mm + 1) * CH] = jnp.sum(
                        part * rad, axis=1
                    )
            return carry

        lax.fori_loop(0, N_GROUP // CHUNK, one_chunk, 0)

    for part, (lo, hi) in enumerate(PARTS):
        for copy in halo[part * len(others) : (part + 1) * len(others)]:
            copy.wait()
        if part == 0:
            pl.semaphore_wait(plane_sem.at[1], 8)
            plane_signal(2)
            e_ref[...] = (flat[0].astype(F32) + shift).astype(BF16)
        gather_part(lo, hi)
        if part == 0:
            lax.fori_loop(0, N_GROUP // CHUNK, cross_chunk, 0)
            gate_ref[...] = jax.nn.sigmoid(dot(agg_of(0), w_gate_ref[...]))
        for m in range(lo, hi):
            l = degree_of(m)
            w_cat = jnp.concatenate([w_mix_ref[l], w_self_ref[l]], axis=0)
            emb = comp(m)[0:ATOMS]
            mixed = dot(jnp.concatenate([agg_of(m), emb], axis=1), w_cat)
            if l == 0:
                add = mixed * jax.nn.sigmoid(mixed)
            else:
                add = mixed * gate_ref[:, (l - 1) * CH : l * CH]
            upd_ref[m] = (emb.astype(F32) + add).astype(BF16)
    store = pltpu.make_async_copy(upd_ref, upd_hbm, load_sem.at[8])
    store.start()
    coef = dot(
        jnp.concatenate([upd_ref[m] for m in range(COMP)], axis=1), spread_ref[...], NT
    )
    put = jnp.where(iota((8, CH), 1) == iota((8, CH), 0) + 72, 1.0, 0.0).astype(BF16)
    coefs = [coef[:, 0:CH], coef[:, CH:] + dot(pos8.astype(BF16), put, TN)]
    r_row = jnp.broadcast_to(routes_ref[...].astype(F32), (ATOMS, ATOMS))
    r_col = r_row.T
    before = iota((ATOMS, ATOMS), 0) < iota((ATOMS, ATOMS), 1)
    rank = jnp.sum(
        jnp.where(before, jnp.where(r_col == r_row, 1.0, 0.0), 0.0), axis=0, keepdims=True
    )
    target = (r_row[0:1, :] * 2.0 + rank).astype(jnp.int32)
    put_rows = jnp.where(iota((MAXN, ATOMS), 0) == target, 1.0, 0.0).astype(BF16)
    flat_send = send_ref.reshape(2, 2 * 128, CH)
    for h in range(2):
        flat_send[h] = dot(put_rows, coefs[h].astype(BF16)).astype(BF16)
    pl.semaphore_wait(plane_sem.at[2], 8)
    count = ny * nz
    me = gy * nz + gz

    def post(j, carry):
        jy, jz = j // nz, lax.rem(j, nz)
        ty = ny // 2 + (jy + 1) // 2 * (1 - 2 * lax.rem(jy, 2))
        tz = nz // 2 + (jz + 1) // 2 * (1 - 2 * lax.rem(jz, 2))
        ty, tz = lax.rem(gy + ty, ny), lax.rem(gz + tz, nz)
        t = ty * nz + tz
        pltpu.make_async_remote_copy(
            src_ref=send_ref.at[:, t],
            dst_ref=recv_ref.at[:, me],
            send_sem=tile_sem.at[0],
            recv_sem=tile_sem.at[1],
            device_id=(gx, ty, tz),
            device_id_type=MESH,
        ).start()
        return carry

    lax.fori_loop(0, count - 1, post, 0)
    own = pltpu.make_async_copy(send_ref.at[:, me], recv_ref.at[:, me], tile_sem.at[2])
    own.start()
    own.wait()
    store.wait()
    part = pl.ds(0, count - 1)
    pltpu.make_async_copy(send_ref.at[:, part], recv_ref.at[:, part], tile_sem.at[0]).wait()
    pltpu.make_async_copy(send_ref.at[:, part], recv_ref.at[:, part], tile_sem.at[1]).wait()


def atom_call(ci, nbr, routes, pos, table, w_in, feats, w_out, w_mix, w_self, w_gate, w_read):
    vm = pl.BlockSpec(memory_space=pltpu.VMEM)
    hbm = pl.BlockSpec(memory_space=pl.ANY)
    return pl.pallas_call(
        atom_kernel,
        out_shape=(
            jax.ShapeDtypeStruct((COMP, ATOMS, CH), BF16),
            jax.ShapeDtypeStruct((2, 128, 2, CH), BF16),
        ),
        in_specs=[pl.BlockSpec(memory_space=pltpu.SMEM)] + [vm] * 5 + [hbm] * 6,
        out_specs=(hbm, hbm),
        scratch_shapes=[
            pltpu.VMEM((COMP + 1, 64, 4, CH), BF16),
            pltpu.VMEM((MAXN, CH), BF16),
            pltpu.VMEM((N_GROUP, EDGE, MAXN), BF16),
            pltpu.VMEM((3, N_GROUP, EDGE), F32),
            pltpu.VMEM((N_GROUP, COMP, EDGE), F32),
            pltpu.VMEM((N_GROUP, N_FUN, EDGE), F32),
            pltpu.VMEM((N_GROUP, ROWS, EDGE), BF16),
            pltpu.VMEM((N_GROUP, EDGE, 2 * DEG * CH), F32),
            pltpu.VMEM((N_GROUP, EDGE, CH), F32),
            pltpu.VMEM((N_GROUP, GROUP, COMP * CH), F32),
            pltpu.VMEM((N_GROUP, GROUP, COMP * CH), F32),
            pltpu.VMEM((COMP, ATOMS, CH), BF16),
            pltpu.VMEM((2, 128, 2, CH), BF16),
            pltpu.VMEM((ATOMS, (DEG - 1) * CH), F32),
            pltpu.VMEM((64, 2 * DEG * CH), BF16),
            pltpu.VMEM((DEG, CH, CH), BF16),
            pltpu.VMEM((DEG, CH, CH), BF16),
            pltpu.VMEM((CH, (DEG - 1) * CH), BF16),
            pltpu.VMEM((DEG, N_FUN, CH), BF16),
            pltpu.VMEM((MAXN, COMP * CH), BF16),
            pltpu.SemaphoreType.DMA((9,)),
            pltpu.SemaphoreType.DMA((27,)),
            pltpu.SemaphoreType.DMA((27,)),
            pltpu.SemaphoreType.DMA((len(PARTS), 27)),
            pltpu.SemaphoreType.DMA((len(PARTS), 27)),
            pltpu.SemaphoreType.DMA((3,)),
            pltpu.SemaphoreType.REGULAR((3,)),
        ],
        compiler_params=pltpu.CompilerParams(collective_id=0, has_side_effects=True),
        name="atoms",
    )(ci, nbr, routes, pos, table, w_in, feats, w_out, w_mix, w_self, w_gate, w_read)


PROBES = 256
SLOTS = 256
BLOCK = 128
UNIT = 16
ROWS_C = 208


def split3(x):
    high = x.astype(BF16)
    x = x - high.astype(F32)
    mid = x.astype(BF16)
    return high, mid, (x - mid.astype(F32)).astype(BF16)


def density_kernel(
    probe_ref, pat_ref, recv_ref, upd_hbm, out_ref, atoms_hbm, rt_ref, px_ref, ct_ref, w_ref,
    upd_ref, sem,
):
    take = pltpu.make_async_copy(upd_hbm, upd_ref, sem.at[0])
    give = pltpu.make_async_copy(upd_ref, atoms_hbm, sem.at[1])
    take.start()
    keep = iota((8, 64), 1) % 8 == iota((8, 64), 0)
    rows = []
    for c in range(3):
        for q in range(4):
            rows.append(
                jnp.where(keep, probe_ref[c : c + 1, q * 64 : (q + 1) * 64], 0.0)
            )
    rows = jnp.concatenate(rows, axis=0)
    widen = jnp.where(iota((64, CH), 0) // 8 == iota((64, CH), 1) // UNIT, 1.0, 0.0).astype(BF16)
    high, mid, low = split3(rows)
    px_ref[...] = (dot(low, widen) + dot(mid, widen)) + dot(high, widen)
    spread = jnp.where(
        iota((SLOTS // 2, SLOTS), 0) == iota((SLOTS // 2, SLOTS), 1) // 2, 1.0, 0.0
    ).astype(BF16)
    wanted = dot(pat_ref[...].astype(F32).astype(BF16), spread)
    before = jnp.where(
        iota((SLOTS, SLOTS), 0) < iota((SLOTS, SLOTS), 1), 1.0, 0.0
    ).astype(BF16)
    for h in range(2):
        rt_ref[h * CH : (h + 1) * CH, :] = (
            recv_ref[h * SLOTS : (h + 1) * SLOTS, :].astype(F32).T.astype(BF16)
        )
    active = wanted * rt_ref[192:208, :].astype(F32)[11:12, :]
    rank = dot(active.astype(BF16), before)
    w_ref[...] = jnp.where(active > 0.5, rank, -1.0)
    most = jnp.max(jnp.sum(active, axis=1, keepdims=True)).astype(jnp.int32)
    place = (iota((BLOCK, SLOTS), 0) % UNIT).astype(F32)

    def fetch(u, buf):
        at = place + (u * UNIT).astype(F32)
        pick = jnp.concatenate(
            [jnp.where(at == w_ref[k : k + 1, :], 1.0, 0.0) for k in range(2)], axis=0
        ).astype(BF16)
        ct_ref[buf] = dot(rt_ref[0:ROWS_C, :], pick, NT)

    def add_unit(buf, totals):
        out = []
        for k in range(2):
            lanes = slice(k * BLOCK, (k + 1) * BLOCK)

            def row(j):
                return ct_ref[buf, j : j + 1, lanes]

            rel = [
                px_ref[c * 32 + k * 16 : c * 32 + (k + 1) * 16, :] - row(200 + c)
                for c in range(3)
            ]
            d, ux, uy, uz = geometry(*rel)
            total = [None] * N_FUN
            for m, val in enumerate(harmonics(ux, uy, uz)):
                for b in range(N_FUN):
                    term = row(m * N_FUN + b)
                    total[b] = term if m == 0 else total[b] + val * term
            add = totals[k]
            for b, phi in enumerate(radial_funs(d)):
                add = add + phi * total[b]
            out.append(add)
        return tuple(out)

    fetch(jnp.int32(0), 0)

    def two_units(i, totals):
        fetch(2 * i + 1, 1)
        totals = add_unit(0, totals)
        fetch(2 * i + 2, 0)
        return add_unit(1, totals)

    zero = jnp.zeros((16, BLOCK), F32)
    totals = two_units(jnp.int32(0), (zero, zero))
    take.wait()
    give.start()
    totals = lax.fori_loop(1, (most + 2 * UNIT - 1) // (2 * UNIT), two_units, totals)
    narrow = jnp.where(iota((CH, 64), 0) // UNIT == iota((CH, 64), 1) // 8, 1.0, 0.0).astype(BF16)
    high, mid, low = split3(jnp.concatenate(totals, axis=0))
    sums = (dot(low, narrow) + dot(mid, narrow)) + dot(high, narrow)
    for q in range(4):
        part = jnp.where(keep, sums[q * 8 : (q + 1) * 8], 0.0)
        out_ref[q // 2 : q // 2 + 1, (q % 2) * 64 : (q % 2 + 1) * 64] = jnp.sum(
            part, axis=0, keepdims=True
        ) * (1.0 / math.sqrt(SLOTS))
    give.wait()


def density_call(probes, pattern, recv, upd):
    vm = pl.BlockSpec(memory_space=pltpu.VMEM)
    hbm = pl.BlockSpec(memory_space=pl.ANY)
    return pl.pallas_call(
        density_kernel,
        out_shape=(
            jax.ShapeDtypeStruct((2, CH), F32),
            jax.ShapeDtypeStruct((COMP, ATOMS, CH), BF16),
        ),
        in_specs=[vm] * 3 + [hbm],
        out_specs=(vm, hbm),
        scratch_shapes=[
            pltpu.VMEM((2 * CH, SLOTS), BF16),
            pltpu.VMEM((96, CH), F32),
            pltpu.VMEM((2, ROWS_C, 2 * BLOCK), F32),
            pltpu.VMEM((2, SLOTS), F32),
            pltpu.VMEM((COMP, ATOMS, CH), BF16),
            pltpu.SemaphoreType.DMA((2,)),
        ],
        name="density",
    )(probes, pattern, recv, upd)


def per_device(
    features, positions, probe_positions, neighbours, routes, pattern, charge_index, charge_table,
    w_radial_in, w_radial_out, w_mix, w_self, w_gate, w_read,
):
    feats = jnp.transpose(features, (1, 0, 2)).reshape(COMP, 32, 4, CH)
    upd, recv = atom_call(
        charge_index, neighbours.T, routes.T, positions, charge_table, w_radial_in, feats,
        w_radial_out, w_mix, w_self, w_gate, jnp.transpose(w_read, (1, 0, 2)),
    )
    density, atoms = density_call(probe_positions, pattern, recv.reshape(512, CH), upd)
    return jnp.transpose(atoms, (1, 0, 2)), density.reshape(PROBES)


def solution(mesh):
    split = ("gx", "gy", "gz")
    rows = P(split, None)
    in_specs = (
        (P(split, None, None), P(None, split), P(None, split), rows, rows, rows) + (P(),) * 8
    )
    out_specs = (P(split, None, None), P(split))
    return jax.shard_map(
        per_device, mesh=mesh, in_specs=in_specs, out_specs=out_specs, check_vma=False
    )
```

```python
import functools, math
import jax
import jax.numpy as jnp
from jax import lax
from jax.experimental import pallas as pl
from jax.experimental.pallas import tpu as pltpu
from jax.sharding import PartitionSpec as P

F32 = jnp.float32
BF16 = jnp.bfloat16
CUTOFF = 8.0
WIDTH_R = 0.75
REACH = 6.0
FLOOR = 0.25
N_FUN = 8
DEG = 5
COMP = 25
CH = 128
ATOMS = 128
FAN = 20
GROUP = 8
N_GROUP = 16
EDGE = GROUP * FAN
CHUNK = 4
WIDE = 8
MAXN = 256


def degree_of(component):
    return int(math.isqrt(component))


def harmonics(x, y, z):
    xx, yy, zz = x * x, y * y, z * z
    c = math.sqrt
    return [
        jnp.ones_like(x),
        c(3.0) * y,
        c(3.0) * z,
        c(3.0) * x,
        c(15.0) * x * y,
        c(15.0) * y * z,
        0.5 * c(5.0) * (3.0 * zz - 1.0),
        c(15.0) * x * z,
        0.5 * c(15.0) * (xx - yy),
        c(35.0 / 8.0) * y * (3.0 * xx - yy),
        c(105.0) * x * y * z,
        c(21.0 / 8.0) * y * (5.0 * zz - 1.0),
        0.5 * c(7.0) * z * (5.0 * zz - 3.0),
        c(21.0 / 8.0) * x * (5.0 * zz - 1.0),
        0.5 * c(105.0) * z * (xx - yy),
        c(35.0 / 8.0) * x * (xx - 3.0 * yy),
        1.5 * c(35.0) * x * y * (xx - yy),
        1.5 * c(17.5) * y * z * (3.0 * xx - yy),
        1.5 * c(5.0) * x * y * (7.0 * zz - 1.0),
        1.5 * c(2.5) * y * z * (7.0 * zz - 3.0),
        0.375 * (35.0 * zz * zz - 30.0 * zz + 3.0),
        1.5 * c(2.5) * x * z * (7.0 * zz - 3.0),
        0.75 * c(5.0) * (xx - yy) * (7.0 * zz - 1.0),
        1.5 * c(17.5) * x * z * (xx - 3.0 * yy),
        0.375 * c(35.0) * (xx * xx - 6.0 * xx * yy + yy * yy),
    ]


def radial_funs(d):
    q = d * (1.0 / CUTOFF)
    env = 1.0 - q * q
    env = env * env
    out = []
    for b in range(N_FUN):
        v = (d - b * (REACH / (N_FUN - 1))) * (1.0 / WIDTH_R)
        out.append(jnp.exp(-(v * v)) * env)
    return out


def geometry(dx, dy, dz):
    d = jnp.sqrt(dx * dx + dy * dy + dz * dz)
    inv = 1.0 / jnp.maximum(d, FLOOR)
    return d, dx * inv, dy * inv, dz * inv


def iota(shape, dim):
    return lax.broadcasted_iota(jnp.int32, shape, dim)


def dot(a, b, dims=None):
    if dims is None:
        dims = (((1,), (0,)), ((), ()))
    return lax.dot_general(a, b, dims, preferred_element_type=F32)


NT = (((1,), (1,)), ((), ()))
TN = (((0,), (0,)), ((), ()))


MESH = pl.DeviceIdType.MESH
ROW_OF = (0, 16, 48, 96, 160)
ROWS = 240


def atom_kernel(
    ci_ref, nbr_ref, routes_ref, pos_ref, table_ref, w_in_ref, feats_hbm, w_out_hbm, w_mix_hbm,
    w_self_hbm, w_gate_hbm, w_read_hbm, upd_hbm, recv_ref,
    f_ref, e_ref, oh_ref, xyz_ref, ys_ref, bas_ref, y_ref, r_ref, s_ref, agg_ref, cross_ref,
    upd_ref, send_ref, put_ref, extra_ref, w_out_ref, w_mix_ref, w_self_ref, w_gate_ref, w_read_ref, spread_ref,
    load_sem, pos_send, pos_recv, halo_send, halo_recv, tile_sem, plane_sem,
):
    gx, gy, gz = lax.axis_index("gx"), lax.axis_index("gy"), lax.axis_index("gz")
    nx, ny, nz = lax.axis_size("gx"), lax.axis_size("gy"), lax.axis_size("gz")

    def place(a, b, c):
        return (
            lax.rem(gx + a + nx, nx), lax.rem(gy + b + ny, ny), lax.rem(gz + c + nz, nz)
        )

    peers = [place(1 - n // 9, 1 - n // 3 % 3, 1 - n % 3) for n in range(27)]
    others = [n for n in range(27) if n != 13]
    around = [(b, c) for b in (-1, 0, 1) for c in (-1, 0, 1) if (b, c) != (0, 0)]

    def plane_signal(step):
        for b, c in around:
            pl.semaphore_signal(
                plane_sem.at[step],
                inc=1,
                device_id=place(0, b << step, c << step),
                device_id_type=MESH,
            )

    first = pltpu.make_async_copy(
        feats_hbm.at[:, 0:1], f_ref.at[0:COMP, 0:1], load_sem.at[0]
    )
    first.start()
    barrier = pltpu.get_barrier_semaphore()
    for n in others:
        pl.semaphore_signal(barrier, inc=1, device_id=peers[n], device_id_type=MESH)
    rest = pltpu.make_async_copy(
        feats_hbm.at[:, 1:32], f_ref.at[0:COMP, 1:32], load_sem.at[1]
    )
    loads = [
        pltpu.make_async_copy(src, dst, load_sem.at[2 + i])
        for i, (src, dst) in enumerate(
            (
                (w_out_hbm, w_out_ref),
                (w_mix_hbm, w_mix_ref),
                (w_self_hbm, w_self_ref),
                (w_gate_hbm, w_gate_ref),
                (w_read_hbm, w_read_ref),
            )
        )
    ]
    rest.start()
    for load in loads:
        load.start()
    pos = pos_ref[...].astype(F32)
    pos8 = jnp.concatenate(
        [pos, jnp.ones((1, ATOMS), F32), jnp.zeros((4, ATOMS), F32)], axis=0
    )
    eye = jnp.where(iota((8, CH), 1) == iota((8, CH), 0), 1.0, 0.0).astype(BF16)
    f_ref[COMP, 0] = dot(pos8.astype(BF16), eye, TN)[0:4].astype(BF16)
    f_ref[:, 59:64] = jnp.zeros((COMP + 1, 5, 4, CH), BF16)
    first.wait()
    pl.semaphore_wait(barrier, 26)
    sent, halo = [], []
    for n in others:
        copy = pltpu.make_async_remote_copy(
            src_ref=f_ref.at[COMP, 0],
            dst_ref=f_ref.at[COMP, 32 + n],
            send_sem=pos_send.at[n],
            recv_sem=pos_recv.at[n],
            device_id=peers[n],
            device_id_type=MESH,
        )
        copy.start()
        sent.append(copy)
    for n in others:
        copy = pltpu.make_async_remote_copy(
            src_ref=f_ref.at[0:COMP, 0],
            dst_ref=f_ref.at[0:COMP, 32 + n],
            send_sem=halo_send.at[n],
            recv_sem=halo_recv.at[n],
            device_id=peers[n],
            device_id_type=MESH,
        )
        copy.start()
        halo.append(copy)
    mine = pltpu.make_async_copy(f_ref.at[:, 0], f_ref.at[:, 45], load_sem.at[7])
    mine.start()
    plane_signal(0)
    nbr = jnp.concatenate(
        [nbr_ref[...].astype(F32), jnp.zeros((4, ATOMS), F32)], axis=0
    ).T
    col = iota((ATOMS, MAXN), 1).astype(F32)
    for k in range(0, FAN, 2):
        halves = []
        for kk in (k, k + 1):
            hot = jnp.where(nbr[:, kk : kk + 1] == col, 1.0, 0.0)
            halves.append(hot.reshape(N_GROUP, GROUP, MAXN))
        oh_ref[:, k * GROUP : (k + 2) * GROUP, :] = jnp.concatenate(halves, axis=1).astype(BF16)
    lvl = iota((8, CH), 0)
    shift = jnp.sum(
        jnp.where(lvl == ci_ref[0], table_ref[...].astype(F32), 0.0), axis=0, keepdims=True
    )
    flat = f_ref.reshape(COMP + 1, MAXN, CH)
    mine.wait()
    for load in loads:
        load.wait()
    spread_ref[...] = jnp.zeros((MAXN, COMP * CH), BF16)
    none8 = jnp.zeros((N_FUN, CH), F32)
    for m in range(COMP):
        one = w_read_ref[degree_of(m)].astype(F32)
        two = [one, none8] if m % 2 == 0 else [none8, one]
        start = (m - m % 2) * N_FUN
        spread_ref[start : start + 16, m * CH : (m + 1) * CH] = jnp.concatenate(
            two, axis=0
        ).astype(BF16)
    r_row = jnp.broadcast_to(routes_ref[...].astype(F32), (ATOMS, ATOMS))
    r_col = r_row.T
    before = iota((ATOMS, ATOMS), 0) < iota((ATOMS, ATOMS), 1)
    rank = jnp.sum(
        jnp.where(before, jnp.where(r_col == r_row, 1.0, 0.0), 0.0), axis=0, keepdims=True
    )
    target = (r_row[0:1, :] * 2.0 + rank).astype(jnp.int32)
    put_ref[...] = jnp.where(iota((MAXN, ATOMS), 0) == target, 1.0, 0.0).astype(BF16)
    put = jnp.where(iota((8, CH), 1) == iota((8, CH), 0) + 72, 1.0, 0.0).astype(BF16)
    extra_ref[...] = dot(pos8.astype(BF16), put, TN)
    for copy in sent:
        copy.wait()
    gpos_t = flat[COMP, ATOMS:MAXN].astype(F32).T
    pt = jnp.concatenate([pos8, gpos_t[0:8]], axis=1).astype(BF16)
    own_group = iota((N_GROUP, ATOMS), 1) // GROUP == iota((N_GROUP, ATOMS), 0)
    tile_sel = jnp.where(
        iota((ATOMS, EDGE), 0) % GROUP == iota((ATOMS, EDGE), 1) % GROUP, 1.0, 0.0
    ).astype(BF16)
    for g in range(N_GROUP):
        got = dot(pt, oh_ref[g], NT)
        for c in range(3):
            xyz_ref[c, g : g + 1, :] = got[c : c + 1, :]
    rel = []
    for c in range(3):
        mine_c = jnp.where(own_group, pos[c : c + 1, :], 0.0).astype(BF16)
        rel.append(xyz_ref[c] - dot(mine_c, tile_sel))
    d, ux, uy, uz = geometry(*rel)
    for m, val in enumerate(harmonics(ux, uy, uz)):
        ys_ref[:, m, :] = val
    for b, val in enumerate(radial_funs(d)):
        bas_ref[:, b, :] = val
    mask8 = jnp.where(iota((GROUP, EDGE), 1) % GROUP == iota((GROUP, EDGE), 0), 1.0, 0.0)
    w_in = w_in_ref[...]
    scale = 1.0 / math.sqrt(FAN)
    pl.semaphore_wait(plane_sem.at[0], 8)
    plane_signal(1)

    def radial_chunk(ch, carry):
        base = ch * CHUNK
        for q in range(CHUNK):
            h = dot(bas_ref[base + q].astype(BF16), w_in, TN)
            h = (h * jax.nn.sigmoid(h)).astype(BF16)
            r_ref[base + q] = dot(h, w_out_ref[...]) * scale
            y = ys_ref[base + q]
            for l in range(DEG):
                lo = l * l
                rows = [y[m : m + 1, :] * mask8 for m in range(lo, lo + 2 * l + 1)]
                rows.append(jnp.zeros((GROUP, EDGE), F32))
                y_ref[base + q, ROW_OF[l] : ROW_OF[l] + (2 * l + 2) * GROUP] = jnp.concatenate(
                    rows, axis=0
                ).astype(BF16)
        return carry

    lax.fori_loop(0, N_GROUP // CHUNK, radial_chunk, 0)
    rest.wait()
    for copy in halo:
        copy.wait()
    pl.semaphore_wait(plane_sem.at[1], 8)
    plane_signal(2)
    e_ref[...] = (flat[0].astype(F32) + shift).astype(BF16)

    def comp(m):
        return e_ref[...] if m == 0 else flat[m]

    def cross_unit(base, q, l):
        rad = r_ref[base + q, :, (DEG + l) * CH : (DEG + l + 1) * CH]
        part = (rad * s_ref[q]).astype(BF16)
        lhs = y_ref[base + q, ROW_OF[l] : ROW_OF[l] + (2 * l + 2) * GROUP]
        got = dot(lhs, part)
        for j in range(2 * l + 1):
            m = l * l + j
            cross_ref[base + q, :, m * CH : (m + 1) * CH] = got[j * GROUP : (j + 1) * GROUP, :]

    units = [(q, l) for l in range(DEG) for q in range(WIDE)]

    def one_chunk(ch, carry):
        base = ch * WIDE
        hot = oh_ref[pl.ds(base, WIDE)].reshape(WIDE * EDGE, MAXN)
        todo = list(units)
        for m in range(0, COMP, 2):
            comps = [m] + ([m + 1] if m + 1 < COMP else [])
            got = dot(hot, jnp.concatenate([comp(mm) for mm in comps], axis=1))
            if m == 0:
                s_ref[...] = got[:, 0:CH].reshape(WIDE, EDGE, CH)
            else:
                for q, l in todo[:4]:
                    cross_unit(base, q, l)
                todo = todo[4:]
            for j, mm in enumerate(comps):
                l = degree_of(mm)
                part = got[:, j * CH : (j + 1) * CH].reshape(WIDE, FAN, GROUP, CH)
                rad = r_ref[pl.ds(base, WIDE), :, l * CH : (l + 1) * CH].reshape(
                    WIDE, FAN, GROUP, CH
                )
                agg_ref[pl.ds(base, WIDE), :, mm * CH : (mm + 1) * CH] = jnp.sum(
                    part * rad, axis=1
                )
        return carry

    lax.fori_loop(0, N_GROUP // WIDE, one_chunk, 0)

    def agg_of(m):
        lanes = slice(m * CH, (m + 1) * CH)
        both = agg_ref[:, :, lanes] + cross_ref[:, :, lanes]
        return both.reshape(ATOMS, CH).astype(BF16)

    gates = jax.nn.sigmoid(dot(agg_of(0), w_gate_ref[...]))
    for l in range(DEG):
        w_cat = jnp.concatenate([w_mix_ref[l], w_self_ref[l]], axis=0)
        for m in range(l * l, (l + 1) * (l + 1)):
            emb = comp(m)[0:ATOMS]
            mixed = dot(jnp.concatenate([agg_of(m), emb], axis=1), w_cat)
            if l == 0:
                add = mixed * jax.nn.sigmoid(mixed)
            else:
                add = mixed * gates[:, (l - 1) * CH : l * CH]
            upd_ref[m] = (emb.astype(F32) + add).astype(BF16)
    store = pltpu.make_async_copy(upd_ref, upd_hbm, load_sem.at[8])
    store.start()
    coef = dot(
        jnp.concatenate([upd_ref[m] for m in range(COMP)], axis=1), spread_ref[...], NT
    )
    coefs = [coef[:, 0:CH], coef[:, CH:] + extra_ref[...]]
    flat_send = send_ref.reshape(2, 2 * 128, CH)
    for h in range(2):
        flat_send[h] = dot(put_ref[...], coefs[h].astype(BF16)).astype(BF16)
    pl.semaphore_wait(plane_sem.at[2], 8)
    count = ny * nz
    me = gy * nz + gz

    def post(j, carry):
        t = lax.rem(me + j, count)
        pltpu.make_async_remote_copy(
            src_ref=send_ref.at[:, t],
            dst_ref=recv_ref.at[:, me],
            send_sem=tile_sem.at[0],
            recv_sem=tile_sem.at[1],
            device_id=(gx, t // nz, lax.rem(t, nz)),
            device_id_type=MESH,
        ).start()
        return carry

    lax.fori_loop(1, count, post, 0)
    own = pltpu.make_async_copy(send_ref.at[:, me], recv_ref.at[:, me], tile_sem.at[2])
    own.start()
    own.wait()
    store.wait()
    part = pl.ds(0, count - 1)
    pltpu.make_async_copy(send_ref.at[:, part], recv_ref.at[:, part], tile_sem.at[0]).wait()
    pltpu.make_async_copy(send_ref.at[:, part], recv_ref.at[:, part], tile_sem.at[1]).wait()


def atom_call(ci, nbr, routes, pos, table, w_in, feats, w_out, w_mix, w_self, w_gate, w_read):
    vm = pl.BlockSpec(memory_space=pltpu.VMEM)
    hbm = pl.BlockSpec(memory_space=pl.ANY)
    return pl.pallas_call(
        atom_kernel,
        out_shape=(
            jax.ShapeDtypeStruct((COMP, ATOMS, CH), BF16),
            jax.ShapeDtypeStruct((2, 128, 2, CH), BF16),
        ),
        in_specs=[pl.BlockSpec(memory_space=pltpu.SMEM)] + [vm] * 5 + [hbm] * 6,
        out_specs=(hbm, hbm),
        scratch_shapes=[
            pltpu.VMEM((COMP + 1, 64, 4, CH), BF16),
            pltpu.VMEM((MAXN, CH), BF16),
            pltpu.VMEM((N_GROUP, EDGE, MAXN), BF16),
            pltpu.VMEM((3, N_GROUP, EDGE), F32),
            pltpu.VMEM((N_GROUP, COMP, EDGE), F32),
            pltpu.VMEM((N_GROUP, N_FUN, EDGE), F32),
            pltpu.VMEM((N_GROUP, ROWS, EDGE), BF16),
            pltpu.VMEM((N_GROUP, EDGE, 2 * DEG * CH), F32),
            pltpu.VMEM((WIDE, EDGE, CH), F32),
            pltpu.VMEM((N_GROUP, GROUP, COMP * CH), F32),
            pltpu.VMEM((N_GROUP, GROUP, COMP * CH), F32),
            pltpu.VMEM((COMP, ATOMS, CH), BF16),
            pltpu.VMEM((2, 128, 2, CH), BF16),
            pltpu.VMEM((MAXN, ATOMS), BF16),
            pltpu.VMEM((ATOMS, CH), F32),
            pltpu.VMEM((64, 2 * DEG * CH), BF16),
            pltpu.VMEM((DEG, CH, CH), BF16),
            pltpu.VMEM((DEG, CH, CH), BF16),
            pltpu.VMEM((CH, (DEG - 1) * CH), BF16),
            pltpu.VMEM((DEG, N_FUN, CH), BF16),
            pltpu.VMEM((MAXN, COMP * CH), BF16),
            pltpu.SemaphoreType.DMA((9,)),
            pltpu.SemaphoreType.DMA((27,)),
            pltpu.SemaphoreType.DMA((27,)),
            pltpu.SemaphoreType.DMA((27,)),
            pltpu.SemaphoreType.DMA((27,)),
            pltpu.SemaphoreType.DMA((3,)),
            pltpu.SemaphoreType.REGULAR((3,)),
        ],
        compiler_params=pltpu.CompilerParams(collective_id=0, has_side_effects=True),
        name="atoms",
    )(ci, nbr, routes, pos, table, w_in, feats, w_out, w_mix, w_self, w_gate, w_read)


PROBES = 256
SLOTS = 256
BLOCK = 128
UNIT = 16
ROWS_C = 208


def split3(x):
    high = x.astype(BF16)
    x = x - high.astype(F32)
    mid = x.astype(BF16)
    return high, mid, (x - mid.astype(F32)).astype(BF16)


def density_kernel(
    probe_ref, pat_ref, recv_ref, upd_hbm, out_ref, atoms_hbm, rt_ref, px_ref, ct_ref, w_ref,
    upd_ref, sem,
):
    take = pltpu.make_async_copy(upd_hbm, upd_ref, sem.at[0])
    give = pltpu.make_async_copy(upd_ref, atoms_hbm, sem.at[1])
    take.start()
    keep = iota((8, 64), 1) % 8 == iota((8, 64), 0)
    rows = []
    for c in range(3):
        for q in range(4):
            rows.append(
                jnp.where(keep, probe_ref[c : c + 1, q * 64 : (q + 1) * 64], 0.0)
            )
    rows = jnp.concatenate(rows, axis=0)
    widen = jnp.where(iota((64, CH), 0) // 8 == iota((64, CH), 1) // UNIT, 1.0, 0.0).astype(BF16)
    high, mid, low = split3(rows)
    px_ref[...] = (dot(low, widen) + dot(mid, widen)) + dot(high, widen)
    spread = jnp.where(
        iota((SLOTS // 2, SLOTS), 0) == iota((SLOTS // 2, SLOTS), 1) // 2, 1.0, 0.0
    ).astype(BF16)
    wanted = dot(pat_ref[...].astype(F32).astype(BF16), spread)
    before = jnp.where(
        iota((SLOTS, SLOTS), 0) < iota((SLOTS, SLOTS), 1), 1.0, 0.0
    ).astype(BF16)
    for h in range(2):
        rt_ref[h * CH : (h + 1) * CH, :] = (
            recv_ref[h * SLOTS : (h + 1) * SLOTS, :].astype(F32).T.astype(BF16)
        )
    active = wanted * rt_ref[192:208, :].astype(F32)[11:12, :]
    rank = dot(active.astype(BF16), before)
    w_ref[...] = jnp.where(active > 0.5, rank, -1.0)
    most = jnp.max(jnp.sum(active, axis=1, keepdims=True)).astype(jnp.int32)
    place = (iota((BLOCK, SLOTS), 0) % UNIT).astype(F32)

    def fetch(u, buf):
        at = place + (u * UNIT).astype(F32)
        pick = jnp.concatenate(
            [jnp.where(at == w_ref[k : k + 1, :], 1.0, 0.0) for k in range(2)], axis=0
        ).astype(BF16)
        ct_ref[buf] = dot(rt_ref[0:ROWS_C, :], pick, NT)

    def add_unit(buf, totals):
        out = []
        for k in range(2):
            lanes = slice(k * BLOCK, (k + 1) * BLOCK)

            def row(j):
                return ct_ref[buf, j : j + 1, lanes]

            rel = [
                px_ref[c * 32 + k * 16 : c * 32 + (k + 1) * 16, :] - row(200 + c)
                for c in range(3)
            ]
            d, ux, uy, uz = geometry(*rel)
            total = [None] * N_FUN
            for m, val in enumerate(harmonics(ux, uy, uz)):
                for b in range(N_FUN):
                    term = row(m * N_FUN + b)
                    total[b] = term if m == 0 else total[b] + val * term
            add = totals[k]
            for b, phi in enumerate(radial_funs(d)):
                add = add + phi * total[b]
            out.append(add)
        return tuple(out)

    fetch(jnp.int32(0), 0)

    def two_units(i, totals):
        fetch(2 * i + 1, 1)
        totals = add_unit(0, totals)
        fetch(2 * i + 2, 0)
        return add_unit(1, totals)

    zero = jnp.zeros((16, BLOCK), F32)
    totals = two_units(jnp.int32(0), (zero, zero))
    take.wait()
    give.start()
    totals = lax.fori_loop(1, (most + 2 * UNIT - 1) // (2 * UNIT), two_units, totals)
    narrow = jnp.where(iota((CH, 64), 0) // UNIT == iota((CH, 64), 1) // 8, 1.0, 0.0).astype(BF16)
    high, mid, low = split3(jnp.concatenate(totals, axis=0))
    sums = (dot(low, narrow) + dot(mid, narrow)) + dot(high, narrow)
    for q in range(4):
        part = jnp.where(keep, sums[q * 8 : (q + 1) * 8], 0.0)
        out_ref[q // 2 : q // 2 + 1, (q % 2) * 64 : (q % 2 + 1) * 64] = jnp.sum(
            part, axis=0, keepdims=True
        ) * (1.0 / math.sqrt(SLOTS))
    give.wait()


def density_call(probes, pattern, recv, upd):
    vm = pl.BlockSpec(memory_space=pltpu.VMEM)
    hbm = pl.BlockSpec(memory_space=pl.ANY)
    return pl.pallas_call(
        density_kernel,
        out_shape=(
            jax.ShapeDtypeStruct((2, CH), F32),
            jax.ShapeDtypeStruct((COMP, ATOMS, CH), BF16),
        ),
        in_specs=[vm] * 3 + [hbm],
        out_specs=(vm, hbm),
        scratch_shapes=[
            pltpu.VMEM((2 * CH, SLOTS), BF16),
            pltpu.VMEM((96, CH), F32),
            pltpu.VMEM((2, ROWS_C, 2 * BLOCK), F32),
            pltpu.VMEM((2, SLOTS), F32),
            pltpu.VMEM((COMP, ATOMS, CH), BF16),
            pltpu.SemaphoreType.DMA((2,)),
        ],
        name="density",
    )(probes, pattern, recv, upd)


def per_device(
    features, positions, probe_positions, neighbours, routes, pattern, charge_index, charge_table,
    w_radial_in, w_radial_out, w_mix, w_self, w_gate, w_read,
):
    feats = jnp.transpose(features, (1, 0, 2)).reshape(COMP, 32, 4, CH)
    upd, recv = atom_call(
        charge_index, neighbours.T, routes.T, positions, charge_table, w_radial_in, feats,
        w_radial_out, w_mix, w_self, w_gate, jnp.transpose(w_read, (1, 0, 2)),
    )
    density, atoms = density_call(probe_positions, pattern, recv.reshape(512, CH), upd)
    return jnp.transpose(atoms, (1, 0, 2)), density.reshape(PROBES)


def solution(mesh):
    split = ("gx", "gy", "gz")
    rows = P(split, None)
    in_specs = (
        (P(split, None, None), P(None, split), P(None, split), rows, rows, rows) + (P(),) * 8
    )
    out_specs = (P(split, None, None), P(split))
    return jax.shard_map(
        per_device, mesh=mesh, in_specs=in_specs, out_specs=out_specs, check_vma=False
    )
```

```python
import functools, math
import jax
import jax.numpy as jnp
from jax import lax
from jax.experimental import pallas as pl
from jax.experimental.pallas import tpu as pltpu
from jax.sharding import PartitionSpec as P

F32 = jnp.float32
BF16 = jnp.bfloat16
CUTOFF = 8.0
WIDTH_R = 0.75
REACH = 6.0
FLOOR = 0.25
N_FUN = 8
DEG = 5
COMP = 25
CH = 128
ATOMS = 128
FAN = 20
GROUP = 8
N_GROUP = 16
EDGE = GROUP * FAN
CHUNK = 4
WIDE = 8
MAXN = 256


def degree_of(component):
    return int(math.isqrt(component))


def harmonics(x, y, z):
    xx, yy, zz = x * x, y * y, z * z
    c = math.sqrt
    return [
        jnp.ones_like(x),
        c(3.0) * y,
        c(3.0) * z,
        c(3.0) * x,
        c(15.0) * x * y,
        c(15.0) * y * z,
        0.5 * c(5.0) * (3.0 * zz - 1.0),
        c(15.0) * x * z,
        0.5 * c(15.0) * (xx - yy),
        c(35.0 / 8.0) * y * (3.0 * xx - yy),
        c(105.0) * x * y * z,
        c(21.0 / 8.0) * y * (5.0 * zz - 1.0),
        0.5 * c(7.0) * z * (5.0 * zz - 3.0),
        c(21.0 / 8.0) * x * (5.0 * zz - 1.0),
        0.5 * c(105.0) * z * (xx - yy),
        c(35.0 / 8.0) * x * (xx - 3.0 * yy),
        1.5 * c(35.0) * x * y * (xx - yy),
        1.5 * c(17.5) * y * z * (3.0 * xx - yy),
        1.5 * c(5.0) * x * y * (7.0 * zz - 1.0),
        1.5 * c(2.5) * y * z * (7.0 * zz - 3.0),
        0.375 * (35.0 * zz * zz - 30.0 * zz + 3.0),
        1.5 * c(2.5) * x * z * (7.0 * zz - 3.0),
        0.75 * c(5.0) * (xx - yy) * (7.0 * zz - 1.0),
        1.5 * c(17.5) * x * z * (xx - 3.0 * yy),
        0.375 * c(35.0) * (xx * xx - 6.0 * xx * yy + yy * yy),
    ]


def radial_funs(d):
    q = d * (1.0 / CUTOFF)
    env = 1.0 - q * q
    env = env * env
    out = []
    for b in range(N_FUN):
        v = (d - b * (REACH / (N_FUN - 1))) * (1.0 / WIDTH_R)
        out.append(jnp.exp(-(v * v)) * env)
    return out


def geometry(dx, dy, dz):
    d = jnp.sqrt(dx * dx + dy * dy + dz * dz)
    inv = 1.0 / jnp.maximum(d, FLOOR)
    return d, dx * inv, dy * inv, dz * inv


def iota(shape, dim):
    return lax.broadcasted_iota(jnp.int32, shape, dim)


def dot(a, b, dims=None):
    if dims is None:
        dims = (((1,), (0,)), ((), ()))
    return lax.dot_general(a, b, dims, preferred_element_type=F32)


NT = (((1,), (1,)), ((), ()))
TN = (((0,), (0,)), ((), ()))


MESH = pl.DeviceIdType.MESH
ROW_OF = (0, 16, 48, 96, 160)
ROWS = 240


def atom_kernel(
    ci_ref, nbr_hbm, routes_hbm, pos_hbm, table_hbm, w_in_hbm, feats_hbm, w_out_hbm, w_mix_hbm,
    w_self_hbm, w_gate_hbm, w_read_hbm, upd_hbm, recv_ref,
    nbr_ref, routes_ref, pos_ref, table_ref, w_in_ref,
    f_ref, e_ref, oh_ref, xyz_ref, ys_ref, bas_ref, y_ref, r_ref, s_ref, agg_ref, cross_ref,
    upd_ref, send_ref, put_ref, extra_ref, w_out_ref, w_mix_ref, w_self_ref, w_gate_ref, w_read_ref, spread_ref,
    small_sem, load_sem, pos_send, pos_recv, halo_send, halo_recv, tile_sem, plane_sem,
):
    gx, gy, gz = lax.axis_index("gx"), lax.axis_index("gy"), lax.axis_index("gz")
    nx, ny, nz = lax.axis_size("gx"), lax.axis_size("gy"), lax.axis_size("gz")

    def place(a, b, c):
        return (
            lax.rem(gx + a + nx, nx), lax.rem(gy + b + ny, ny), lax.rem(gz + c + nz, nz)
        )

    peers = [place(1 - n // 9, 1 - n // 3 % 3, 1 - n % 3) for n in range(27)]
    others = [n for n in range(27) if n != 13]
    around = [(b, c) for b in (-1, 0, 1) for c in (-1, 0, 1) if (b, c) != (0, 0)]

    def plane_signal(step):
        for b, c in around:
            pl.semaphore_signal(
                plane_sem.at[step],
                inc=1,
                device_id=place(0, b << step, c << step),
                device_id_type=MESH,
            )

    small = [
        pltpu.make_async_copy(src, dst, small_sem.at[i])
        for i, (src, dst) in enumerate(
            (
                (pos_hbm, pos_ref),
                (nbr_hbm, nbr_ref),
                (table_hbm, table_ref),
                (routes_hbm, routes_ref),
                (w_in_hbm, w_in_ref),
            )
        )
    ]
    small[0].start()
    first = pltpu.make_async_copy(
        feats_hbm.at[:, 0:1], f_ref.at[0:COMP, 0:1], load_sem.at[0]
    )
    first.start()
    barrier = pltpu.get_barrier_semaphore()
    for n in others:
        pl.semaphore_signal(barrier, inc=1, device_id=peers[n], device_id_type=MESH)
    rest = pltpu.make_async_copy(
        feats_hbm.at[:, 1:32], f_ref.at[0:COMP, 1:32], load_sem.at[1]
    )
    loads = [
        pltpu.make_async_copy(src, dst, load_sem.at[2 + i])
        for i, (src, dst) in enumerate(
            (
                (w_out_hbm, w_out_ref),
                (w_mix_hbm, w_mix_ref),
                (w_self_hbm, w_self_ref),
                (w_gate_hbm, w_gate_ref),
                (w_read_hbm, w_read_ref),
            )
        )
    ]
    for load in small[1:] + [rest] + loads:
        load.start()
    small[0].wait()
    pos = pos_ref[...].astype(F32)
    pos8 = jnp.concatenate(
        [pos, jnp.ones((1, ATOMS), F32), jnp.zeros((4, ATOMS), F32)], axis=0
    )
    eye = jnp.where(iota((8, CH), 1) == iota((8, CH), 0), 1.0, 0.0).astype(BF16)
    f_ref[COMP, 0] = dot(pos8.astype(BF16), eye, TN)[0:4].astype(BF16)
    f_ref[:, 59:64] = jnp.zeros((COMP + 1, 5, 4, CH), BF16)
    first.wait()
    pl.semaphore_wait(barrier, 26)
    sent, halo = [], []
    for n in others:
        copy = pltpu.make_async_remote_copy(
            src_ref=f_ref.at[COMP, 0],
            dst_ref=f_ref.at[COMP, 32 + n],
            send_sem=pos_send.at[n],
            recv_sem=pos_recv.at[n],
            device_id=peers[n],
            device_id_type=MESH,
        )
        copy.start()
        sent.append(copy)
    for n in others:
        copy = pltpu.make_async_remote_copy(
            src_ref=f_ref.at[0:COMP, 0],
            dst_ref=f_ref.at[0:COMP, 32 + n],
            send_sem=halo_send.at[n],
            recv_sem=halo_recv.at[n],
            device_id=peers[n],
            device_id_type=MESH,
        )
        copy.start()
        halo.append(copy)
    mine = pltpu.make_async_copy(f_ref.at[:, 0], f_ref.at[:, 45], load_sem.at[7])
    mine.start()
    plane_signal(0)
    for load in small[1:]:
        load.wait()
    nbr = jnp.concatenate(
        [nbr_ref[...].astype(F32), jnp.zeros((4, ATOMS), F32)], axis=0
    ).T
    col = iota((ATOMS, MAXN), 1).astype(F32)
    for k in range(0, FAN, 2):
        halves = []
        for kk in (k, k + 1):
            hot = jnp.where(nbr[:, kk : kk + 1] == col, 1.0, 0.0)
            halves.append(hot.reshape(N_GROUP, GROUP, MAXN))
        oh_ref[:, k * GROUP : (k + 2) * GROUP, :] = jnp.concatenate(halves, axis=1).astype(BF16)
    lvl = iota((8, CH), 0)
    shift = jnp.sum(
        jnp.where(lvl == ci_ref[0], table_ref[...].astype(F32), 0.0), axis=0, keepdims=True
    )
    flat = f_ref.reshape(COMP + 1, MAXN, CH)
    mine.wait()
    for load in loads:
        load.wait()
    spread_ref[...] = jnp.zeros((MAXN, COMP * CH), BF16)
    none8 = jnp.zeros((N_FUN, CH), F32)
    for m in range(COMP):
        one = w_read_ref[degree_of(m)].astype(F32)
        two = [one, none8] if m % 2 == 0 else [none8, one]
        start = (m - m % 2) * N_FUN
        spread_ref[start : start + 16, m * CH : (m + 1) * CH] = jnp.concatenate(
            two, axis=0
        ).astype(BF16)
    r_row = jnp.broadcast_to(routes_ref[...].astype(F32), (ATOMS, ATOMS))
    r_col = r_row.T
    before = iota((ATOMS, ATOMS), 0) < iota((ATOMS, ATOMS), 1)
    rank = jnp.sum(
        jnp.where(before, jnp.where(r_col == r_row, 1.0, 0.0), 0.0), axis=0, keepdims=True
    )
    target = (r_row[0:1, :] * 2.0 + rank).astype(jnp.int32)
    put_ref[...] = jnp.where(iota((MAXN, ATOMS), 0) == target, 1.0, 0.0).astype(BF16)
    put = jnp.where(iota((8, CH), 1) == iota((8, CH), 0) + 72, 1.0, 0.0).astype(BF16)
    extra_ref[...] = dot(pos8.astype(BF16), put, TN)
    for copy in sent:
        copy.wait()
    gpos_t = flat[COMP, ATOMS:MAXN].astype(F32).T
    pt = jnp.concatenate([pos8, gpos_t[0:8]], axis=1).astype(BF16)
    own_group = iota((N_GROUP, ATOMS), 1) // GROUP == iota((N_GROUP, ATOMS), 0)
    tile_sel = jnp.where(
        iota((ATOMS, EDGE), 0) % GROUP == iota((ATOMS, EDGE), 1) % GROUP, 1.0, 0.0
    ).astype(BF16)
    for g in range(N_GROUP):
        got = dot(pt, oh_ref[g], NT)
        for c in range(3):
            xyz_ref[c, g : g + 1, :] = got[c : c + 1, :]
    rel = []
    for c in range(3):
        mine_c = jnp.where(own_group, pos[c : c + 1, :], 0.0).astype(BF16)
        rel.append(xyz_ref[c] - dot(mine_c, tile_sel))
    d, ux, uy, uz = geometry(*rel)
    for m, val in enumerate(harmonics(ux, uy, uz)):
        ys_ref[:, m, :] = val
    for b, val in enumerate(radial_funs(d)):
        bas_ref[:, b, :] = val
    mask8 = jnp.where(iota((GROUP, EDGE), 1) % GROUP == iota((GROUP, EDGE), 0), 1.0, 0.0)
    w_in = w_in_ref[...]
    scale = 1.0 / math.sqrt(FAN)
    pl.semaphore_wait(plane_sem.at[0], 8)
    plane_signal(1)

    def radial_chunk(ch, carry):
        base = ch * CHUNK
        for q in range(CHUNK):
            h = dot(bas_ref[base + q].astype(BF16), w_in, TN)
            h = (h * jax.nn.sigmoid(h)).astype(BF16)
            r_ref[base + q] = dot(h, w_out_ref[...]) * scale
            y = ys_ref[base + q]
            for l in range(DEG):
                lo = l * l
                rows = [y[m : m + 1, :] * mask8 for m in range(lo, lo + 2 * l + 1)]
                rows.append(jnp.zeros((GROUP, EDGE), F32))
                y_ref[base + q, ROW_OF[l] : ROW_OF[l] + (2 * l + 2) * GROUP] = jnp.concatenate(
                    rows, axis=0
                ).astype(BF16)
        return carry

    lax.fori_loop(0, N_GROUP // CHUNK, radial_chunk, 0)
    rest.wait()
    for copy in halo:
        copy.wait()
    pl.semaphore_wait(plane_sem.at[1], 8)
    plane_signal(2)
    e_ref[...] = (flat[0].astype(F32) + shift).astype(BF16)

    def comp(m):
        return e_ref[...] if m == 0 else flat[m]

    def cross_unit(base, q, l):
        rad = r_ref[base + q, :, (DEG + l) * CH : (DEG + l + 1) * CH]
        part = (rad * s_ref[q]).astype(BF16)
        lhs = y_ref[base + q, ROW_OF[l] : ROW_OF[l] + (2 * l + 2) * GROUP]
        got = dot(lhs, part)
        for j in range(2 * l + 1):
            m = l * l + j
            cross_ref[base + q, :, m * CH : (m + 1) * CH] = got[j * GROUP : (j + 1) * GROUP, :]

    units = [(q, l) for l in range(DEG) for q in range(WIDE)]

    def one_chunk(ch, carry):
        base = ch * WIDE
        hot = oh_ref[pl.ds(base, WIDE)].reshape(WIDE * EDGE, MAXN)
        todo = list(units)
        for m in range(0, COMP, 2):
            comps = [m] + ([m + 1] if m + 1 < COMP else [])
            got = dot(hot, jnp.concatenate([comp(mm) for mm in comps], axis=1))
            if m == 0:
                s_ref[...] = got[:, 0:CH].reshape(WIDE, EDGE, CH)
            else:
                for q, l in todo[:4]:
                    cross_unit(base, q, l)
                todo = todo[4:]
            for j, mm in enumerate(comps):
                l = degree_of(mm)
                part = got[:, j * CH : (j + 1) * CH].reshape(WIDE, FAN, GROUP, CH)
                rad = r_ref[pl.ds(base, WIDE), :, l * CH : (l + 1) * CH].reshape(
                    WIDE, FAN, GROUP, CH
                )
                agg_ref[pl.ds(base, WIDE), :, mm * CH : (mm + 1) * CH] = jnp.sum(
                    part * rad, axis=1
                )
        return carry

    lax.fori_loop(0, N_GROUP // WIDE, one_chunk, 0)

    def agg_of(m):
        lanes = slice(m * CH, (m + 1) * CH)
        both = agg_ref[:, :, lanes] + cross_ref[:, :, lanes]
        return both.reshape(ATOMS, CH).astype(BF16)

    gates = jax.nn.sigmoid(dot(agg_of(0), w_gate_ref[...]))
    for l in range(DEG):
        w_cat = jnp.concatenate([w_mix_ref[l], w_self_ref[l]], axis=0)
        for m in range(l * l, (l + 1) * (l + 1)):
            emb = comp(m)[0:ATOMS]
            mixed = dot(jnp.concatenate([agg_of(m), emb], axis=1), w_cat)
            if l == 0:
                add = mixed * jax.nn.sigmoid(mixed)
            else:
                add = mixed * gates[:, (l - 1) * CH : l * CH]
            upd_ref[m] = (emb.astype(F32) + add).astype(BF16)
    store = pltpu.make_async_copy(upd_ref, upd_hbm, load_sem.at[8])
    store.start()
    coef = dot(
        jnp.concatenate([upd_ref[m] for m in range(COMP)], axis=1), spread_ref[...], NT
    )
    coefs = [coef[:, 0:CH], coef[:, CH:] + extra_ref[...]]
    flat_send = send_ref.reshape(2, 2 * 128, CH)
    for h in range(2):
        flat_send[h] = dot(put_ref[...], coefs[h].astype(BF16)).astype(BF16)
    pl.semaphore_wait(plane_sem.at[2], 8)
    count = ny * nz
    me = gy * nz + gz

    def post(j, carry):
        t = lax.rem(me + j, count)
        pltpu.make_async_remote_copy(
            src_ref=send_ref.at[:, t],
            dst_ref=recv_ref.at[:, me],
            send_sem=tile_sem.at[0],
            recv_sem=tile_sem.at[1],
            device_id=(gx, t // nz, lax.rem(t, nz)),
            device_id_type=MESH,
        ).start()
        return carry

    lax.fori_loop(1, count, post, 0)
    own = pltpu.make_async_copy(send_ref.at[:, me], recv_ref.at[:, me], tile_sem.at[2])
    own.start()
    own.wait()
    store.wait()
    part = pl.ds(0, count - 1)
    pltpu.make_async_copy(send_ref.at[:, part], recv_ref.at[:, part], tile_sem.at[0]).wait()
    pltpu.make_async_copy(send_ref.at[:, part], recv_ref.at[:, part], tile_sem.at[1]).wait()


def atom_call(ci, nbr, routes, pos, table, w_in, feats, w_out, w_mix, w_self, w_gate, w_read):
    hbm = pl.BlockSpec(memory_space=pl.ANY)
    return pl.pallas_call(
        atom_kernel,
        out_shape=(
            jax.ShapeDtypeStruct((COMP, ATOMS, CH), BF16),
            jax.ShapeDtypeStruct((2, 128, 2, CH), BF16),
        ),
        in_specs=[pl.BlockSpec(memory_space=pltpu.SMEM)] + [hbm] * 11,
        out_specs=(hbm, hbm),
        scratch_shapes=[
            pltpu.VMEM((FAN, ATOMS), jnp.int32),
            pltpu.VMEM((1, ATOMS), jnp.int32),
            pltpu.VMEM((3, ATOMS), BF16),
            pltpu.VMEM((8, CH), BF16),
            pltpu.VMEM((N_FUN, 64), BF16),
            pltpu.VMEM((COMP + 1, 64, 4, CH), BF16),
            pltpu.VMEM((MAXN, CH), BF16),
            pltpu.VMEM((N_GROUP, EDGE, MAXN), BF16),
            pltpu.VMEM((3, N_GROUP, EDGE), F32),
            pltpu.VMEM((N_GROUP, COMP, EDGE), F32),
            pltpu.VMEM((N_GROUP, N_FUN, EDGE), F32),
            pltpu.VMEM((N_GROUP, ROWS, EDGE), BF16),
            pltpu.VMEM((N_GROUP, EDGE, 2 * DEG * CH), F32),
            pltpu.VMEM((WIDE, EDGE, CH), F32),
            pltpu.VMEM((N_GROUP, GROUP, COMP * CH), F32),
            pltpu.VMEM((N_GROUP, GROUP, COMP * CH), F32),
            pltpu.VMEM((COMP, ATOMS, CH), BF16),
            pltpu.VMEM((2, 128, 2, CH), BF16),
            pltpu.VMEM((MAXN, ATOMS), BF16),
            pltpu.VMEM((ATOMS, CH), F32),
            pltpu.VMEM((64, 2 * DEG * CH), BF16),
            pltpu.VMEM((DEG, CH, CH), BF16),
            pltpu.VMEM((DEG, CH, CH), BF16),
            pltpu.VMEM((CH, (DEG - 1) * CH), BF16),
            pltpu.VMEM((DEG, N_FUN, CH), BF16),
            pltpu.VMEM((MAXN, COMP * CH), BF16),
            pltpu.SemaphoreType.DMA((5,)),
            pltpu.SemaphoreType.DMA((9,)),
            pltpu.SemaphoreType.DMA((27,)),
            pltpu.SemaphoreType.DMA((27,)),
            pltpu.SemaphoreType.DMA((27,)),
            pltpu.SemaphoreType.DMA((27,)),
            pltpu.SemaphoreType.DMA((3,)),
            pltpu.SemaphoreType.REGULAR((3,)),
        ],
        compiler_params=pltpu.CompilerParams(collective_id=0, has_side_effects=True),
        name="atoms",
    )(ci, nbr, routes, pos, table, w_in, feats, w_out, w_mix, w_self, w_gate, w_read)


PROBES = 256
SLOTS = 256
BLOCK = 128
UNIT = 16
ROWS_C = 208


def split3(x):
    high = x.astype(BF16)
    x = x - high.astype(F32)
    mid = x.astype(BF16)
    return high, mid, (x - mid.astype(F32)).astype(BF16)


def density_kernel(
    probe_ref, pat_ref, recv_ref, upd_hbm, out_ref, atoms_hbm, rt_ref, px_ref, ct_ref, w_ref,
    upd_ref, sem,
):
    take = pltpu.make_async_copy(upd_hbm, upd_ref, sem.at[0])
    give = pltpu.make_async_copy(upd_ref, atoms_hbm, sem.at[1])
    take.start()
    keep = iota((8, 64), 1) % 8 == iota((8, 64), 0)
    rows = []
    for c in range(3):
        for q in range(4):
            rows.append(
                jnp.where(keep, probe_ref[c : c + 1, q * 64 : (q + 1) * 64], 0.0)
            )
    rows = jnp.concatenate(rows, axis=0)
    widen = jnp.where(iota((64, CH), 0) // 8 == iota((64, CH), 1) // UNIT, 1.0, 0.0).astype(BF16)
    high, mid, low = split3(rows)
    px_ref[...] = (dot(low, widen) + dot(mid, widen)) + dot(high, widen)
    spread = jnp.where(
        iota((SLOTS // 2, SLOTS), 0) == iota((SLOTS // 2, SLOTS), 1) // 2, 1.0, 0.0
    ).astype(BF16)
    wanted = dot(pat_ref[...].astype(F32).astype(BF16), spread)
    before = jnp.where(
        iota((SLOTS, SLOTS), 0) < iota((SLOTS, SLOTS), 1), 1.0, 0.0
    ).astype(BF16)
    for h in range(2):
        rt_ref[h * CH : (h + 1) * CH, :] = (
            recv_ref[h * SLOTS : (h + 1) * SLOTS, :].astype(F32).T.astype(BF16)
        )
    active = wanted * rt_ref[192:208, :].astype(F32)[11:12, :]
    rank = dot(active.astype(BF16), before)
    w_ref[...] = jnp.where(active > 0.5, rank, -1.0)
    most = jnp.max(jnp.sum(active, axis=1, keepdims=True)).astype(jnp.int32)
    place = (iota((BLOCK, SLOTS), 0) % UNIT).astype(F32)

    def fetch(u, buf):
        at = place + (u * UNIT).astype(F32)
        pick = jnp.concatenate(
            [jnp.where(at == w_ref[k : k + 1, :], 1.0, 0.0) for k in range(2)], axis=0
        ).astype(BF16)
        ct_ref[buf] = dot(rt_ref[0:ROWS_C, :], pick, NT)

    def add_unit(buf, totals):
        out = []
        for k in range(2):
            lanes = slice(k * BLOCK, (k + 1) * BLOCK)

            def row(j):
                return ct_ref[buf, j : j + 1, lanes]

            rel = [
                px_ref[c * 32 + k * 16 : c * 32 + (k + 1) * 16, :] - row(200 + c)
                for c in range(3)
            ]
            d, ux, uy, uz = geometry(*rel)
            total = [None] * N_FUN
            for m, val in enumerate(harmonics(ux, uy, uz)):
                for b in range(N_FUN):
                    term = row(m * N_FUN + b)
                    total[b] = term if m == 0 else total[b] + val * term
            add = totals[k]
            for b, phi in enumerate(radial_funs(d)):
                add = add + phi * total[b]
            out.append(add)
        return tuple(out)

    fetch(jnp.int32(0), 0)

    def two_units(i, totals):
        fetch(2 * i + 1, 1)
        totals = add_unit(0, totals)
        fetch(2 * i + 2, 0)
        return add_unit(1, totals)

    zero = jnp.zeros((16, BLOCK), F32)
    totals = two_units(jnp.int32(0), (zero, zero))
    take.wait()
    give.start()
    totals = lax.fori_loop(1, (most + 2 * UNIT - 1) // (2 * UNIT), two_units, totals)
    narrow = jnp.where(iota((CH, 64), 0) // UNIT == iota((CH, 64), 1) // 8, 1.0, 0.0).astype(BF16)
    high, mid, low = split3(jnp.concatenate(totals, axis=0))
    sums = (dot(low, narrow) + dot(mid, narrow)) + dot(high, narrow)
    for q in range(4):
        part = jnp.where(keep, sums[q * 8 : (q + 1) * 8], 0.0)
        out_ref[q // 2 : q // 2 + 1, (q % 2) * 64 : (q % 2 + 1) * 64] = jnp.sum(
            part, axis=0, keepdims=True
        ) * (1.0 / math.sqrt(SLOTS))
    give.wait()


def density_call(probes, pattern, recv, upd):
    vm = pl.BlockSpec(memory_space=pltpu.VMEM)
    hbm = pl.BlockSpec(memory_space=pl.ANY)
    return pl.pallas_call(
        density_kernel,
        out_shape=(
            jax.ShapeDtypeStruct((2, CH), F32),
            jax.ShapeDtypeStruct((COMP, ATOMS, CH), BF16),
        ),
        in_specs=[vm] * 3 + [hbm],
        out_specs=(vm, hbm),
        scratch_shapes=[
            pltpu.VMEM((2 * CH, SLOTS), BF16),
            pltpu.VMEM((96, CH), F32),
            pltpu.VMEM((2, ROWS_C, 2 * BLOCK), F32),
            pltpu.VMEM((2, SLOTS), F32),
            pltpu.VMEM((COMP, ATOMS, CH), BF16),
            pltpu.SemaphoreType.DMA((2,)),
        ],
        name="density",
    )(probes, pattern, recv, upd)


def per_device(
    features, positions, probe_positions, neighbours, routes, pattern, charge_index, charge_table,
    w_radial_in, w_radial_out, w_mix, w_self, w_gate, w_read,
):
    feats = jnp.transpose(features, (1, 0, 2)).reshape(COMP, 32, 4, CH)
    upd, recv = atom_call(
        charge_index, neighbours.T, routes.T, positions, charge_table, w_radial_in, feats,
        w_radial_out, w_mix, w_self, w_gate, jnp.transpose(w_read, (1, 0, 2)),
    )
    density, atoms = density_call(probe_positions, pattern, recv.reshape(512, CH), upd)
    return jnp.transpose(atoms, (1, 0, 2)), density.reshape(PROBES)


def solution(mesh):
    split = ("gx", "gy", "gz")
    rows = P(split, None)
    in_specs = (
        (P(split, None, None), P(None, split), P(None, split), rows, rows, rows) + (P(),) * 8
    )
    out_specs = (P(split, None, None), P(split))
    return jax.shard_map(
        per_device, mesh=mesh, in_specs=in_specs, out_specs=out_specs, check_vma=False
    )
```

```python
import functools, math
import jax
import jax.numpy as jnp
from jax import lax
from jax.experimental import pallas as pl
from jax.experimental.pallas import tpu as pltpu
from jax.sharding import PartitionSpec as P

F32 = jnp.float32
BF16 = jnp.bfloat16
CUTOFF = 8.0
WIDTH_R = 0.75
REACH = 6.0
FLOOR = 0.25
N_FUN = 8
DEG = 5
COMP = 25
CH = 128
ATOMS = 128
FAN = 20
GROUP = 8
N_GROUP = 16
EDGE = GROUP * FAN
CHUNK = 4
WIDE = 8
MAXN = 256


def degree_of(component):
    return int(math.isqrt(component))


def harmonics(x, y, z):
    xx, yy, zz = x * x, y * y, z * z
    c = math.sqrt
    return [
        jnp.ones_like(x),
        c(3.0) * y,
        c(3.0) * z,
        c(3.0) * x,
        c(15.0) * x * y,
        c(15.0) * y * z,
        0.5 * c(5.0) * (3.0 * zz - 1.0),
        c(15.0) * x * z,
        0.5 * c(15.0) * (xx - yy),
        c(35.0 / 8.0) * y * (3.0 * xx - yy),
        c(105.0) * x * y * z,
        c(21.0 / 8.0) * y * (5.0 * zz - 1.0),
        0.5 * c(7.0) * z * (5.0 * zz - 3.0),
        c(21.0 / 8.0) * x * (5.0 * zz - 1.0),
        0.5 * c(105.0) * z * (xx - yy),
        c(35.0 / 8.0) * x * (xx - 3.0 * yy),
        1.5 * c(35.0) * x * y * (xx - yy),
        1.5 * c(17.5) * y * z * (3.0 * xx - yy),
        1.5 * c(5.0) * x * y * (7.0 * zz - 1.0),
        1.5 * c(2.5) * y * z * (7.0 * zz - 3.0),
        0.375 * (35.0 * zz * zz - 30.0 * zz + 3.0),
        1.5 * c(2.5) * x * z * (7.0 * zz - 3.0),
        0.75 * c(5.0) * (xx - yy) * (7.0 * zz - 1.0),
        1.5 * c(17.5) * x * z * (xx - 3.0 * yy),
        0.375 * c(35.0) * (xx * xx - 6.0 * xx * yy + yy * yy),
    ]


def radial_funs(d):
    q = d * (1.0 / CUTOFF)
    env = 1.0 - q * q
    env = env * env
    out = []
    for b in range(N_FUN):
        v = (d - b * (REACH / (N_FUN - 1))) * (1.0 / WIDTH_R)
        out.append(jnp.exp(-(v * v)) * env)
    return out


def geometry(dx, dy, dz):
    d = jnp.sqrt(dx * dx + dy * dy + dz * dz)
    inv = 1.0 / jnp.maximum(d, FLOOR)
    return d, dx * inv, dy * inv, dz * inv


def iota(shape, dim):
    return lax.broadcasted_iota(jnp.int32, shape, dim)


def dot(a, b, dims=None):
    if dims is None:
        dims = (((1,), (0,)), ((), ()))
    return lax.dot_general(a, b, dims, preferred_element_type=F32)


NT = (((1,), (1,)), ((), ()))
TN = (((0,), (0,)), ((), ()))


MESH = pl.DeviceIdType.MESH
ROW_OF = (0, 16, 48, 96, 160)
ROWS = 240


def atom_kernel(
    ci_ref, nbr_hbm, routes_hbm, pos_hbm, table_hbm, w_in_hbm, feats_hbm, w_out_hbm, w_mix_hbm,
    w_self_hbm, w_gate_hbm, w_read_hbm, upd_hbm, recv_ref,
    nbr_ref, routes_ref, pos_ref, table_ref, w_in_ref,
    f_ref, e_ref, oh_ref, xyz_ref, ys_ref, bas_ref, y_ref, r_ref, s_ref, agg_ref, cross_ref,
    upd_ref, send_ref, put_ref, extra_ref, w_out_ref, w_mix_ref, w_self_ref, w_gate_ref, w_read_ref, spread_ref,
    small_sem, load_sem, pos_send, pos_recv, halo_send, halo_recv, tile_sem, plane_sem,
):
    gx, gy, gz = lax.axis_index("gx"), lax.axis_index("gy"), lax.axis_index("gz")
    nx, ny, nz = lax.axis_size("gx"), lax.axis_size("gy"), lax.axis_size("gz")

    def place(a, b, c):
        return (
            lax.rem(gx + a + nx, nx), lax.rem(gy + b + ny, ny), lax.rem(gz + c + nz, nz)
        )

    peers = [place(1 - n // 9, 1 - n // 3 % 3, 1 - n % 3) for n in range(27)]
    others = [n for n in range(27) if n != 13]
    around = [(b, c) for b in (-1, 0, 1) for c in (-1, 0, 1) if (b, c) != (0, 0)]

    def plane_signal(step):
        for b, c in around:
            pl.semaphore_signal(
                plane_sem.at[step],
                inc=1,
                device_id=place(0, b << step, c << step),
                device_id_type=MESH,
            )

    small = [
        pltpu.make_async_copy(src, dst, small_sem.at[i])
        for i, (src, dst) in enumerate(
            (
                (pos_hbm, pos_ref),
                (nbr_hbm, nbr_ref),
                (table_hbm, table_ref),
                (routes_hbm, routes_ref),
                (w_in_hbm, w_in_ref),
            )
        )
    ]
    small[0].start()
    first = pltpu.make_async_copy(
        feats_hbm.at[:, 0:1], f_ref.at[0:COMP, 0:1], load_sem.at[0]
    )
    first.start()
    barrier = pltpu.get_barrier_semaphore()
    for n in others:
        pl.semaphore_signal(barrier, inc=1, device_id=peers[n], device_id_type=MESH)
    rest = pltpu.make_async_copy(
        feats_hbm.at[:, 1:32], f_ref.at[0:COMP, 1:32], load_sem.at[1]
    )
    loads = [
        pltpu.make_async_copy(src, dst, load_sem.at[2 + i])
        for i, (src, dst) in enumerate(
            (
                (w_out_hbm, w_out_ref),
                (w_mix_hbm, w_mix_ref),
                (w_self_hbm, w_self_ref),
                (w_gate_hbm, w_gate_ref),
                (w_read_hbm, w_read_ref),
            )
        )
    ]
    for load in small[1:] + [rest] + loads:
        load.start()
    small[0].wait()
    pos = pos_ref[...].astype(F32)
    pos8 = jnp.concatenate(
        [pos, jnp.ones((1, ATOMS), F32), jnp.zeros((4, ATOMS), F32)], axis=0
    )
    eye = jnp.where(iota((8, CH), 1) == iota((8, CH), 0), 1.0, 0.0).astype(BF16)
    f_ref[COMP, 0] = dot(pos8.astype(BF16), eye, TN)[0:4].astype(BF16)
    f_ref[:, 59:64] = jnp.zeros((COMP + 1, 5, 4, CH), BF16)
    first.wait()
    pl.semaphore_wait(barrier, 26)
    sent, halo = [], []
    for n in others:
        copy = pltpu.make_async_remote_copy(
            src_ref=f_ref.at[COMP, 0],
            dst_ref=f_ref.at[COMP, 32 + n],
            send_sem=pos_send.at[n],
            recv_sem=pos_recv.at[n],
            device_id=peers[n],
            device_id_type=MESH,
        )
        copy.start()
        sent.append(copy)
    for n in others:
        copy = pltpu.make_async_remote_copy(
            src_ref=f_ref.at[0:COMP, 0],
            dst_ref=f_ref.at[0:COMP, 32 + n],
            send_sem=halo_send.at[n],
            recv_sem=halo_recv.at[n],
            device_id=peers[n],
            device_id_type=MESH,
        )
        copy.start()
        halo.append(copy)
    mine = pltpu.make_async_copy(f_ref.at[:, 0], f_ref.at[:, 45], load_sem.at[7])
    mine.start()
    plane_signal(0)
    for load in small[1:]:
        load.wait()
    nbr = jnp.concatenate(
        [nbr_ref[...].astype(F32), jnp.zeros((4, ATOMS), F32)], axis=0
    ).T
    col = iota((ATOMS, MAXN), 1).astype(F32)
    for k in range(0, FAN, 2):
        halves = []
        for kk in (k, k + 1):
            hot = jnp.where(nbr[:, kk : kk + 1] == col, 1.0, 0.0)
            halves.append(hot.reshape(N_GROUP, GROUP, MAXN))
        oh_ref[:, k * GROUP : (k + 2) * GROUP, :] = jnp.concatenate(halves, axis=1).astype(BF16)
    lvl = iota((8, CH), 0)
    shift = jnp.sum(
        jnp.where(lvl == ci_ref[0], table_ref[...].astype(F32), 0.0), axis=0, keepdims=True
    )
    flat = f_ref.reshape(COMP + 1, MAXN, CH)
    mine.wait()
    for load in loads:
        load.wait()
    spread_ref[...] = jnp.zeros((MAXN, COMP * CH), BF16)
    none8 = jnp.zeros((N_FUN, CH), F32)
    for m in range(COMP):
        one = w_read_ref[degree_of(m)].astype(F32)
        two = [one, none8] if m % 2 == 0 else [none8, one]
        start = (m - m % 2) * N_FUN
        spread_ref[start : start + 16, m * CH : (m + 1) * CH] = jnp.concatenate(
            two, axis=0
        ).astype(BF16)
    r_row = jnp.broadcast_to(routes_ref[...].astype(F32), (ATOMS, ATOMS))
    r_col = r_row.T
    before = iota((ATOMS, ATOMS), 0) < iota((ATOMS, ATOMS), 1)
    rank = jnp.sum(
        jnp.where(before, jnp.where(r_col == r_row, 1.0, 0.0), 0.0), axis=0, keepdims=True
    )
    target = (r_row[0:1, :] * 2.0 + rank).astype(jnp.int32)
    put_ref[...] = jnp.where(iota((MAXN, ATOMS), 0) == target, 1.0, 0.0).astype(BF16)
    put = jnp.where(iota((8, CH), 1) == iota((8, CH), 0) + 72, 1.0, 0.0).astype(BF16)
    extra_ref[...] = dot(pos8.astype(BF16), put, TN)
    for copy in sent:
        copy.wait()
    gpos_t = flat[COMP, ATOMS:MAXN].astype(F32).T
    pt = jnp.concatenate([pos8, gpos_t[0:8]], axis=1).astype(BF16)
    own_group = iota((N_GROUP, ATOMS), 1) // GROUP == iota((N_GROUP, ATOMS), 0)
    tile_sel = jnp.where(
        iota((ATOMS, EDGE), 0) % GROUP == iota((ATOMS, EDGE), 1) % GROUP, 1.0, 0.0
    ).astype(BF16)
    for g in range(N_GROUP):
        got = dot(pt, oh_ref[g], NT)
        for c in range(3):
            xyz_ref[c, g : g + 1, :] = got[c : c + 1, :]
    rel = []
    for c in range(3):
        mine_c = jnp.where(own_group, pos[c : c + 1, :], 0.0).astype(BF16)
        rel.append(xyz_ref[c] - dot(mine_c, tile_sel))
    d, ux, uy, uz = geometry(*rel)
    for m, val in enumerate(harmonics(ux, uy, uz)):
        ys_ref[:, m, :] = val
    for b, val in enumerate(radial_funs(d)):
        bas_ref[:, b, :] = val
    mask8 = jnp.where(iota((GROUP, EDGE), 1) % GROUP == iota((GROUP, EDGE), 0), 1.0, 0.0)
    w_in = w_in_ref[...]
    scale = 1.0 / math.sqrt(FAN)
    pl.semaphore_wait(plane_sem.at[0], 8)
    plane_signal(1)

    def radial_chunk(ch, carry):
        base = ch * CHUNK
        for q in range(CHUNK):
            h = dot(bas_ref[base + q].astype(BF16), w_in, TN)
            h = (h * jax.nn.sigmoid(h)).astype(BF16)
            r_ref[base + q] = dot(h, w_out_ref[...]) * scale
            y = ys_ref[base + q]
            for l in range(DEG):
                lo = l * l
                rows = [y[m : m + 1, :] * mask8 for m in range(lo, lo + 2 * l + 1)]
                rows.append(jnp.zeros((GROUP, EDGE), F32))
                y_ref[base + q, ROW_OF[l] : ROW_OF[l] + (2 * l + 2) * GROUP] = jnp.concatenate(
                    rows, axis=0
                ).astype(BF16)
        return carry

    lax.fori_loop(0, N_GROUP // CHUNK, radial_chunk, 0)
    rest.wait()
    for copy in halo:
        copy.wait()
    pl.semaphore_wait(plane_sem.at[1], 8)
    plane_signal(2)
    e_ref[...] = (flat[0].astype(F32) + shift).astype(BF16)

    def comp(m):
        return e_ref[...] if m == 0 else flat[m]

    def cross_unit(base, q, l):
        rad = r_ref[base + q, :, (DEG + l) * CH : (DEG + l + 1) * CH]
        part = (rad * s_ref[q]).astype(BF16)
        lhs = y_ref[base + q, ROW_OF[l] : ROW_OF[l] + (2 * l + 2) * GROUP]
        got = dot(lhs, part)
        for j in range(2 * l + 1):
            m = l * l + j
            cross_ref[base + q, :, m * CH : (m + 1) * CH] = got[j * GROUP : (j + 1) * GROUP, :]

    units = [(q, l) for l in range(DEG) for q in range(WIDE)]

    def one_chunk(ch, carry):
        base = ch * WIDE
        hot = oh_ref[pl.ds(base, WIDE)].reshape(WIDE * EDGE, MAXN)
        todo = list(units)
        for m in range(0, COMP, 2):
            comps = [m] + ([m + 1] if m + 1 < COMP else [])
            got = dot(hot, jnp.concatenate([comp(mm) for mm in comps], axis=1))
            if m == 0:
                s_ref[...] = got[:, 0:CH].reshape(WIDE, EDGE, CH)
            else:
                for q, l in todo[:4]:
                    cross_unit(base, q, l)
                todo = todo[4:]
            for j, mm in enumerate(comps):
                l = degree_of(mm)
                part = got[:, j * CH : (j + 1) * CH].reshape(WIDE, FAN, GROUP, CH)
                rad = r_ref[pl.ds(base, WIDE), :, l * CH : (l + 1) * CH].reshape(
                    WIDE, FAN, GROUP, CH
                )
                agg_ref[pl.ds(base, WIDE), :, mm * CH : (mm + 1) * CH] = jnp.sum(
                    part * rad, axis=1
                )
        return carry

    lax.fori_loop(0, N_GROUP // WIDE, one_chunk, 0)

    def agg_of(m):
        lanes = slice(m * CH, (m + 1) * CH)
        both = agg_ref[:, :, lanes] + cross_ref[:, :, lanes]
        return both.reshape(ATOMS, CH).astype(BF16)

    gates = jax.nn.sigmoid(dot(agg_of(0), w_gate_ref[...]))
    for l in range(DEG):
        w_cat = jnp.concatenate([w_mix_ref[l], w_self_ref[l]], axis=0)
        for m in range(l * l, (l + 1) * (l + 1)):
            emb = comp(m)[0:ATOMS]
            mixed = dot(jnp.concatenate([agg_of(m), emb], axis=1), w_cat)
            if l == 0:
                add = mixed * jax.nn.sigmoid(mixed)
            else:
                add = mixed * gates[:, (l - 1) * CH : l * CH]
            upd_ref[m] = (emb.astype(F32) + add).astype(BF16)
    store = pltpu.make_async_copy(upd_ref, upd_hbm, load_sem.at[8])
    store.start()
    coef = dot(
        jnp.concatenate([upd_ref[m] for m in range(COMP)], axis=1), spread_ref[...], NT
    )
    coefs = [coef[:, 0:CH], coef[:, CH:] + extra_ref[...]]
    flat_send = send_ref.reshape(2, 2 * 128, CH)
    for h in range(2):
        flat_send[h] = dot(put_ref[...], coefs[h].astype(BF16)).astype(BF16)
    pl.semaphore_wait(plane_sem.at[2], 8)
    count = ny * nz
    me = gy * nz + gz

    def post(j, carry):
        t = lax.rem(me + j, count)
        pltpu.make_async_remote_copy(
            src_ref=send_ref.at[:, t],
            dst_ref=recv_ref.at[:, me],
            send_sem=tile_sem.at[0],
            recv_sem=tile_sem.at[1],
            device_id=(gx, t // nz, lax.rem(t, nz)),
            device_id_type=MESH,
        ).start()
        return carry

    lax.fori_loop(1, count, post, 0)
    own = pltpu.make_async_copy(send_ref.at[:, me], recv_ref.at[:, me], tile_sem.at[2])
    own.start()
    own.wait()
    store.wait()
    part = pl.ds(0, count - 1)
    pltpu.make_async_copy(send_ref.at[:, part], recv_ref.at[:, part], tile_sem.at[0]).wait()
    pltpu.make_async_copy(send_ref.at[:, part], recv_ref.at[:, part], tile_sem.at[1]).wait()


def atom_call(ci, nbr, routes, pos, table, w_in, feats, w_out, w_mix, w_self, w_gate, w_read):
    hbm = pl.BlockSpec(memory_space=pl.ANY)
    return pl.pallas_call(
        atom_kernel,
        out_shape=(
            jax.ShapeDtypeStruct((COMP, ATOMS, CH), BF16),
            jax.ShapeDtypeStruct((2, 128, 2, CH), BF16),
        ),
        in_specs=[pl.BlockSpec(memory_space=pltpu.SMEM)] + [hbm] * 11,
        out_specs=(hbm, hbm),
        scratch_shapes=[
            pltpu.VMEM((FAN, ATOMS), jnp.int32),
            pltpu.VMEM((1, ATOMS), jnp.int32),
            pltpu.VMEM((3, ATOMS), BF16),
            pltpu.VMEM((8, CH), BF16),
            pltpu.VMEM((N_FUN, 64), BF16),
            pltpu.VMEM((COMP + 1, 64, 4, CH), BF16),
            pltpu.VMEM((MAXN, CH), BF16),
            pltpu.VMEM((N_GROUP, EDGE, MAXN), BF16),
            pltpu.VMEM((3, N_GROUP, EDGE), F32),
            pltpu.VMEM((N_GROUP, COMP, EDGE), F32),
            pltpu.VMEM((N_GROUP, N_FUN, EDGE), F32),
            pltpu.VMEM((N_GROUP, ROWS, EDGE), BF16),
            pltpu.VMEM((N_GROUP, EDGE, 2 * DEG * CH), F32),
            pltpu.VMEM((WIDE, EDGE, CH), F32),
            pltpu.VMEM((N_GROUP, GROUP, COMP * CH), F32),
            pltpu.VMEM((N_GROUP, GROUP, COMP * CH), F32),
            pltpu.VMEM((COMP, ATOMS, CH), BF16),
            pltpu.VMEM((2, 128, 2, CH), BF16),
            pltpu.VMEM((MAXN, ATOMS), BF16),
            pltpu.VMEM((ATOMS, CH), F32),
            pltpu.VMEM((64, 2 * DEG * CH), BF16),
            pltpu.VMEM((DEG, CH, CH), BF16),
            pltpu.VMEM((DEG, CH, CH), BF16),
            pltpu.VMEM((CH, (DEG - 1) * CH), BF16),
            pltpu.VMEM((DEG, N_FUN, CH), BF16),
            pltpu.VMEM((MAXN, COMP * CH), BF16),
            pltpu.SemaphoreType.DMA((5,)),
            pltpu.SemaphoreType.DMA((9,)),
            pltpu.SemaphoreType.DMA((27,)),
            pltpu.SemaphoreType.DMA((27,)),
            pltpu.SemaphoreType.DMA((27,)),
            pltpu.SemaphoreType.DMA((27,)),
            pltpu.SemaphoreType.DMA((3,)),
            pltpu.SemaphoreType.REGULAR((3,)),
        ],
        compiler_params=pltpu.CompilerParams(collective_id=0, has_side_effects=True),
        name="atoms",
    )(ci, nbr, routes, pos, table, w_in, feats, w_out, w_mix, w_self, w_gate, w_read)


PROBES = 256
SLOTS = 256
BLOCK = 128
UNIT = 16
ROWS_C = 208


def split3(x):
    high = x.astype(BF16)
    x = x - high.astype(F32)
    mid = x.astype(BF16)
    return high, mid, (x - mid.astype(F32)).astype(BF16)


def density_kernel(
    probe_ref, pat_ref, recv_ref, upd_hbm, out_ref, atoms_hbm, rt_ref, px_ref, ct_ref, w_ref,
    upd_ref, sem,
):
    take = pltpu.make_async_copy(upd_hbm, upd_ref, sem.at[0])
    give = pltpu.make_async_copy(upd_ref, atoms_hbm, sem.at[1])
    take.start()
    keep = iota((8, 64), 1) % 8 == iota((8, 64), 0)
    rows = []
    for c in range(3):
        for q in range(4):
            rows.append(
                jnp.where(keep, probe_ref[c : c + 1, q * 64 : (q + 1) * 64], 0.0)
            )
    rows = jnp.concatenate(rows, axis=0)
    widen = jnp.where(iota((64, CH), 0) // 8 == iota((64, CH), 1) // UNIT, 1.0, 0.0).astype(BF16)
    high, mid, low = split3(rows)
    px_ref[...] = (dot(low, widen) + dot(mid, widen)) + dot(high, widen)
    spread = jnp.where(
        iota((SLOTS // 2, SLOTS), 0) == iota((SLOTS // 2, SLOTS), 1) // 2, 1.0, 0.0
    ).astype(BF16)
    wanted = dot(pat_ref[...].astype(F32).astype(BF16), spread)
    before = jnp.where(
        iota((SLOTS, SLOTS), 0) < iota((SLOTS, SLOTS), 1), 1.0, 0.0
    ).astype(BF16)
    for h in range(2):
        rt_ref[h * CH : (h + 1) * CH, :] = (
            recv_ref[h * SLOTS : (h + 1) * SLOTS, :].astype(F32).T.astype(BF16)
        )
    active = wanted * rt_ref[192:208, :].astype(F32)[11:12, :]
    rank = dot(active.astype(BF16), before)
    w_ref[...] = jnp.where(active > 0.5, rank, -1.0)
    most = jnp.max(jnp.sum(active, axis=1, keepdims=True)).astype(jnp.int32)
    place = (iota((BLOCK, SLOTS), 0) % UNIT).astype(F32)

    def fetch(u, buf):
        at = place + (u * UNIT).astype(F32)
        pick = jnp.concatenate(
            [jnp.where(at == w_ref[k : k + 1, :], 1.0, 0.0) for k in range(2)], axis=0
        ).astype(BF16)
        ct_ref[buf] = dot(rt_ref[0:ROWS_C, :], pick, NT)

    def add_unit(buf, totals):
        out = []
        for k in range(2):
            lanes = slice(k * BLOCK, (k + 1) * BLOCK)

            def row(j):
                return ct_ref[buf, j : j + 1, lanes]

            rel = [
                px_ref[c * 32 + k * 16 : c * 32 + (k + 1) * 16, :] - row(200 + c)
                for c in range(3)
            ]
            d, ux, uy, uz = geometry(*rel)
            total = [None] * N_FUN
            for m, val in enumerate(harmonics(ux, uy, uz)):
                for b in range(N_FUN):
                    term = row(m * N_FUN + b)
                    total[b] = term if m == 0 else total[b] + val * term
            add = totals[k]
            for b, phi in enumerate(radial_funs(d)):
                add = add + phi * total[b]
            out.append(add)
        return tuple(out)

    fetch(jnp.int32(0), 0)

    def two_units(i, totals):
        fetch(2 * i + 1, 1)
        totals = add_unit(0, totals)
        fetch(2 * i + 2, 0)
        return add_unit(1, totals)

    zero = jnp.zeros((16, BLOCK), F32)
    totals = two_units(jnp.int32(0), (zero, zero))
    take.wait()
    give.start()
    units = jnp.maximum((most + UNIT - 1) // UNIT, 2)
    totals = lax.fori_loop(1, units // 2, two_units, totals)
    totals = lax.fori_loop(0, units % 2, lambda i, totals: add_unit(0, totals), totals)
    narrow = jnp.where(iota((CH, 64), 0) // UNIT == iota((CH, 64), 1) // 8, 1.0, 0.0).astype(BF16)
    high, mid, low = split3(jnp.concatenate(totals, axis=0))
    sums = (dot(low, narrow) + dot(mid, narrow)) + dot(high, narrow)
    for q in range(4):
        part = jnp.where(keep, sums[q * 8 : (q + 1) * 8], 0.0)
        out_ref[q // 2 : q // 2 + 1, (q % 2) * 64 : (q % 2 + 1) * 64] = jnp.sum(
            part, axis=0, keepdims=True
        ) * (1.0 / math.sqrt(SLOTS))
    give.wait()


def density_call(probes, pattern, recv, upd):
    vm = pl.BlockSpec(memory_space=pltpu.VMEM)
    hbm = pl.BlockSpec(memory_space=pl.ANY)
    return pl.pallas_call(
        density_kernel,
        out_shape=(
            jax.ShapeDtypeStruct((2, CH), F32),
            jax.ShapeDtypeStruct((COMP, ATOMS, CH), BF16),
        ),
        in_specs=[vm] * 3 + [hbm],
        out_specs=(vm, hbm),
        scratch_shapes=[
            pltpu.VMEM((2 * CH, SLOTS), BF16),
            pltpu.VMEM((96, CH), F32),
            pltpu.VMEM((2, ROWS_C, 2 * BLOCK), F32),
            pltpu.VMEM((2, SLOTS), F32),
            pltpu.VMEM((COMP, ATOMS, CH), BF16),
            pltpu.SemaphoreType.DMA((2,)),
        ],
        name="density",
    )(probes, pattern, recv, upd)


def per_device(
    features, positions, probe_positions, neighbours, routes, pattern, charge_index, charge_table,
    w_radial_in, w_radial_out, w_mix, w_self, w_gate, w_read,
):
    feats = jnp.transpose(features, (1, 0, 2)).reshape(COMP, 32, 4, CH)
    upd, recv = atom_call(
        charge_index, neighbours.T, routes.T, positions, charge_table, w_radial_in, feats,
        w_radial_out, w_mix, w_self, w_gate, jnp.transpose(w_read, (1, 0, 2)),
    )
    density, atoms = density_call(probe_positions, pattern, recv.reshape(512, CH), upd)
    return jnp.transpose(atoms, (1, 0, 2)), density.reshape(PROBES)


def solution(mesh):
    split = ("gx", "gy", "gz")
    rows = P(split, None)
    in_specs = (
        (P(split, None, None), P(None, split), P(None, split), rows, rows, rows) + (P(),) * 8
    )
    out_specs = (P(split, None, None), P(split))
    return jax.shard_map(
        per_device, mesh=mesh, in_specs=in_specs, out_specs=out_specs, check_vma=False
    )
```
